32 devices in a mesh: dp: 16 (over z, y, core), seq: 2 (over x).
Axes of the slice: x: 2, y: 2, z: 4, core: 2. Of those that a mesh axis runs over, the one named last changes fastest.
Arguments:
- latents: float32 [16, 256, 1152], P('dp', 'seq'), may hold values from -6 to 6
- condition: float32 [8, 1152], replicated, may hold values from -6 to 6
- slot_latent: int32 [16, 1], P('dp'), may hold values from 0 to 7, as said below
- slot_counts: int32 [16], P('dp'), may hold values from 0 to 1, as said below
- output_gradient: float32 [16, 256, 1152], P('dp', 'seq'), may hold values from -6 to 6
- ada_weight: float32 [1152, 6912], P(None, ('dp', 'seq')), may hold values from -0.1875 to 0.1875
- ada_bias: float32 [6912], P(('dp', 'seq')), may hold values from -1.75 to 1.75
- qkv_weight: float32 [1152, 3456], P('dp', 'seq'), may hold values from -5 to 5, as said below
- qkv_bias: float32 [3456], P('seq'), may hold values from -1.25 to 1.25
- out_weight: float32 [1152, 1152], P('dp', 'seq'), may hold values from -0.75 to 0.75
- out_bias: float32 [1152], P('seq'), may hold values from -1.25 to 1.25
- up_weight: float32 [1152, 4608], P('dp', 'seq'), may hold values from -0.1875 to 0.1875
- up_bias: float32 [4608], P('seq'), may hold values from -1.25 to 1.25
- down_weight: float32 [4608, 1152], P('dp', 'seq'), may hold values from -0.09375 to 0.09375
- down_bias: float32 [1152], P('seq'), may hold values from -1.25 to 1.25
- mean_adaw: float32 [1152, 6912], P(None, ('dp', 'seq')), may hold values from -16 to 16
- mean_adab: float32 [6912], P(('dp', 'seq')), may hold values from -16 to 16
- mean_qkvw: float32 [1152, 3456], P('dp', 'seq'), may hold values from -16 to 16
- mean_qkvb: float32 [3456], P('seq'), may hold values from -16 to 16
- mean_outw: float32 [1152, 1152], P('dp', 'seq'), may hold values from -16 to 16
- mean_outb: float32 [1152], P('seq'), may hold values from -16 to 16
- mean_upw: float32 [1152, 4608], P('dp', 'seq'), may hold values from -16 to 16
- mean_upb: float32 [4608], P('seq'), may hold values from -16 to 16
- mean_downw: float32 [4608, 1152], P('dp', 'seq'), may hold values from -16 to 16
- mean_downb: float32 [1152], P('seq'), may hold values from -16 to 16
- sqmean_adaw: float32 [1152, 6912], P(None, ('dp', 'seq')), may hold values from 0.3 to 3
- sqmean_adab: float32 [6912], P(('dp', 'seq')), may hold values from 0.3 to 3
- sqmean_qkvw: float32 [1152, 3456], P('dp', 'seq'), may hold values from 0.3 to 3
- sqmean_qkvb: float32 [3456], P('seq'), may hold values from 0.3 to 3
- sqmean_outw: float32 [1152, 1152], P('dp', 'seq'), may hold values from 0.3 to 3
- sqmean_outb: float32 [1152], P('seq'), may hold values from 0.3 to 3
- sqmean_upw: float32 [1152, 4608], P('dp', 'seq'), may hold values from 0.3 to 3
- sqmean_upb: float32 [4608], P('seq'), may hold values from 0.3 to 3
- sqmean_downw: float32 [4608, 1152], P('dp', 'seq'), may hold values from 0.3 to 3
- sqmean_downb: float32 [1152], P('seq'), may hold values from 0.3 to 3
Outputs:
- block_output: float32 [16, 256, 1152], P('dp', 'seq')
- latent_gradient: float32 [16, 256, 1152], P('dp', 'seq')
- condition_grad: float32 [8, 1152], replicated
- grad_adaw: float32 [1152, 6912], P(None, ('dp', 'seq'))
- grad_adab: float32 [6912], P(('dp', 'seq'))
- grad_qkvw: float32 [1152, 3456], P('dp', 'seq')
- grad_qkvb: float32 [3456], P('seq')
- grad_outw: float32 [1152, 1152], P('dp', 'seq')
- grad_outb: float32 [1152], P('seq')
- grad_upw: float32 [1152, 4608], P('dp', 'seq')
- grad_upb: float32 [4608], P('seq')
- grad_downw: float32 [4608, 1152], P('dp', 'seq')
- grad_downb: float32 [1152], P('seq')
- newval_adaw: float32 [1152, 6912], P(None, ('dp', 'seq'))
- newval_adab: float32 [6912], P(('dp', 'seq'))
- newval_qkvw: float32 [1152, 3456], P('dp', 'seq')
- newval_qkvb: float32 [3456], P('seq')
- newval_outw: float32 [1152, 1152], P('dp', 'seq')
- newval_outb: float32 [1152], P('seq')
- newval_upw: float32 [1152, 4608], P('dp', 'seq')
- newval_upb: float32 [4608], P('seq')
- newval_downw: float32 [4608, 1152], P('dp', 'seq')
- newval_downb: float32 [1152], P('seq')
- newmean_adaw: float32 [1152, 6912], P(None, ('dp', 'seq'))
- newmean_adab: float32 [6912], P(('dp', 'seq'))
- newmean_qkvw: float32 [1152, 3456], P('dp', 'seq')
- newmean_qkvb: float32 [3456], P('seq')
- newmean_outw: float32 [1152, 1152], P('dp', 'seq')
- newmean_outb: float32 [1152], P('seq')
- newmean_upw: float32 [1152, 4608], P('dp', 'seq')
- newmean_upb: float32 [4608], P('seq')
- newmean_downw: float32 [4608, 1152], P('dp', 'seq')
- newmean_downb: float32 [1152], P('seq')
- newsqr_adaw: float32 [1152, 6912], P(None, ('dp', 'seq'))
- newsqr_adab: float32 [6912], P(('dp', 'seq'))
- newsqr_qkvw: float32 [1152, 3456], P('dp', 'seq')
- newsqr_qkvb: float32 [3456], P('seq')
- newsqr_outw: float32 [1152, 1152], P('dp', 'seq')
- newsqr_outb: float32 [1152], P('seq')
- newsqr_upw: float32 [1152, 4608], P('dp', 'seq')
- newsqr_upb: float32 [4608], P('seq')
- newsqr_downw: float32 [4608, 1152], P('dp', 'seq')
- newsqr_downb: float32 [1152], P('seq')
The draws below stay inside these ranges and needn't reach their ends.
Inputs may be any that keep to these rules, and one draw needn't show every extreme that they name: `slot_counts`: live slots of a group come first; the entries sum to 8; some group has all 1 slots live in every draw, some groups may have none. `slot_latent`: the live slots name every latent exactly once; entries of slots that are not live are arbitrary latents. `qkv_weight`: query and value columns have entries of order 1152^-1/2; key columns may have entries up to the ends of the range.
All inputs are finite; a program needn't handle non-finite values.
Results may differ from the reference program's by a relative error of at most 0.012.
The reference program's roundings to bfloat16 on the way count: a program that leaves them out, or rounds other values in their place, can miss the bound.
Values may be sent and summed in bfloat16 or wider, within the bound.
A program may use at most 192 MiB of HBM per device.

```python
import math
import jax
import jax.numpy as jnp
from jax import lax

MODEL_DIMENSION = 1152
H = 16
HD = 72
FF = 4608
SLOTS = 1
STEP = 2
LATENT_TOKENS = 256
SLOT_COUNT = 16
LAT = 8
N_DP = 16


def slot_plan(key):
    key_owner = jax.random.fold_in(key, 11)
    key_order = jax.random.fold_in(key, 12)
    key_ids = jax.random.fold_in(key, 13)
    key_pad = jax.random.fold_in(key, 14)
    tickets = N_DP * SLOTS
    owner_group = jnp.arange(tickets, dtype=jnp.int32) // SLOTS
    chosen = jax.random.randint(key_owner, (), 0, N_DP, dtype=jnp.int32)
    shuffled = jax.random.permutation(key_order, tickets).astype(jnp.int32)
    ticket_score = jnp.where(owner_group == chosen, shuffled - tickets, shuffled)
    ticket_order = jnp.argsort(ticket_score, stable=True)
    taken_flags = jnp.zeros((tickets,), jnp.int32).at[ticket_order[:LAT]].set(1)
    counts = jnp.sum(taken_flags.reshape(N_DP, SLOTS), axis=1).astype(jnp.int32)
    live_flags = (jnp.arange(SLOTS, dtype=jnp.int32)[None, :] < counts[:, None]).reshape(-1)
    position = jnp.cumsum(live_flags.astype(jnp.int32)) - 1
    latent_perm = jax.random.permutation(key_ids, LAT).astype(jnp.int32)
    pad_ids = jax.random.randint(key_pad, (tickets,), 0, LAT, dtype=jnp.int32)
    latent_table = jnp.where(live_flags, latent_perm[jnp.clip(position, 0, LAT - 1)], pad_ids)
    return (counts, latent_table.reshape(N_DP, SLOTS).astype(jnp.int32))


def draw_slot_counts(key, part):
    return slot_plan(key)[0]


def draw_slot_latent(key, part):
    return slot_plan(key)[1]


def draw_qkv_weight(key, part):
    base_draw = jax.random.normal(key, (MODEL_DIMENSION, 3 * MODEL_DIMENSION), jnp.float32) * MODEL_DIMENSION ** (-0.5)
    base_draw = jnp.clip(base_draw, -6.0 * MODEL_DIMENSION ** (-0.5), 6.0 * MODEL_DIMENSION ** (-0.5))
    return base_draw


def level_of(stream_key, dims, cuts, smallest, top_value):
    def one(dim, blocks):
        heights = jax.random.uniform(jax.random.fold_in(jax.random.fold_in(stream_key, 6), dim), (blocks,), jnp.float32, smallest / len(cuts), top_value / len(cuts))
        return jnp.repeat(jnp.exp(heights), dims[dim] // blocks).reshape((-1,) + (1,) * (len(dims) - dim - 1))

    level = one(*cuts[0])
    for cut in cuts[1:]:
        level = level * one(*cut)
    return level


def bell_draw(own_key, shape, scale, most, shards=(), kind=jnp.bfloat16):
    values = jax.random.normal(own_key, shape, jnp.float32) * scale
    if len(shards) > 0:
        values = level_of(own_key, shape, shards, -0.22, 0.18) * values
    return jnp.clip(values, min=-most, max=most).astype(kind)


def setup_inputs(seed: int = 0) -> dict:
    arg_keys = jax.random.split(jax.random.key(seed), 36)
    latents = bell_draw(arg_keys[0], (SLOT_COUNT, LATENT_TOKENS, MODEL_DIMENSION), 1.0, 6.0, ((0, 16), (1, 2)), jnp.float32)
    condition = bell_draw(arg_keys[1], (LAT, MODEL_DIMENSION), 1.0, 6.0, (), jnp.float32)
    slot_latent = draw_slot_latent(jax.random.fold_in(arg_keys[35], 71), 0)
    slot_counts = draw_slot_counts(jax.random.fold_in(arg_keys[35], 71), 0)
    output_gradient = bell_draw(arg_keys[4], (SLOT_COUNT, LATENT_TOKENS, MODEL_DIMENSION), 1.0, 6.0, ((0, 16), (1, 2)), jnp.float32)
    ada_weight = bell_draw(arg_keys[5], (MODEL_DIMENSION, 6 * MODEL_DIMENSION), MODEL_DIMENSION ** -0.5, 0.1875, ((1, 32),), jnp.float32)
    ada_bias = bell_draw(arg_keys[6], (6 * MODEL_DIMENSION,), 0.3, 1.75, ((0, 32),), jnp.float32)
    qkv_weight = draw_qkv_weight(jax.random.fold_in(arg_keys[35], 71), 0)
    qkv_bias = bell_draw(arg_keys[8], (3 * MODEL_DIMENSION,), 0.2, 1.25, ((0, 2),), jnp.float32)
    out_weight = bell_draw(arg_keys[9], (MODEL_DIMENSION, MODEL_DIMENSION), (max(MODEL_DIMENSION // 16, 1)) ** -0.5, 0.75, ((0, 16), (1, 2)), jnp.float32)
    out_bias = bell_draw(arg_keys[10], (MODEL_DIMENSION,), 0.2, 1.25, ((0, 2),), jnp.float32)
    up_weight = bell_draw(arg_keys[11], (MODEL_DIMENSION, FF), MODEL_DIMENSION ** -0.5, 0.1875, ((0, 16), (1, 2)), jnp.float32)
    up_bias = bell_draw(arg_keys[12], (FF,), 0.2, 1.25, ((0, 2),), jnp.float32)
    down_weight = bell_draw(arg_keys[13], (FF, MODEL_DIMENSION), FF ** -0.5, 0.09375, ((0, 16), (1, 2)), jnp.float32)
    down_bias = bell_draw(arg_keys[14], (MODEL_DIMENSION,), 0.2, 1.25, ((0, 2),), jnp.float32)
    mean_adaw = bell_draw(arg_keys[15], (MODEL_DIMENSION, 6 * MODEL_DIMENSION), 3.0, 16.0, ((1, 32),), jnp.float32)
    mean_adab = bell_draw(arg_keys[16], (6 * MODEL_DIMENSION,), 3.0, 16.0, ((0, 32),), jnp.float32)
    mean_qkvw = bell_draw(arg_keys[17], (MODEL_DIMENSION, 3 * MODEL_DIMENSION), 3.0, 16.0, ((0, 16), (1, 2)), jnp.float32)
    mean_qkvb = bell_draw(arg_keys[18], (3 * MODEL_DIMENSION,), 3.0, 16.0, ((0, 2),), jnp.float32)
    mean_outw = bell_draw(arg_keys[19], (MODEL_DIMENSION, MODEL_DIMENSION), 3.0, 16.0, ((0, 16), (1, 2)), jnp.float32)
    mean_outb = bell_draw(arg_keys[20], (MODEL_DIMENSION,), 3.0, 16.0, ((0, 2),), jnp.float32)
    mean_upw = bell_draw(arg_keys[21], (MODEL_DIMENSION, FF), 3.0, 16.0, ((0, 16), (1, 2)), jnp.float32)
    mean_upb = bell_draw(arg_keys[22], (FF,), 3.0, 16.0, ((0, 2),), jnp.float32)
    mean_downw = bell_draw(arg_keys[23], (FF, MODEL_DIMENSION), 3.0, 16.0, ((0, 16), (1, 2)), jnp.float32)
    mean_downb = bell_draw(arg_keys[24], (MODEL_DIMENSION,), 3.0, 16.0, ((0, 2),), jnp.float32)
    sqmean_adaw = jnp.clip(jnp.exp(math.log(3.0) - 2.3025851 * jax.random.uniform(arg_keys[25], (MODEL_DIMENSION, 6 * MODEL_DIMENSION), jnp.float32) ** level_of(arg_keys[25], (MODEL_DIMENSION, 6 * MODEL_DIMENSION), ((1, 32),), -0.2, 0.2)), 0.3, 3.0)
    sqmean_adab = jnp.clip(jnp.exp(math.log(3.0) - 2.3025851 * jax.random.uniform(arg_keys[26], (6 * MODEL_DIMENSION,), jnp.float32) ** level_of(arg_keys[26], (6 * MODEL_DIMENSION,), ((0, 32),), -0.2, 0.2)), 0.3, 3.0)
    sqmean_qkvw = jnp.clip(jnp.exp(math.log(3.0) - 2.3025851 * jax.random.uniform(arg_keys[27], (MODEL_DIMENSION, 3 * MODEL_DIMENSION), jnp.float32) ** level_of(arg_keys[27], (MODEL_DIMENSION, 3 * MODEL_DIMENSION), ((0, 16), (1, 2)), -0.2, 0.2)), 0.3, 3.0)
    sqmean_qkvb = jnp.clip(jnp.exp(math.log(3.0) - 2.3025851 * jax.random.uniform(arg_keys[28], (3 * MODEL_DIMENSION,), jnp.float32) ** level_of(arg_keys[28], (3 * MODEL_DIMENSION,), ((0, 2),), -0.2, 0.2)), 0.3, 3.0)
    sqmean_outw = jnp.clip(jnp.exp(math.log(3.0) - 2.3025851 * jax.random.uniform(arg_keys[29], (MODEL_DIMENSION, MODEL_DIMENSION), jnp.float32) ** level_of(arg_keys[29], (MODEL_DIMENSION, MODEL_DIMENSION), ((0, 16), (1, 2)), -0.2, 0.2)), 0.3, 3.0)
    sqmean_outb = jnp.clip(jnp.exp(math.log(3.0) - 2.3025851 * jax.random.uniform(arg_keys[30], (MODEL_DIMENSION,), jnp.float32) ** level_of(arg_keys[30], (MODEL_DIMENSION,), ((0, 2),), -0.2, 0.2)), 0.3, 3.0)
    sqmean_upw = jnp.clip(jnp.exp(math.log(3.0) - 2.3025851 * jax.random.uniform(arg_keys[31], (MODEL_DIMENSION, FF), jnp.float32) ** level_of(arg_keys[31], (MODEL_DIMENSION, FF), ((0, 16), (1, 2)), -0.2, 0.2)), 0.3, 3.0)
    sqmean_upb = jnp.clip(jnp.exp(math.log(3.0) - 2.3025851 * jax.random.uniform(arg_keys[32], (FF,), jnp.float32) ** level_of(arg_keys[32], (FF,), ((0, 2),), -0.2, 0.2)), 0.3, 3.0)
    sqmean_downw = jnp.clip(jnp.exp(math.log(3.0) - 2.3025851 * jax.random.uniform(arg_keys[33], (FF, MODEL_DIMENSION), jnp.float32) ** level_of(arg_keys[33], (FF, MODEL_DIMENSION), ((0, 16), (1, 2)), -0.2, 0.2)), 0.3, 3.0)
    sqmean_downb = jnp.clip(jnp.exp(math.log(3.0) - 2.3025851 * jax.random.uniform(arg_keys[34], (MODEL_DIMENSION,), jnp.float32) ** level_of(arg_keys[34], (MODEL_DIMENSION,), ((0, 2),), -0.2, 0.2)), 0.3, 3.0)
    return {"latents": latents, "condition": condition, "slot_latent": slot_latent, "slot_counts": slot_counts, "output_gradient": output_gradient, "ada_weight": ada_weight, "ada_bias": ada_bias, "qkv_weight": qkv_weight, "qkv_bias": qkv_bias, "out_weight": out_weight, "out_bias": out_bias, "up_weight": up_weight, "up_bias": up_bias, "down_weight": down_weight, "down_bias": down_bias, "mean_adaw": mean_adaw, "mean_adab": mean_adab, "mean_qkvw": mean_qkvw, "mean_qkvb": mean_qkvb, "mean_outw": mean_outw, "mean_outb": mean_outb, "mean_upw": mean_upw, "mean_upb": mean_upb, "mean_downw": mean_downw, "mean_downb": mean_downb, "sqmean_adaw": sqmean_adaw, "sqmean_adab": sqmean_adab, "sqmean_qkvw": sqmean_qkvw, "sqmean_qkvb": sqmean_qkvb, "sqmean_outw": sqmean_outw, "sqmean_outb": sqmean_outb, "sqmean_upw": sqmean_upw, "sqmean_upb": sqmean_upb, "sqmean_downw": sqmean_downw, "sqmean_downb": sqmean_downb}


EPS_NORM = 1e-06
GELU_COEF = 0.7978845608
GELU_CUBE = 0.044715
BETA_ONE = 0.9
BETA_TWO = 0.999
LEARN_RATE = 0.05
EPS_ADAM = 1e-08

def rounded(values):
    return lax.optimization_barrier(values.astype(jnp.bfloat16)).astype(jnp.float32)

def normalize(values):
    center = values - lax.optimization_barrier(jnp.mean(values, axis=-1, keepdims=True))
    spread = lax.rsqrt(lax.optimization_barrier(jnp.mean(center * center, axis=-1, keepdims=True)) + EPS_NORM)
    return (center * spread, spread)

def norm_back(upstream, normed, spread):
    return spread * (upstream - lax.optimization_barrier(jnp.mean(upstream, axis=-1, keepdims=True)) - normed * lax.optimization_barrier(jnp.mean(upstream * normed, axis=-1, keepdims=True)))

def gelu_tanh(values):
    tanh_part = jnp.tanh(GELU_COEF * (values + GELU_CUBE * values * values * values))
    return 0.5 * values * (1.0 + tanh_part)

def gelu_slope(values):
    tanh_part = jnp.tanh(GELU_COEF * (values + GELU_CUBE * values * values * values))
    return 0.5 * (1.0 + tanh_part) + 0.5 * values * (1.0 - tanh_part * tanh_part) * GELU_COEF * (1.0 + 3.0 * GELU_CUBE * values * values)

def silu_slope(values):
    sigmoid_part = jax.nn.sigmoid(values)
    return sigmoid_part * (1.0 + values * (1.0 - sigmoid_part))

def adamw_step(parameter, gradient, first_mom, second):
    first_new = BETA_ONE * first_mom + (1.0 - BETA_ONE) * gradient
    second_new = BETA_TWO * second + (1.0 - BETA_TWO) * gradient * gradient
    first_hat = first_new / (1.0 - BETA_ONE ** STEP)
    second_hat = second_new / (1.0 - BETA_TWO ** STEP)
    return (parameter - LEARN_RATE * first_hat / (jnp.sqrt(second_hat) + EPS_ADAM), first_new, second_new)

def one_latent(tokens, upstream, modrow, params):
    mat_qkv, vec_qkv, mat_out, vec_out, mat_up, vec_up, mat_down, vec_down = params
    shift_att, scale_att, gate_att, shift_mlp, scale_mlp, gate_mlp = jnp.split(modrow, 6)
    seq_len = tokens.shape[0]
    scale = HD ** (-0.5)
    normed_att, spread_att = normalize(tokens)
    attn_in = (normed_att * (1.0 + scale_att) + shift_att).astype(jnp.bfloat16)
    qkv_all = rounded(jnp.dot(attn_in, mat_qkv, preferred_element_type=jnp.float32) + vec_qkv)
    queries = qkv_all[:, :MODEL_DIMENSION].reshape(seq_len, H, HD)
    keys_all = qkv_all[:, MODEL_DIMENSION:2 * MODEL_DIMENSION].reshape(seq_len, H, HD)
    values_all = qkv_all[:, 2 * MODEL_DIMENSION:].reshape(seq_len, H, HD)
    scores = jnp.einsum('qhd,khd->hqk', queries, keys_all) * scale
    row_max = lax.optimization_barrier(jnp.max(scores, axis=-1, keepdims=True))
    row_total = lax.optimization_barrier(jnp.sum(jnp.exp(scores - row_max), axis=-1, keepdims=True))
    attn_probs = jnp.exp(scores - row_max) / row_total
    probs_wide = rounded(attn_probs)
    attended = jnp.einsum('hqk,khd->qhd', probs_wide, values_all)
    attended_b = attended.reshape(seq_len, MODEL_DIMENSION).astype(jnp.bfloat16)
    branch_att = jnp.dot(attended_b, mat_out, preferred_element_type=jnp.float32) + vec_out
    middle = tokens + gate_att * branch_att
    normed_mlp, spread_mlp = normalize(middle)
    mlp_in = (normed_mlp * (1.0 + scale_mlp) + shift_mlp).astype(jnp.bfloat16)
    hidden = jnp.dot(mlp_in, mat_up, preferred_element_type=jnp.float32) + vec_up
    activated = gelu_tanh(hidden).astype(jnp.bfloat16)
    branch_mlp = jnp.dot(activated, mat_down, preferred_element_type=jnp.float32) + vec_down
    block_output = middle + gate_mlp * branch_mlp
    back_down = upstream * gate_mlp
    back_down_b = back_down.astype(jnp.bfloat16)
    grad_downw = jnp.dot(activated.T, back_down_b, preferred_element_type=jnp.float32)
    grad_downb = lax.optimization_barrier(jnp.sum(back_down, axis=0))
    back_hidden = jnp.dot(back_down_b, mat_down.T, preferred_element_type=jnp.float32) * gelu_slope(hidden)
    back_hidden_b = back_hidden.astype(jnp.bfloat16)
    grad_upw = jnp.dot(mlp_in.T, back_hidden_b, preferred_element_type=jnp.float32)
    grad_upb = lax.optimization_barrier(jnp.sum(back_hidden, axis=0))
    back_mlp_in = jnp.dot(back_hidden_b, mat_up.T, preferred_element_type=jnp.float32)
    back_middle = upstream + norm_back(back_mlp_in * (1.0 + scale_mlp), normed_mlp, spread_mlp)
    back_att = back_middle * gate_att
    back_att_b = back_att.astype(jnp.bfloat16)
    grad_outw = jnp.dot(attended_b.T, back_att_b, preferred_element_type=jnp.float32)
    grad_outb = lax.optimization_barrier(jnp.sum(back_att, axis=0))
    back_attended = rounded(jnp.dot(back_att_b, mat_out.T, preferred_element_type=jnp.float32)).reshape(seq_len, H, HD)
    back_probs = jnp.einsum('qhd,khd->hqk', back_attended, values_all)
    row_delta = jnp.einsum('qhd,qhd->hq', back_attended, attended)[:, :, None]
    back_scores = rounded(attn_probs * (back_probs - row_delta) * scale)
    back_queries = jnp.einsum('hqk,khd->qhd', back_scores, keys_all).reshape(seq_len, MODEL_DIMENSION)
    back_keys = jnp.einsum('hqk,qhd->khd', back_scores, queries).reshape(seq_len, MODEL_DIMENSION)
    back_values = jnp.einsum('hqk,qhd->khd', probs_wide, back_attended).reshape(seq_len, MODEL_DIMENSION)
    back_qkv = jnp.concatenate([back_queries, back_keys, back_values], axis=1)
    back_qkv_b = back_qkv.astype(jnp.bfloat16)
    grad_qkvw = jnp.dot(attn_in.T, back_qkv_b, preferred_element_type=jnp.float32)
    grad_qkvb = lax.optimization_barrier(jnp.sum(back_qkv, axis=0))
    back_attn_in = jnp.dot(back_qkv_b, mat_qkv.T, preferred_element_type=jnp.float32)
    back_tokens = back_middle + norm_back(back_attn_in * (1.0 + scale_att), normed_att, spread_att)
    modgrad = jnp.concatenate([lax.optimization_barrier(jnp.sum(back_attn_in, axis=0)), lax.optimization_barrier(jnp.sum(back_attn_in * normed_att, axis=0)), lax.optimization_barrier(jnp.sum(back_middle * branch_att, axis=0)), lax.optimization_barrier(jnp.sum(back_mlp_in, axis=0)), lax.optimization_barrier(jnp.sum(back_mlp_in * normed_mlp, axis=0)), lax.optimization_barrier(jnp.sum(upstream * branch_mlp, axis=0))])
    gradients = (grad_qkvw, grad_qkvb, grad_outw, grad_outb, grad_upw, grad_upb, grad_downw, grad_downb)
    return (block_output, back_tokens, modgrad, gradients)

def reference(latents, condition, slot_latent, slot_counts, output_gradient, ada_weight, ada_bias, qkv_weight, qkv_bias, out_weight, out_bias, up_weight, up_bias, down_weight, down_bias, mean_adaw, mean_adab, mean_qkvw, mean_qkvb, mean_outw, mean_outb, mean_upw, mean_upb, mean_downw, mean_downb, sqmean_adaw, sqmean_adab, sqmean_qkvw, sqmean_qkvb, sqmean_outw, sqmean_outb, sqmean_upw, sqmean_upb, sqmean_downw, sqmean_downb):
    live_slots = (jnp.arange(SLOTS)[None, :] < slot_counts[:, None]).reshape(-1)
    latent_ids = slot_latent.reshape(-1)
    slot_matches = (latent_ids[:, None] == jnp.arange(LAT)[None, :]) & live_slots[:, None]
    slot_lookup = lax.optimization_barrier(jnp.sum(jnp.where(slot_matches, jnp.arange(SLOT_COUNT)[:, None], 0), axis=0)).astype(jnp.int32)
    silu_cond = jax.nn.silu(condition).astype(jnp.bfloat16)
    modulation = jnp.dot(silu_cond, ada_weight.astype(jnp.bfloat16), preferred_element_type=jnp.float32) + rounded(ada_bias)
    params = (qkv_weight.astype(jnp.bfloat16), rounded(qkv_bias), out_weight.astype(jnp.bfloat16), rounded(out_bias), up_weight.astype(jnp.bfloat16), rounded(up_bias), down_weight.astype(jnp.bfloat16), rounded(down_bias))
    starting = tuple((jnp.zeros(item.shape, jnp.float32) for item in (qkv_weight, qkv_bias, out_weight, out_bias, up_weight, up_bias, down_weight, down_bias)))

    def scan_step(totals, latent_index):
        slot_index = slot_lookup[latent_index]
        tokens = lax.dynamic_index_in_dim(latents, slot_index, 0, keepdims=False)
        upstream = lax.dynamic_index_in_dim(output_gradient, slot_index, 0, keepdims=False)
        block_output, back_tokens, modgrad, gradients = one_latent(tokens, upstream, modulation[latent_index], params)
        totals = jax.tree.map(jnp.add, totals, gradients)
        return (totals, (block_output, back_tokens, modgrad))
    totals, (forward_results, backward_results, modgrads) = lax.scan(scan_step, starting, jnp.arange(LAT))
    block_output = jnp.zeros((SLOT_COUNT, LATENT_TOKENS, MODEL_DIMENSION), jnp.float32).at[slot_lookup].set(forward_results)
    latent_gradient = jnp.zeros((SLOT_COUNT, LATENT_TOKENS, MODEL_DIMENSION), jnp.float32).at[slot_lookup].set(backward_results)
    grad_adaw = jnp.dot(rounded(jax.nn.silu(condition)).T, modgrads, precision=lax.Precision.HIGHEST)
    grad_adab = lax.optimization_barrier(jnp.sum(modgrads, axis=0))
    condition_grad = jnp.dot(modgrads, rounded(ada_weight).T, precision=lax.Precision.HIGHEST) * silu_slope(condition)
    grads_all = (grad_adaw, grad_adab) + tuple(totals)
    params_all = (ada_weight, ada_bias, qkv_weight, qkv_bias, out_weight, out_bias, up_weight, up_bias, down_weight, down_bias)
    means_all = (mean_adaw, mean_adab, mean_qkvw, mean_qkvb, mean_outw, mean_outb, mean_upw, mean_upb, mean_downw, mean_downb)
    squares_all = (sqmean_adaw, sqmean_adab, sqmean_qkvw, sqmean_qkvb, sqmean_outw, sqmean_outb, sqmean_upw, sqmean_upb, sqmean_downw, sqmean_downb)
    updates = [adamw_step(p_item, g_item, m_item, v_item) for p_item, g_item, m_item, v_item in zip(params_all, grads_all, means_all, squares_all)]
    newvals = tuple((entry[0] for entry in updates))
    newmeans = tuple((entry[1] for entry in updates))
    newsqrs = tuple((entry[2] for entry in updates))
    return (block_output, latent_gradient, condition_grad) + grads_all + newvals + newmeans + newsqrs
```

```python
import functools

import jax
import jax.numpy as jnp
from jax import lax
from jax.experimental import pallas as pl
from jax.experimental.pallas import tpu as pltpu
from jax.sharding import PartitionSpec as P

H = 16
HD = 72
STEP = 2


EPS_NORM = 1e-06
GELU_COEF = 0.7978845608
GELU_CUBE = 0.044715
BETA_ONE = 0.9
BETA_TWO = 0.999
LEARN_RATE = 0.05
EPS_ADAM = 1e-08


def rounded(values):
    return lax.optimization_barrier(values.astype(jnp.bfloat16)).astype(jnp.float32)


def normalize(values):
    center = values - jnp.mean(values, axis=-1, keepdims=True)
    spread = lax.rsqrt(jnp.mean(center * center, axis=-1, keepdims=True) + EPS_NORM)
    return (center * spread, spread)


def norm_back(upstream, normed, spread):
    return spread * (
        upstream
        - jnp.mean(upstream, axis=-1, keepdims=True)
        - normed * jnp.mean(upstream * normed, axis=-1, keepdims=True)
    )


def gelu_tanh(values):
    tanh_part = jnp.tanh(GELU_COEF * (values + GELU_CUBE * values * values * values))
    return 0.5 * values * (1.0 + tanh_part)


def gelu_slope(values):
    tanh_part = jnp.tanh(GELU_COEF * (values + GELU_CUBE * values * values * values))
    return 0.5 * (1.0 + tanh_part) + 0.5 * values * (1.0 - tanh_part * tanh_part) * GELU_COEF * (
        1.0 + 3.0 * GELU_CUBE * values * values
    )


def silu_slope(values):
    sigmoid_part = jax.nn.sigmoid(values)
    return sigmoid_part * (1.0 + values * (1.0 - sigmoid_part))


def adamw_step(parameter, gradient, first_mom, second):
    first_new = BETA_ONE * first_mom + (1.0 - BETA_ONE) * gradient
    second_new = BETA_TWO * second + (1.0 - BETA_TWO) * gradient * gradient
    first_hat = first_new / (1.0 - BETA_ONE**STEP)
    second_hat = second_new / (1.0 - BETA_TWO**STEP)
    return (
        parameter - LEARN_RATE * first_hat / (jnp.sqrt(second_hat) + EPS_ADAM),
        first_new,
        second_new,
    )


def flat_index(axes):
    index = lax.axis_index(axes[0])
    for axis in axes[1:]:
        index = index * lax.axis_size(axis) + lax.axis_index(axis)
    return index


def swap_bit(values, axes, step):
    total = 1
    for axis in axes:
        total *= lax.axis_size(axis)
    return lax.ppermute(values, axes, [(i, i ^ step) for i in range(total)])


def axes_size(axes):
    total = 1
    for axis in axes:
        total *= lax.axis_size(axis)
    return total


def gather_tree(values, axes):
    index, blocks, step = flat_index(axes), values[None], 1
    while step < axes_size(axes):
        other = swap_bit(blocks, axes, step)
        upper = (index // step) % 2 == 1
        blocks = jnp.concatenate(
            [jnp.where(upper, other, blocks), jnp.where(upper, blocks, other)], axis=0
        )
        step *= 2
    return blocks


def scatter_tree(blocks, axes, sent=None):
    index, step = flat_index(axes), axes_size(axes) // 2
    while step >= 1:
        low, high = blocks[:step], blocks[step:]
        upper = (index // step) % 2 == 1
        away = jnp.where(upper, low, high)
        if sent is not None:
            away = away.astype(sent)
        kept = jnp.where(upper, high, low)
        blocks = kept + swap_bit(away, axes, step).astype(kept.dtype)
        step //= 2
    return blocks[0]


def sum_tree(values, axes):
    step = 1
    while step < axes_size(axes):
        values = values + swap_bit(values, axes, step)
        step *= 2
    return values


def join_columns(halves, widths):
    parts, start = [], 0
    for width in widths:
        part = halves[:, :, start : start + width]
        parts.append(jnp.moveaxis(part, 0, 1).reshape(part.shape[1], -1))
        start += width
    return parts


def split_columns(parts):
    ways = lax.axis_size("seq")
    blocks = [
        jnp.moveaxis(part.reshape(part.shape[0], ways, -1), 1, 0) for part in parts
    ]
    return jnp.concatenate(blocks, axis=2)


def piece_moves(turn):
    rows, ways = lax.axis_size("dp"), lax.axis_size("seq")
    pairs = []
    for g in range(rows):
        for x in range(ways):
            piece = g * ways + (turn + x) % ways
            pairs.append((g * ways + x, (piece % rows) * ways + piece // rows))
    return pairs


def own_piece():
    return lax.axis_index("seq") * lax.axis_size("dp") + lax.axis_index("dp")


def pick(blocks, index):
    return lax.dynamic_index_in_dim(blocks, index, 0, keepdims=False)


def rows_from_owners(block):
    ways, x = lax.axis_size("seq"), lax.axis_index("seq")
    pieces = block.reshape(ways, -1, block.shape[1])
    got = jnp.stack(
        [
            lax.ppermute(pick(pieces, (turn + x) % ways), ("dp", "seq"), piece_moves(turn))
            for turn in range(ways)
        ]
    )
    place = own_piece() % ways
    return jnp.concatenate([pick(got, (place - i + ways) % ways) for i in range(ways)], axis=1)


def rows_to_owners(piece):
    ways, x = lax.axis_size("seq"), lax.axis_index("seq")
    columns = jnp.moveaxis(piece.reshape(piece.shape[0], ways, -1), 1, 0)
    place = own_piece() % ways
    got = jnp.stack(
        [
            lax.ppermute(
                pick(columns, (place - turn + ways) % ways),
                ("dp", "seq"),
                [(taker, owner) for owner, taker in piece_moves(turn)],
            )
            for turn in range(ways)
        ]
    )
    ordered = jnp.stack([pick(got, (q - x + ways) % ways) for q in range(ways)])
    return ordered.reshape(-1, ordered.shape[2])


def all_tokens(values):
    return gather_tree(values, ("seq",)).reshape(-1, values.shape[1])


def own_tokens(terms):
    blocks = terms.reshape(lax.axis_size("seq"), -1, terms.shape[1])
    return scatter_tree(blocks, ("seq",), jnp.bfloat16)


def weight_term(left, right):
    return jnp.einsum("rc,rd->cd", left, right, preferred_element_type=jnp.float32).astype(
        jnp.bfloat16
    )


def spread_terms(terms):
    widths = [term.shape[1] // lax.axis_size("seq") for term in terms]
    joined = jnp.concatenate(terms, axis=1) if len(terms) > 1 else terms[0]
    rows = lax.psum_scatter(joined, "dp", scatter_dimension=0, tiled=True)
    pieces, start = [], 0
    for term in terms:
        pieces.append(rows[:, start : start + term.shape[1]])
        start += term.shape[1]
    own = scatter_tree(split_columns(pieces).astype(jnp.float32), ("seq",), jnp.bfloat16)
    blocks, start = [], 0
    for width in widths:
        blocks.append(own[:, start : start + width])
        start += width
    return blocks


def on_device_general(
    latents,
    condition,
    slot_latent,
    slot_counts,
    output_gradient,
    ada_weight,
    ada_bias,
    qkv_weight,
    qkv_bias,
    out_weight,
    out_bias,
    up_weight,
    up_bias,
    down_weight,
    down_bias,
    mean_adaw,
    mean_adab,
    mean_qkvw,
    mean_qkvb,
    mean_outw,
    mean_outb,
    mean_upw,
    mean_upb,
    mean_downw,
    mean_downb,
    sqmean_adaw,
    sqmean_adab,
    sqmean_qkvw,
    sqmean_qkvb,
    sqmean_outw,
    sqmean_outb,
    sqmean_upw,
    sqmean_upb,
    sqmean_downw,
    sqmean_downb,
):
    slot_total, tok_dev, model_width = latents.shape
    row_count = slot_total * tok_dev
    scale = HD ** (-0.5)
    live_slots = jnp.arange(slot_total) < slot_counts[0]
    live_mask = live_slots[:, None, None]
    latent_count = condition.shape[0]
    slot_matches = (
        (slot_latent[0][:, None] == jnp.arange(latent_count)[None, :]) & live_slots[:, None]
    ).astype(jnp.float32)
    silu_cond = jax.nn.silu(condition).astype(jnp.bfloat16)
    mod_cols = jnp.dot(
        silu_cond, ada_weight.astype(jnp.bfloat16), preferred_element_type=jnp.float32
    ) + rounded(ada_bias)
    modulation = jnp.moveaxis(gather_tree(mod_cols, ("dp", "seq")), 0, 1).reshape(
        latent_count, -1
    )
    slot_mod = jnp.dot(slot_matches, modulation, precision=lax.Precision.HIGHEST)[:, None, :]
    shift_att, scale_att, gate_att, shift_mlp, scale_mlp, gate_mlp = jnp.split(slot_mod, 6, axis=2)
    upstream = jnp.where(live_mask, output_gradient, 0.0)
    biases = (qkv_bias, out_bias, down_bias)
    bias_rows = gather_tree(
        jnp.concatenate(biases).astype(jnp.bfloat16)[None], ("seq",)
    )
    vec_qkv, vec_out, vec_down = (
        part[0].astype(jnp.float32)
        for part in join_columns(bias_rows, [item.shape[0] for item in biases])
    )
    wide = (qkv_weight, out_weight)
    wide_halves = gather_tree(jnp.concatenate(wide, axis=1).astype(jnp.bfloat16), ("seq",))
    wide_rows = jnp.concatenate(
        join_columns(wide_halves, [item.shape[1] for item in wide])
        + [up_weight.astype(jnp.bfloat16)],
        axis=1,
    )
    wide_full = lax.all_gather(wide_rows, "dp", axis=0, tiled=True)
    qkv_end = 3 * model_width
    mat_qkv = wide_full[:, :qkv_end]
    mat_out = wide_full[:, qkv_end : qkv_end + model_width]
    mat_up = wide_full[:, qkv_end + model_width :]
    down_rows = rows_from_owners(down_weight.astype(jnp.bfloat16))
    mat_down = lax.all_gather(down_rows, "dp", axis=0, tiled=True)
    normed_att, spread_att = normalize(latents)
    attn_in = (
        (normed_att * (1.0 + scale_att) + shift_att)
        .astype(jnp.bfloat16)
        .reshape(row_count, model_width)
    )
    qkv_all = (jnp.dot(attn_in, mat_qkv, preferred_element_type=jnp.float32) + vec_qkv).astype(
        jnp.bfloat16
    )
    queries = qkv_all[:, :model_width].reshape(slot_total, tok_dev, H, HD)
    keys_own = qkv_all[:, model_width : 2 * model_width].reshape(slot_total, tok_dev, model_width)
    values_own = qkv_all[:, 2 * model_width :].reshape(slot_total, tok_dev, model_width)
    pairs_own = jnp.concatenate([keys_own, values_own], axis=2)
    pairs_all = jnp.moveaxis(gather_tree(pairs_own, ("seq",)), 0, 1)
    pairs_all = pairs_all.reshape(slot_total, -1, 2 * model_width)
    keys_all, values_all = pairs_all[:, :, :model_width], pairs_all[:, :, model_width:]
    keys_heads = keys_all.reshape(slot_total, -1, H, HD)
    values_heads = values_all.reshape(slot_total, -1, H, HD)
    scores = (
        jnp.einsum("sqhd,skhd->shqk", queries, keys_heads, preferred_element_type=jnp.float32)
        * scale
    )
    row_max = jnp.max(scores, axis=-1, keepdims=True)
    row_total = jnp.sum(jnp.exp(scores - row_max), axis=-1, keepdims=True)
    attn_probs = jnp.exp(scores - row_max) / row_total
    probs_b = attn_probs.astype(jnp.bfloat16)
    attended = jnp.einsum(
        "shqk,skhd->sqhd", probs_b, values_heads, preferred_element_type=jnp.float32
    )
    attended_b = attended.reshape(row_count, model_width).astype(jnp.bfloat16)
    branch_att = (
        jnp.dot(attended_b, mat_out, preferred_element_type=jnp.float32) + vec_out
    ).reshape(slot_total, tok_dev, model_width)
    middle = latents + gate_att * branch_att
    normed_mlp, spread_mlp = normalize(middle)
    mlp_in = (
        (normed_mlp * (1.0 + scale_mlp) + shift_mlp)
        .astype(jnp.bfloat16)
        .reshape(row_count, model_width)
    )
    mlp_all = all_tokens(mlp_in)
    hidden = jnp.dot(mlp_all, mat_up, preferred_element_type=jnp.float32) + rounded(up_bias)
    activated = gelu_tanh(hidden).astype(jnp.bfloat16)
    activated, mat_down = lax.optimization_barrier((activated, mat_down))
    branch_mlp = (
        own_tokens(jnp.dot(activated, mat_down, preferred_element_type=jnp.float32)) + vec_down
    ).reshape(slot_total, tok_dev, model_width)
    block_output = jnp.where(live_mask, middle + gate_mlp * branch_mlp, 0.0)
    back_down = upstream * gate_mlp
    back_down_b = back_down.astype(jnp.bfloat16).reshape(row_count, model_width)
    back_down_all = all_tokens(back_down_b)
    down_sums = lax.psum_scatter(
        weight_term(activated, back_down_all), "dp", scatter_dimension=0, tiled=True
    )
    grad_downw = rows_to_owners(down_sums).astype(jnp.float32)
    sum_downb = jnp.sum(back_down, axis=(0, 1))
    back_hidden = jnp.einsum(
        "rd,fd->rf", back_down_all, mat_down, preferred_element_type=jnp.float32
    ) * gelu_slope(hidden)
    back_hidden_b = back_hidden.astype(jnp.bfloat16)
    grad_upw = lax.psum_scatter(
        weight_term(mlp_all, back_hidden_b), "dp", scatter_dimension=0, tiled=True
    ).astype(jnp.float32)
    up_total = jnp.zeros((lax.axis_size("seq") * up_bias.shape[0],), jnp.float32)
    sum_upb = lax.dynamic_update_slice_in_dim(
        up_total, jnp.sum(back_hidden, axis=0), lax.axis_index("seq") * up_bias.shape[0], 0
    )
    back_mlp_in = own_tokens(
        jnp.einsum("rf,cf->rc", back_hidden_b, mat_up, preferred_element_type=jnp.float32)
    ).reshape(slot_total, tok_dev, model_width)
    back_middle = upstream + norm_back(back_mlp_in * (1.0 + scale_mlp), normed_mlp, spread_mlp)
    back_att = back_middle * gate_att
    back_att_b = back_att.astype(jnp.bfloat16).reshape(row_count, model_width)
    term_out = weight_term(attended_b, back_att_b)
    sum_outb = jnp.sum(back_att, axis=(0, 1))
    back_attended = jnp.einsum(
        "rd,cd->rc", back_att_b, mat_out, preferred_element_type=jnp.float32
    ).astype(jnp.bfloat16)
    back_attended = back_attended.reshape(slot_total, tok_dev, H, HD)
    back_probs = jnp.einsum(
        "sqhd,skhd->shqk", back_attended, values_heads, preferred_element_type=jnp.float32
    )
    row_delta = jnp.einsum("sqhd,sqhd->shq", back_attended.astype(jnp.float32), attended)[..., None]
    back_scores = (attn_probs * (back_probs - row_delta) * scale).astype(jnp.bfloat16)
    back_queries = jnp.einsum(
        "shqk,skhd->sqhd", back_scores, keys_heads, preferred_element_type=jnp.float32
    )
    key_terms = jnp.einsum(
        "shqk,sqhd->skhd", back_scores, queries, preferred_element_type=jnp.float32
    ).reshape(slot_total, -1, model_width)
    value_terms = jnp.einsum(
        "shqk,sqhd->skhd", probs_b, back_attended, preferred_element_type=jnp.float32
    ).reshape(slot_total, -1, model_width)
    pair_terms = jnp.concatenate([key_terms, value_terms], axis=2)
    pair_terms = pair_terms.reshape(slot_total, -1, tok_dev, 2 * model_width)
    back_pairs = scatter_tree(jnp.moveaxis(pair_terms, 1, 0), ("seq",), jnp.bfloat16)
    back_keys, back_values = back_pairs[:, :, :model_width], back_pairs[:, :, model_width:]
    back_qkv = jnp.concatenate(
        [
            back_queries.reshape(row_count, model_width),
            back_keys.reshape(row_count, model_width),
            back_values.reshape(row_count, model_width),
        ],
        axis=1,
    )
    back_qkv_b = back_qkv.astype(jnp.bfloat16)
    term_qkv = weight_term(attn_in, back_qkv_b)
    grad_qkvw, grad_outw = spread_terms([term_qkv, term_out])
    sum_qkvb = jnp.sum(back_qkv, axis=0)
    back_attn_in = jnp.einsum(
        "rd,cd->rc", back_qkv_b, mat_qkv, preferred_element_type=jnp.float32
    ).reshape(slot_total, tok_dev, model_width)
    latent_gradient = jnp.where(
        live_mask,
        back_middle + norm_back(back_attn_in * (1.0 + scale_att), normed_att, spread_att),
        0.0,
    )
    slot_modgrad = jnp.concatenate(
        [
            jnp.sum(back_attn_in, axis=1),
            jnp.sum(back_attn_in * normed_att, axis=1),
            jnp.sum(back_middle * branch_att, axis=1),
            jnp.sum(back_mlp_in, axis=1),
            jnp.sum(back_mlp_in * normed_mlp, axis=1),
            jnp.sum(upstream * branch_mlp, axis=1),
        ],
        axis=1,
    )
    modgrad_table = jnp.dot(slot_matches.T, slot_modgrad, precision=lax.Precision.HIGHEST)
    modgrad_cols = scatter_tree(
        jnp.moveaxis(modgrad_table.reshape(latent_count, -1, ada_bias.shape[0]), 1, 0),
        ("dp", "seq"),
    )
    grad_adaw = jnp.dot(
        rounded(jax.nn.silu(condition)).T, modgrad_cols, precision=lax.Precision.HIGHEST
    )
    grad_adab = jnp.sum(modgrad_cols, axis=0)
    cond_term = jnp.dot(modgrad_cols, rounded(ada_weight).T, precision=lax.Precision.HIGHEST)
    cond_sum = sum_tree(cond_term, ("dp", "seq"))
    bias_sums = (sum_qkvb, sum_outb, sum_upb, sum_downb)
    totals, start, bias_totals = sum_tree(jnp.concatenate(bias_sums), ("dp", "seq")), 0, []
    for item in bias_sums:
        bias_totals.append(totals[start : start + item.shape[0]])
        start += item.shape[0]
    total_qkvb, total_outb, total_upb, total_downb = bias_totals
    condition_grad = cond_sum * silu_slope(condition)
    seq_index = lax.axis_index("seq")

    def own_part(full_sum, local_bias):
        length = local_bias.shape[0]
        return lax.dynamic_slice_in_dim(full_sum, seq_index * length, length)

    grad_qkvb = own_part(total_qkvb, qkv_bias)
    grad_outb = own_part(total_outb, out_bias)
    grad_upb = own_part(total_upb, up_bias)
    grad_downb = own_part(total_downb, down_bias)
    grads_all = (
        grad_adaw,
        grad_adab,
        grad_qkvw,
        grad_qkvb,
        grad_outw,
        grad_outb,
        grad_upw,
        grad_upb,
        grad_downw,
        grad_downb,
    )
    params_all = (
        ada_weight,
        ada_bias,
        qkv_weight,
        qkv_bias,
        out_weight,
        out_bias,
        up_weight,
        up_bias,
        down_weight,
        down_bias,
    )
    means_all = (
        mean_adaw,
        mean_adab,
        mean_qkvw,
        mean_qkvb,
        mean_outw,
        mean_outb,
        mean_upw,
        mean_upb,
        mean_downw,
        mean_downb,
    )
    squares_all = (
        sqmean_adaw,
        sqmean_adab,
        sqmean_qkvw,
        sqmean_qkvb,
        sqmean_outw,
        sqmean_outb,
        sqmean_upw,
        sqmean_upb,
        sqmean_downw,
        sqmean_downb,
    )
    updates = [
        adamw_step(p_item, g_item, m_item, v_item)
        for p_item, g_item, m_item, v_item in zip(params_all, grads_all, means_all, squares_all)
    ]
    newvals = tuple((entry[0] for entry in updates))
    newmeans = tuple((entry[1] for entry in updates))
    newsqrs = tuple((entry[2] for entry in updates))
    return (
        (block_output, latent_gradient, condition_grad) + grads_all + newvals + newmeans + newsqrs
    )


MESH_ID = pl.DeviceIdType.MESH
ANY = pl.BlockSpec(memory_space=pl.ANY)
VMEM = pl.BlockSpec(memory_space=pltpu.VMEM)


def params_of(number):
    return pltpu.CompilerParams(
        collective_id=number, has_side_effects=True, vmem_limit_bytes=56 * 2**20
    )


def place():
    group, x = lax.axis_index("dp"), lax.axis_index("seq")
    core, chip = group % 2, group // 2
    return chip // 2, chip % 2, core, x


def device(a, b, core, x):
    return ((a * 2 + b) * 2 + core, x)


def remote(src, dst, send, recv, target):
    return pltpu.make_async_remote_copy(
        src_ref=src,
        dst_ref=dst,
        send_sem=send,
        recv_sem=recv,
        device_id=target,
        device_id_type=MESH_ID,
    )


def greet_grid(lines):
    a, b, core, x = place()
    barrier = pltpu.get_barrier_semaphore()

    def greet(target):
        pl.semaphore_signal(barrier, inc=1, device_id=target, device_id_type=MESH_ID)

    greet(device(a, 1 - b, core, x))
    pl.when(a > 0)(lambda: greet(device(a - 1, b, core, x)))
    pl.when(a < lines - 1)(lambda: greet(device(a + 1, b, core, x)))
    pl.semaphore_wait(barrier, 1 + (a > 0).astype(jnp.int32) + (a < lines - 1).astype(jnp.int32))


def greet_four():
    a, b, core, x = place()
    barrier = pltpu.get_barrier_semaphore()
    for target in (device(a, b, 1 - core, x), device(a, b, core, 1 - x)):
        pl.semaphore_signal(barrier, inc=1, device_id=target, device_id_type=MESH_ID)
    pl.semaphore_wait(barrier, 2)


def gather_grid_kernel(lines, count, *refs):
    ins, outs = refs[:count], refs[count : 2 * count]
    keep, up_send, down_send, side_send, line_recv, side_recv = refs[2 * count :]
    a, b, core, x = place()
    own = a * 2 + b
    copies = [pltpu.make_async_copy(ins[p], outs[p].at[own], keep.at[p]) for p in range(count)]
    greet_grid(lines)

    def up(p, s, src):
        return remote(
            src, outs[p].at[s * 2 + b], up_send.at[p, s], line_recv.at[p, s],
            device(a + 1, b, core, x),
        )

    def down(p, s, src):
        return remote(
            src, outs[p].at[s * 2 + b], down_send.at[p, s], line_recv.at[p, s],
            device(a - 1, b, core, x),
        )

    def side(p, s, src):
        return remote(
            src, outs[p].at[s * 2 + b], side_send.at[p, s], side_recv.at[p, s],
            device(a, 1 - b, core, x),
        )

    def arrived(p, s):
        block = outs[p].at[s * 2 + b]
        remote(
            block, block, up_send.at[p, s], line_recv.at[p, s], device(a, 1 - b, core, x)
        ).wait_recv()
        return block

    for p in range(count):
        pl.when(a < lines - 1)(lambda: up(p, a, ins[p]).start())
        pl.when(a > 0)(lambda: down(p, a, ins[p]).start())
        side(p, a, ins[p]).start()
        copies[p].start()
    for hop in range(1, lines):
        for p in range(count):

            def from_below():
                block = arrived(p, a - hop)
                pl.when(a < lines - 1)(lambda: up(p, a - hop, block).start())
                side(p, a - hop, block).start()

            def from_above():
                block = arrived(p, a + hop)
                pl.when(a > 0)(lambda: down(p, a + hop, block).start())
                side(p, a + hop, block).start()

            pl.when(a - hop >= 0)(from_below)
            pl.when(a + hop < lines)(from_above)
    for p in range(count):
        copies[p].wait()
        for s in range(lines):
            block = outs[p].at[s * 2 + 1 - b]
            remote(
                block, block, side_send.at[p, s], side_recv.at[p, s], device(a, 1 - b, core, x)
            ).wait_recv()
            sent = outs[p].at[s * 2 + b]
            side(p, s, sent).wait_send()
            pl.when((s <= a) & (a < lines - 1))(lambda: up(p, s, sent).wait_send())
            pl.when((s >= a) & (a > 0))(lambda: down(p, s, sent).wait_send())


def gather_grid(pieces, number):
    lines, count = lax.axis_size("dp") // 4, len(pieces)
    dma = pltpu.SemaphoreType.DMA
    return pl.pallas_call(
        functools.partial(gather_grid_kernel, lines, count),
        out_shape=[
            jax.ShapeDtypeStruct((2 * lines,) + piece.shape, piece.dtype) for piece in pieces
        ],
        in_specs=[ANY] * count,
        out_specs=[ANY] * count,
        scratch_shapes=[dma((count,))] + [dma((count, lines))] * 5,
        compiler_params=params_of(number),
        name="gather_grid",
    )(*pieces)


def strips(rows):
    return 48 if rows % 48 == 0 else rows


def reduce_grid_kernel(lines, count, *refs):
    ins, outs = refs[:count], refs[count : 2 * count]
    held, lower, upper = (refs[(2 + i) * count : (3 + i) * count] for i in range(3))
    up_send, down_send, side_send, up_recv, down_recv, side_recv = refs[5 * count :]
    a, b, core, x = place()
    greet_grid(lines)

    def side(p, t):
        return remote(
            ins[p].at[t * 2 + 1 - b], held[p].at[t], side_send.at[p, t], side_recv.at[p, t],
            device(a, 1 - b, core, x),
        )

    def up(p, t):
        return remote(
            held[p].at[t], lower[p].at[t], up_send.at[p, t], up_recv.at[p, t],
            device(a + 1, b, core, x),
        )

    def down(p, t):
        return remote(
            held[p].at[t], upper[p].at[t], down_send.at[p, t], down_recv.at[p, t],
            device(a - 1, b, core, x),
        )

    def sum_into(p, t, target, others):
        rows = ins[p].shape[1]
        step = strips(rows)

        def strip(i, carry):
            part = pl.ds(i * step, step)
            total = ins[p][t * 2 + b, part, :].astype(jnp.float32)
            for other in others:
                total = total + other[part, :].astype(jnp.float32)
            target[part, :] = total.astype(target.dtype)
            return carry

        lax.fori_loop(0, rows // step, strip, 0)

    order = []
    for i in range(lines):
        order.append(lines - 1 - i // 2 if i % 2 == 0 else i // 2)
    for p in range(count):
        for t in order:
            side(p, t).start()
    for p in range(count):
        for t in order:
            side(p, t).wait_recv()
            mine = held[p].at[t]

            def upward():
                def joined():
                    up(p, t).wait_recv()
                    sum_into(p, t, mine, [mine, lower[p].at[t]])

                pl.when(a > 0)(joined)
                pl.when(a == 0)(lambda: sum_into(p, t, mine, [mine]))
                up(p, t).start()

            def downward():
                def joined():
                    down(p, t).wait_recv()
                    sum_into(p, t, mine, [mine, upper[p].at[t]])

                pl.when(a < lines - 1)(joined)
                pl.when(a == lines - 1)(lambda: sum_into(p, t, mine, [mine]))
                down(p, t).start()

            pl.when(a < t)(upward)
            pl.when(a > t)(downward)
    for p in range(count):
        terms = held[p].at[a], lower[p].at[a], upper[p].at[a]
        pl.when(a > 0)(lambda: up(p, a).wait_recv())
        pl.when(a < lines - 1)(lambda: down(p, a).wait_recv())
        pl.when(a == 0)(lambda: sum_into(p, a, outs[p], [terms[0], terms[2]]))
        pl.when(a == lines - 1)(lambda: sum_into(p, a, outs[p], [terms[0], terms[1]]))
        pl.when((a > 0) & (a < lines - 1))(lambda: sum_into(p, a, outs[p], terms))
    for p in range(count):
        for t in range(lines):
            side(p, t).wait_send()
            pl.when(a < t)(lambda: up(p, t).wait_send())
            pl.when(a > t)(lambda: down(p, t).wait_send())


def reduce_grid(pieces, number):
    lines, count = lax.axis_size("dp") // 4, len(pieces)
    dma = pltpu.SemaphoreType.DMA
    slots = [pltpu.VMEM((lines,) + piece.shape[1:], piece.dtype) for piece in pieces]
    return pl.pallas_call(
        functools.partial(reduce_grid_kernel, lines, count),
        out_shape=[jax.ShapeDtypeStruct(piece.shape[1:], piece.dtype) for piece in pieces],
        in_specs=[VMEM] * count,
        out_specs=[VMEM] * count,
        scratch_shapes=slots * 3 + [dma((count, lines))] * 6,
        compiler_params=params_of(number),
        name="reduce_grid",
    )(*pieces)


def gather_four_kernel(count, *refs):
    ins, outs = refs[:count], refs[count : 2 * count]
    keep, sib_send, x_send, fwd_send, sib_recv, x_recv, fwd_recv = refs[2 * count :]
    a, b, core, x = place()
    own, across = core * 2 + x, core * 2 + 1 - x
    sibling, peer = device(a, b, 1 - core, x), device(a, b, core, 1 - x)
    greet_four()
    to_x, to_sib, to_fwd, copies = [], [], [], []
    for p in range(count):
        block, far = outs[p].at[own], outs[p].at[across]
        to_x.append(remote(ins[p], block, x_send.at[p], x_recv.at[p], peer))
        to_sib.append(remote(ins[p], block, sib_send.at[p], sib_recv.at[p], sibling))
        to_fwd.append(remote(far, far, fwd_send.at[p], fwd_recv.at[p], sibling))
        copies.append(pltpu.make_async_copy(ins[p], block, keep.at[p]))
    for p in range(count):
        to_x[p].start()
        to_sib[p].start()
        copies[p].start()
    for p in range(count):
        to_x[p].wait_recv()
        to_fwd[p].start()
    for p in range(count):
        to_sib[p].wait_recv()
        to_fwd[p].wait_recv()
        copies[p].wait()
        to_x[p].wait_send()
        to_sib[p].wait_send()
        to_fwd[p].wait_send()


def gather_four(pieces, number):
    count = len(pieces)
    return pl.pallas_call(
        functools.partial(gather_four_kernel, count),
        out_shape=[jax.ShapeDtypeStruct((4,) + piece.shape, piece.dtype) for piece in pieces],
        in_specs=[VMEM] * count,
        out_specs=[VMEM] * count,
        scratch_shapes=[pltpu.SemaphoreType.DMA((count,))] * 7,
        compiler_params=params_of(number),
        name="gather_four",
    )(*pieces)


def reduce_four_kernel(count, *refs):
    ins, outs = refs[:count], refs[count : 2 * count]
    near, out_x, in_x = (refs[(2 + i) * count : (3 + i) * count] for i in range(3))
    sib_send, sib_recv, x_send, x_recv = refs[5 * count :]
    a, b, core, x = place()
    own, across = core * 2 + x, core * 2 + 1 - x
    sibling, peer = device(a, b, 1 - core, x), device(a, b, core, 1 - x)
    greet_four()
    to_sib, to_x = [], []
    for p in range(count):
        to_sib.append(
            [
                remote(
                    ins[p].at[(1 - core) * 2 + side], near[p].at[i], sib_send.at[p, i],
                    sib_recv.at[p, i], sibling,
                )
                for i, side in enumerate((1 - x, x))
            ]
        )
        to_x.append(remote(out_x[p], in_x[p], x_send.at[p], x_recv.at[p], peer))
    for i in range(2):
        for p in range(count):
            to_sib[p][i].start()
    for p in range(count):
        to_sib[p][0].wait_recv()
        out_x[p][...] = (ins[p][across] + near[p][0]).astype(out_x[p].dtype)
        to_x[p].start()
    for p in range(count):
        to_sib[p][1].wait_recv()
        outs[p][...] = ins[p][own] + near[p][1]
    for p in range(count):
        to_x[p].wait_recv()
        outs[p][...] += in_x[p][...].astype(jnp.float32)
        to_x[p].wait_send()
        for i in range(2):
            to_sib[p][i].wait_send()


def reduce_four(pieces, number):
    count = len(pieces)
    dma = pltpu.SemaphoreType.DMA
    shapes = [piece.shape[1:] for piece in pieces]
    return pl.pallas_call(
        functools.partial(reduce_four_kernel, count),
        out_shape=[jax.ShapeDtypeStruct(shape, jnp.float32) for shape in shapes],
        in_specs=[VMEM] * count,
        out_specs=[VMEM] * count,
        scratch_shapes=[pltpu.VMEM((2,) + shape, jnp.float32) for shape in shapes]
        + [pltpu.VMEM(shape, jnp.bfloat16) for shape in shapes] * 2
        + [dma((count, 2))] * 2
        + [dma((count,))] * 2,
        compiler_params=params_of(number),
        name="reduce_four",
    )(*pieces)


def swap_core(values):
    return lax.ppermute(values, "dp", [(i, i ^ 1) for i in range(lax.axis_size("dp"))])


def swap_x(values):
    return lax.ppermute(values, "seq", [(0, 1), (1, 0)])


def row_moves(turn):
    groups = lax.axis_size("dp")
    chips, pairs = groups // 2, []
    for d in range(groups):
        for x in range(2):
            block = d * 2 + (turn + x) % 2
            f, c = block // chips, block % chips
            pairs.append((d * 2 + x, (c * 2 + f % 2) * 2 + f // 2))
    return pairs


def flip(pair, swapped):
    low = jnp.where(swapped, pair[1], pair[0])
    high = jnp.where(swapped, pair[0], pair[1])
    return low, high


def rows_to_blocks(pieces):
    x = lax.axis_index("seq")
    b = (lax.axis_index("dp") // 2) % 2
    sent = flip(pieces, x == 1)
    got = [lax.ppermute(sent[turn], ("dp", "seq"), row_moves(turn)) for turn in range(2)]
    return jnp.concatenate(flip(got, b == 1), axis=1)


def blocks_to_rows(block):
    x = lax.axis_index("seq")
    b = (lax.axis_index("dp") // 2) % 2
    half = block.shape[1] // 2
    sent = flip((block[:, :half], block[:, half:]), b == 1)
    got = [
        lax.ppermute(sent[turn], ("dp", "seq"), [(q, p) for p, q in row_moves(turn)])
        for turn in range(2)
    ]
    return flip(got, x == 1)


def cut(values, index, size, axis=1):
    return lax.dynamic_slice_in_dim(values, index * size, size, axis)


def gather_columns(qkv_block, up_block):
    x, core = lax.axis_index("seq"), lax.axis_index("dp") % 2
    width = qkv_block.shape[1] // 6
    first = x == 0
    got = swap_x(qkv_block[:, 2 * width : 4 * width])
    head, tail = qkv_block[:, : 2 * width], qkv_block[:, 4 * width :]
    queries = jnp.where(first, head, got)
    keys = jnp.where(first, tail, head)
    values = jnp.where(first, got, tail)
    high = core == 1

    def halves(block):
        size = block.shape[1] // 2
        low, up = block[:, :size], block[:, size:]
        return jnp.where(high, up, low), jnp.where(high, low, up)

    pairs = [halves(block) for block in (queries, keys, values, up_block)]
    mine = jnp.concatenate([pair[0] for pair in pairs], axis=1)
    other = swap_core(jnp.concatenate([pair[1] for pair in pairs], axis=1))
    full = jnp.concatenate(
        [jnp.where(high, other, mine), jnp.where(high, mine, other)], axis=0
    )
    return full[:, : 3 * width], full[:, 3 * width :]


def scatter_columns(qkv_block, up_block):
    x, core = lax.axis_index("seq"), lax.axis_index("dp") % 2
    width = qkv_block.shape[1] // 3
    first, high = x == 0, core == 1
    full = jnp.concatenate([qkv_block, up_block], axis=1)
    rows = full.shape[0] // 2
    low, up = full[:rows], full[rows:]
    mine = jnp.where(high, up, low)
    other = swap_core(jnp.where(high, low, up))
    parts = []
    for start, stop in ((0, width), (width, 2 * width), (2 * width, 3 * width), (3 * width, None)):
        own, far = mine[:, start:stop], other[:, start:stop]
        parts.append(
            jnp.concatenate([jnp.where(high, far, own), jnp.where(high, own, far)], axis=1)
        )
    queries, keys, values, up_rows = parts
    got = swap_x(jnp.where(first, values, queries))
    qkv_rows = jnp.concatenate(
        [jnp.where(first, queries, keys), got, jnp.where(first, keys, values)],
        axis=1,
    )
    return qkv_rows, up_rows


def on_device_grid(
    latents,
    condition,
    slot_latent,
    slot_counts,
    output_gradient,
    ada_weight,
    ada_bias,
    qkv_weight,
    qkv_bias,
    out_weight,
    out_bias,
    up_weight,
    up_bias,
    down_weight,
    down_bias,
    mean_adaw,
    mean_adab,
    mean_qkvw,
    mean_qkvb,
    mean_outw,
    mean_outb,
    mean_upw,
    mean_upb,
    mean_downw,
    mean_downb,
    sqmean_adaw,
    sqmean_adab,
    sqmean_qkvw,
    sqmean_qkvb,
    sqmean_outw,
    sqmean_outb,
    sqmean_upw,
    sqmean_upb,
    sqmean_downw,
    sqmean_downb,
):
    slot_total, tok_dev, model_width = latents.shape
    scale = HD ** (-0.5)
    latent_count = condition.shape[0]
    x_index, group = lax.axis_index("seq"), lax.axis_index("dp")
    core = group % 2
    share = 2 * x_index + core
    live = slot_counts[0] > 0
    slot_match = ((slot_latent[0, 0] == jnp.arange(latent_count)) & live).astype(jnp.float32)
    bf16 = jnp.bfloat16

    silu_cond = jax.nn.silu(condition).astype(bf16)
    mod_cols = jnp.dot(
        silu_cond, ada_weight.astype(bf16), preferred_element_type=jnp.float32
    ) + rounded(ada_bias)

    qkv_block, up_block = gather_columns(qkv_weight.astype(bf16), up_weight.astype(bf16))
    hidden_rows = down_weight.shape[0] // 2
    out_rows = out_weight.shape[0] // 2
    down_b, out_b = down_weight.astype(bf16), out_weight.astype(bf16)
    rows_block = rows_to_blocks(
        [
            jnp.concatenate(
                [cut(down_b, i, hidden_rows, 0), cut(out_b, i, out_rows, 0)], axis=0
            )
            for i in range(2)
        ]
    )
    down_block, out_block = rows_block[:hidden_rows], rows_block[hidden_rows:]
    mod_grid, qkv_grid, out_grid, up_grid, down_grid = gather_grid(
        [mod_cols, qkv_block, out_block, up_block, down_block], 1
    )
    mat_qkv = qkv_grid.reshape(model_width, -1)
    mat_out = out_grid.reshape(-1, model_width)
    mat_up = up_grid.reshape(model_width, -1)
    mat_down = down_grid.reshape(-1, model_width)
    width = mat_out.shape[0]
    hidden_width = mat_up.shape[1]
    heads = width // HD

    (mod_four,) = gather_four([mod_grid.reshape(-1, mod_grid.shape[2])], 2)
    mod_all = mod_four.reshape(4, -1, latent_count, mod_cols.shape[1])
    slot_mod = jnp.einsum("jcln,l->cjn", mod_all, slot_match, precision=lax.Precision.HIGHEST)
    slot_mod = slot_mod.reshape(6, 1, model_width)
    shift_att, scale_att, gate_att, shift_mlp, scale_mlp, gate_mlp = (
        slot_mod[i] for i in range(6)
    )

    biases = (qkv_bias, out_bias, down_bias)
    bias_own = jnp.concatenate(biases).astype(bf16)[None]
    bias_other = swap_x(bias_own)
    bias_pair = flip((bias_own, bias_other), x_index == 1)
    starts = [0]
    for item in biases:
        starts.append(starts[-1] + item.shape[0])
    vec_qkv, vec_out, vec_down = (
        jnp.concatenate(
            [half[0, starts[i] : starts[i + 1]] for half in bias_pair]
        ).astype(jnp.float32)
        for i in range(3)
    )
    vec_qkv = cut(vec_qkv.reshape(3, -1), share, width).reshape(-1)
    vec_up = cut(rounded(up_bias), core, hidden_width, 0)

    tokens = latents[0]
    upstream = jnp.where(live, output_gradient[0], 0.0)
    normed_att, spread_att = normalize(tokens)
    attn_own = (normed_att * (1.0 + scale_att) + shift_att).astype(bf16)
    back_down = upstream * gate_mlp
    attn_in, back_down_all = (
        item.reshape(-1, model_width)
        for item in gather_four([attn_own, back_down.astype(bf16)], 3)
    )
    qkv_all = (jnp.dot(attn_in, mat_qkv, preferred_element_type=jnp.float32) + vec_qkv).astype(bf16)
    split = (2, -1, heads, HD)
    queries = qkv_all[:, :width].reshape(split)
    keys_heads = qkv_all[:, width : 2 * width].reshape(split)
    values_heads = qkv_all[:, 2 * width :].reshape(split)
    scores = (
        jnp.einsum("sqhd,skhd->shqk", queries, keys_heads, preferred_element_type=jnp.float32)
        * scale
    )
    row_max = jnp.max(scores, axis=-1, keepdims=True)
    row_total = jnp.sum(jnp.exp(scores - row_max), axis=-1, keepdims=True)
    attn_probs = jnp.exp(scores - row_max) / row_total
    probs_b = attn_probs.astype(bf16)
    attended = jnp.einsum(
        "shqk,skhd->sqhd", probs_b, values_heads, preferred_element_type=jnp.float32
    )
    attended_b = attended.reshape(-1, width).astype(bf16)
    blocks = (4, tok_dev, model_width)
    (branch_sum,) = reduce_four(
        [jnp.dot(attended_b, mat_out, preferred_element_type=jnp.float32).reshape(blocks)], 4
    )
    branch_att = branch_sum + vec_out
    middle = tokens + gate_att * branch_att
    normed_mlp, spread_mlp = normalize(middle)
    mlp_own = (normed_mlp * (1.0 + scale_mlp) + shift_mlp).astype(bf16)
    (mlp_four,) = gather_four([mlp_own], 5)
    mlp_in = mlp_four.reshape(-1, model_width)
    hidden = jnp.dot(mlp_in, mat_up, preferred_element_type=jnp.float32) + vec_up
    activated = gelu_tanh(hidden).astype(bf16)
    branch_terms = jnp.dot(activated, mat_down, preferred_element_type=jnp.float32)
    term_down = weight_term(activated, back_down_all)
    sum_downb = jnp.sum(back_down, axis=0)
    back_hidden = jnp.einsum(
        "rd,fd->rf", back_down_all, mat_down, preferred_element_type=jnp.float32
    ) * gelu_slope(hidden)
    back_hidden_b = back_hidden.astype(bf16)
    term_up = weight_term(mlp_in, back_hidden_b)
    sum_upb = jnp.sum(back_hidden, axis=0)
    back_terms = jnp.einsum(
        "rf,cf->rc", back_hidden_b, mat_up, preferred_element_type=jnp.float32
    )
    branch_mlp, back_mlp_in = reduce_four(
        [branch_terms.reshape(blocks), back_terms.reshape(blocks)], 6
    )
    branch_mlp = branch_mlp + vec_down
    block_output = jnp.where(live, middle + gate_mlp * branch_mlp, 0.0)
    back_middle = upstream + norm_back(back_mlp_in * (1.0 + scale_mlp), normed_mlp, spread_mlp)
    back_att = back_middle * gate_att
    (back_att_four,) = gather_four([back_att.astype(bf16)], 7)
    back_att_all = back_att_four.reshape(-1, model_width)
    term_out = weight_term(attended_b, back_att_all)
    sum_outb = jnp.sum(back_att, axis=0)
    back_attended = jnp.einsum(
        "rd,cd->rc", back_att_all, mat_out, preferred_element_type=jnp.float32
    ).astype(bf16)
    back_attended = back_attended.reshape(split)
    back_probs = jnp.einsum(
        "sqhd,skhd->shqk", back_attended, values_heads, preferred_element_type=jnp.float32
    )
    row_delta = jnp.einsum("sqhd,sqhd->shq", back_attended.astype(jnp.float32), attended)[..., None]
    back_scores = (attn_probs * (back_probs - row_delta) * scale).astype(bf16)
    back_queries = jnp.einsum(
        "shqk,skhd->sqhd", back_scores, keys_heads, preferred_element_type=jnp.float32
    )
    back_keys = jnp.einsum(
        "shqk,sqhd->skhd", back_scores, queries, preferred_element_type=jnp.float32
    )
    back_values = jnp.einsum(
        "shqk,sqhd->skhd", probs_b, back_attended, preferred_element_type=jnp.float32
    )
    back_qkv = jnp.concatenate(
        [item.reshape(-1, width) for item in (back_queries, back_keys, back_values)], axis=1
    )
    back_qkv_b = back_qkv.astype(bf16)
    term_qkv = weight_term(attn_in, back_qkv_b)
    sum_qkvb = jnp.sum(back_qkv, axis=0)
    attn_terms = jnp.einsum(
        "rd,cd->rc", back_qkv_b, mat_qkv, preferred_element_type=jnp.float32
    )
    (back_attn_in,) = reduce_four([attn_terms.reshape(blocks)], 8)
    latent_gradient = jnp.where(
        live,
        back_middle + norm_back(back_attn_in * (1.0 + scale_att), normed_att, spread_att),
        0.0,
    )[None]
    block_output = block_output[None]
    chips = lax.axis_size("dp") // 2
    qkv_sum, out_sum, up_sum, down_sum = reduce_grid(
        [
            term.reshape(chips, -1, term.shape[1])
            for term in (term_qkv, term_out, term_up, term_down)
        ],
        9,
    )
    grad_qkvw, grad_upw = scatter_columns(qkv_sum, up_sum)
    owned = blocks_to_rows(jnp.concatenate([down_sum, out_sum], axis=0))
    grad_downw = jnp.concatenate([item[:hidden_rows] for item in owned], axis=0)
    grad_outw = jnp.concatenate([item[hidden_rows:] for item in owned], axis=0)
    grad_qkvw, grad_outw, grad_upw, grad_downw = (
        item.astype(jnp.float32) for item in (grad_qkvw, grad_outw, grad_upw, grad_downw)
    )

    slot_modgrad = jnp.concatenate(
        [
            jnp.sum(back_attn_in, axis=0),
            jnp.sum(back_attn_in * normed_att, axis=0),
            jnp.sum(back_middle * branch_att, axis=0),
            jnp.sum(back_mlp_in, axis=0),
            jnp.sum(back_mlp_in * normed_mlp, axis=0),
            jnp.sum(upstream * branch_mlp, axis=0),
        ]
    )
    modgrad_table = slot_match[:, None] * slot_modgrad[None, :]
    modgrad_cols = scatter_tree(
        jnp.moveaxis(modgrad_table.reshape(latent_count, -1, ada_bias.shape[0]), 1, 0),
        ("dp", "seq"),
    )
    grad_adaw = jnp.dot(
        rounded(jax.nn.silu(condition)).T, modgrad_cols, precision=lax.Precision.HIGHEST
    )
    grad_adab = jnp.sum(modgrad_cols, axis=0)
    cond_term = jnp.dot(modgrad_cols, rounded(ada_weight).T, precision=lax.Precision.HIGHEST)
    cond_sum = sum_tree(cond_term, ("dp", "seq"))
    qkvb_wide = lax.dynamic_update_slice(
        jnp.zeros((3, 4 * width), jnp.float32), sum_qkvb.reshape(3, width), (0, share * width)
    ).reshape(-1)
    upb_wide = lax.dynamic_update_slice(
        jnp.zeros((4 * hidden_width,), jnp.float32), sum_upb, (share * hidden_width,)
    )
    bias_sums = (qkvb_wide, sum_outb, upb_wide, sum_downb)
    totals, start, bias_totals = sum_tree(jnp.concatenate(bias_sums), ("dp", "seq")), 0, []
    for item in bias_sums:
        bias_totals.append(totals[start : start + item.shape[0]])
        start += item.shape[0]
    total_qkvb, total_outb, total_upb, total_downb = bias_totals
    condition_grad = cond_sum * silu_slope(condition)
    seq_index = lax.axis_index("seq")

    def own_part(full_sum, local_bias):
        length = local_bias.shape[0]
        return lax.dynamic_slice_in_dim(full_sum, seq_index * length, length)

    grad_qkvb = own_part(total_qkvb, qkv_bias)
    grad_outb = own_part(total_outb, out_bias)
    grad_upb = own_part(total_upb, up_bias)
    grad_downb = own_part(total_downb, down_bias)
    grads_all = (
        grad_adaw,
        grad_adab,
        grad_qkvw,
        grad_qkvb,
        grad_outw,
        grad_outb,
        grad_upw,
        grad_upb,
        grad_downw,
        grad_downb,
    )
    params_all = (
        ada_weight,
        ada_bias,
        qkv_weight,
        qkv_bias,
        out_weight,
        out_bias,
        up_weight,
        up_bias,
        down_weight,
        down_bias,
    )
    means_all = (
        mean_adaw,
        mean_adab,
        mean_qkvw,
        mean_qkvb,
        mean_outw,
        mean_outb,
        mean_upw,
        mean_upb,
        mean_downw,
        mean_downb,
    )
    squares_all = (
        sqmean_adaw,
        sqmean_adab,
        sqmean_qkvw,
        sqmean_qkvb,
        sqmean_outw,
        sqmean_outb,
        sqmean_upw,
        sqmean_upb,
        sqmean_downw,
        sqmean_downb,
    )
    updates = [
        adamw_step(p_item, g_item, m_item, v_item)
        for p_item, g_item, m_item, v_item in zip(params_all, grads_all, means_all, squares_all)
    ]
    newvals = tuple((entry[0] for entry in updates))
    newmeans = tuple((entry[1] for entry in updates))
    newsqrs = tuple((entry[2] for entry in updates))
    return (
        (block_output, latent_gradient, condition_grad) + grads_all + newvals + newmeans + newsqrs
    )


def fits(mesh, slots, width, hidden):
    groups, ways = mesh.shape["dp"], mesh.shape["seq"]
    return (
        slots == groups
        and ways == 2
        and groups % 4 == 0
        and H % 4 == 0
        and width == H * HD
        and width % (2 * groups * 4) == 0
        and hidden % (2 * groups * 16) == 0
    )


def build(mesh, on_device):
    return jax.shard_map(
        on_device,
        mesh=mesh,
        in_specs=(
            P("dp", "seq", None),
            P(),
            P("dp", None),
            P("dp"),
            P("dp", "seq", None),
            P(None, ("dp", "seq")),
            P(("dp", "seq")),
            P("dp", "seq"),
            P("seq"),
            P("dp", "seq"),
            P("seq"),
            P("dp", "seq"),
            P("seq"),
            P("dp", "seq"),
            P("seq"),
            P(None, ("dp", "seq")),
            P(("dp", "seq")),
            P("dp", "seq"),
            P("seq"),
            P("dp", "seq"),
            P("seq"),
            P("dp", "seq"),
            P("seq"),
            P("dp", "seq"),
            P("seq"),
            P(None, ("dp", "seq")),
            P(("dp", "seq")),
            P("dp", "seq"),
            P("seq"),
            P("dp", "seq"),
            P("seq"),
            P("dp", "seq"),
            P("seq"),
            P("dp", "seq"),
            P("seq"),
        ),
        out_specs=(
            P("dp", "seq", None),
            P("dp", "seq", None),
            P(),
            P(None, ("dp", "seq")),
            P(("dp", "seq")),
            P("dp", "seq"),
            P("seq"),
            P("dp", "seq"),
            P("seq"),
            P("dp", "seq"),
            P("seq"),
            P("dp", "seq"),
            P("seq"),
            P(None, ("dp", "seq")),
            P(("dp", "seq")),
            P("dp", "seq"),
            P("seq"),
            P("dp", "seq"),
            P("seq"),
            P("dp", "seq"),
            P("seq"),
            P("dp", "seq"),
            P("seq"),
            P(None, ("dp", "seq")),
            P(("dp", "seq")),
            P("dp", "seq"),
            P("seq"),
            P("dp", "seq"),
            P("seq"),
            P("dp", "seq"),
            P("seq"),
            P("dp", "seq"),
            P("seq"),
            P(None, ("dp", "seq")),
            P(("dp", "seq")),
            P("dp", "seq"),
            P("seq"),
            P("dp", "seq"),
            P("seq"),
            P("dp", "seq"),
            P("seq"),
            P("dp", "seq"),
            P("seq"),
        ),
        check_vma=False,
    )


def solution(mesh):
    def program(latents, *rest):
        hidden, width = rest[12].shape
        chosen = fits(mesh, latents.shape[0], width, hidden)
        return build(mesh, on_device_grid if chosen else on_device_general)(latents, *rest)

    return program
```

```python
import functools

import jax
import jax.numpy as jnp
from jax import lax
from jax.experimental import pallas as pl
from jax.experimental.pallas import tpu as pltpu
from jax.sharding import PartitionSpec as P

H = 16
HD = 72
STEP = 2


EPS_NORM = 1e-06
GELU_COEF = 0.7978845608
GELU_CUBE = 0.044715
BETA_ONE = 0.9
BETA_TWO = 0.999
LEARN_RATE = 0.05
EPS_ADAM = 1e-08


def rounded(values):
    return lax.optimization_barrier(values.astype(jnp.bfloat16)).astype(jnp.float32)


def normalize(values):
    center = values - jnp.mean(values, axis=-1, keepdims=True)
    spread = lax.rsqrt(jnp.mean(center * center, axis=-1, keepdims=True) + EPS_NORM)
    return (center * spread, spread)


def norm_back(upstream, normed, spread):
    return spread * (
        upstream
        - jnp.mean(upstream, axis=-1, keepdims=True)
        - normed * jnp.mean(upstream * normed, axis=-1, keepdims=True)
    )


def gelu_tanh(values):
    tanh_part = jnp.tanh(GELU_COEF * (values + GELU_CUBE * values * values * values))
    return 0.5 * values * (1.0 + tanh_part)


def gelu_slope(values):
    tanh_part = jnp.tanh(GELU_COEF * (values + GELU_CUBE * values * values * values))
    return 0.5 * (1.0 + tanh_part) + 0.5 * values * (1.0 - tanh_part * tanh_part) * GELU_COEF * (
        1.0 + 3.0 * GELU_CUBE * values * values
    )


def silu_slope(values):
    sigmoid_part = jax.nn.sigmoid(values)
    return sigmoid_part * (1.0 + values * (1.0 - sigmoid_part))


def adamw_step(parameter, gradient, first_mom, second):
    first_new = BETA_ONE * first_mom + (1.0 - BETA_ONE) * gradient
    second_new = BETA_TWO * second + (1.0 - BETA_TWO) * gradient * gradient
    first_hat = first_new / (1.0 - BETA_ONE**STEP)
    second_hat = second_new / (1.0 - BETA_TWO**STEP)
    return (
        parameter - LEARN_RATE * first_hat / (jnp.sqrt(second_hat) + EPS_ADAM),
        first_new,
        second_new,
    )


def flat_index(axes):
    index = lax.axis_index(axes[0])
    for axis in axes[1:]:
        index = index * lax.axis_size(axis) + lax.axis_index(axis)
    return index


def swap_bit(values, axes, step):
    total = 1
    for axis in axes:
        total *= lax.axis_size(axis)
    return lax.ppermute(values, axes, [(i, i ^ step) for i in range(total)])


def axes_size(axes):
    total = 1
    for axis in axes:
        total *= lax.axis_size(axis)
    return total


def gather_tree(values, axes):
    index, blocks, step = flat_index(axes), values[None], 1
    while step < axes_size(axes):
        other = swap_bit(blocks, axes, step)
        upper = (index // step) % 2 == 1
        blocks = jnp.concatenate(
            [jnp.where(upper, other, blocks), jnp.where(upper, blocks, other)], axis=0
        )
        step *= 2
    return blocks


def scatter_tree(blocks, axes, sent=None):
    index, step = flat_index(axes), axes_size(axes) // 2
    while step >= 1:
        low, high = blocks[:step], blocks[step:]
        upper = (index // step) % 2 == 1
        away = jnp.where(upper, low, high)
        if sent is not None:
            away = away.astype(sent)
        kept = jnp.where(upper, high, low)
        blocks = kept + swap_bit(away, axes, step).astype(kept.dtype)
        step //= 2
    return blocks[0]


def sum_tree(values, axes):
    step = 1
    while step < axes_size(axes):
        values = values + swap_bit(values, axes, step)
        step *= 2
    return values


def join_columns(halves, widths):
    parts, start = [], 0
    for width in widths:
        part = halves[:, :, start : start + width]
        parts.append(jnp.moveaxis(part, 0, 1).reshape(part.shape[1], -1))
        start += width
    return parts


def split_columns(parts):
    ways = lax.axis_size("seq")
    blocks = [
        jnp.moveaxis(part.reshape(part.shape[0], ways, -1), 1, 0) for part in parts
    ]
    return jnp.concatenate(blocks, axis=2)


def piece_moves(turn):
    rows, ways = lax.axis_size("dp"), lax.axis_size("seq")
    pairs = []
    for g in range(rows):
        for x in range(ways):
            piece = g * ways + (turn + x) % ways
            pairs.append((g * ways + x, (piece % rows) * ways + piece // rows))
    return pairs


def own_piece():
    return lax.axis_index("seq") * lax.axis_size("dp") + lax.axis_index("dp")


def pick(blocks, index):
    return lax.dynamic_index_in_dim(blocks, index, 0, keepdims=False)


def rows_from_owners(block):
    ways, x = lax.axis_size("seq"), lax.axis_index("seq")
    pieces = block.reshape(ways, -1, block.shape[1])
    got = jnp.stack(
        [
            lax.ppermute(pick(pieces, (turn + x) % ways), ("dp", "seq"), piece_moves(turn))
            for turn in range(ways)
        ]
    )
    place = own_piece() % ways
    return jnp.concatenate([pick(got, (place - i + ways) % ways) for i in range(ways)], axis=1)


def rows_to_owners(piece):
    ways, x = lax.axis_size("seq"), lax.axis_index("seq")
    columns = jnp.moveaxis(piece.reshape(piece.shape[0], ways, -1), 1, 0)
    place = own_piece() % ways
    got = jnp.stack(
        [
            lax.ppermute(
                pick(columns, (place - turn + ways) % ways),
                ("dp", "seq"),
                [(taker, owner) for owner, taker in piece_moves(turn)],
            )
            for turn in range(ways)
        ]
    )
    ordered = jnp.stack([pick(got, (q - x + ways) % ways) for q in range(ways)])
    return ordered.reshape(-1, ordered.shape[2])


def all_tokens(values):
    return gather_tree(values, ("seq",)).reshape(-1, values.shape[1])


def own_tokens(terms):
    blocks = terms.reshape(lax.axis_size("seq"), -1, terms.shape[1])
    return scatter_tree(blocks, ("seq",), jnp.bfloat16)


def weight_term(left, right):
    return jnp.einsum("rc,rd->cd", left, right, preferred_element_type=jnp.float32).astype(
        jnp.bfloat16
    )


def spread_terms(terms):
    widths = [term.shape[1] // lax.axis_size("seq") for term in terms]
    joined = jnp.concatenate(terms, axis=1) if len(terms) > 1 else terms[0]
    rows = lax.psum_scatter(joined, "dp", scatter_dimension=0, tiled=True)
    pieces, start = [], 0
    for term in terms:
        pieces.append(rows[:, start : start + term.shape[1]])
        start += term.shape[1]
    own = scatter_tree(split_columns(pieces).astype(jnp.float32), ("seq",), jnp.bfloat16)
    blocks, start = [], 0
    for width in widths:
        blocks.append(own[:, start : start + width])
        start += width
    return blocks


def on_device_general(
    latents,
    condition,
    slot_latent,
    slot_counts,
    output_gradient,
    ada_weight,
    ada_bias,
    qkv_weight,
    qkv_bias,
    out_weight,
    out_bias,
    up_weight,
    up_bias,
    down_weight,
    down_bias,
    mean_adaw,
    mean_adab,
    mean_qkvw,
    mean_qkvb,
    mean_outw,
    mean_outb,
    mean_upw,
    mean_upb,
    mean_downw,
    mean_downb,
    sqmean_adaw,
    sqmean_adab,
    sqmean_qkvw,
    sqmean_qkvb,
    sqmean_outw,
    sqmean_outb,
    sqmean_upw,
    sqmean_upb,
    sqmean_downw,
    sqmean_downb,
):
    slot_total, tok_dev, model_width = latents.shape
    row_count = slot_total * tok_dev
    scale = HD ** (-0.5)
    live_slots = jnp.arange(slot_total) < slot_counts[0]
    live_mask = live_slots[:, None, None]
    latent_count = condition.shape[0]
    slot_matches = (
        (slot_latent[0][:, None] == jnp.arange(latent_count)[None, :]) & live_slots[:, None]
    ).astype(jnp.float32)
    silu_cond = jax.nn.silu(condition).astype(jnp.bfloat16)
    mod_cols = jnp.dot(
        silu_cond, ada_weight.astype(jnp.bfloat16), preferred_element_type=jnp.float32
    ) + rounded(ada_bias)
    modulation = jnp.moveaxis(gather_tree(mod_cols, ("dp", "seq")), 0, 1).reshape(
        latent_count, -1
    )
    slot_mod = jnp.dot(slot_matches, modulation, precision=lax.Precision.HIGHEST)[:, None, :]
    shift_att, scale_att, gate_att, shift_mlp, scale_mlp, gate_mlp = jnp.split(slot_mod, 6, axis=2)
    upstream = jnp.where(live_mask, output_gradient, 0.0)
    biases = (qkv_bias, out_bias, down_bias)
    bias_rows = gather_tree(
        jnp.concatenate(biases).astype(jnp.bfloat16)[None], ("seq",)
    )
    vec_qkv, vec_out, vec_down = (
        part[0].astype(jnp.float32)
        for part in join_columns(bias_rows, [item.shape[0] for item in biases])
    )
    wide = (qkv_weight, out_weight)
    wide_halves = gather_tree(jnp.concatenate(wide, axis=1).astype(jnp.bfloat16), ("seq",))
    wide_rows = jnp.concatenate(
        join_columns(wide_halves, [item.shape[1] for item in wide])
        + [up_weight.astype(jnp.bfloat16)],
        axis=1,
    )
    wide_full = lax.all_gather(wide_rows, "dp", axis=0, tiled=True)
    qkv_end = 3 * model_width
    mat_qkv = wide_full[:, :qkv_end]
    mat_out = wide_full[:, qkv_end : qkv_end + model_width]
    mat_up = wide_full[:, qkv_end + model_width :]
    down_rows = rows_from_owners(down_weight.astype(jnp.bfloat16))
    mat_down = lax.all_gather(down_rows, "dp", axis=0, tiled=True)
    normed_att, spread_att = normalize(latents)
    attn_in = (
        (normed_att * (1.0 + scale_att) + shift_att)
        .astype(jnp.bfloat16)
        .reshape(row_count, model_width)
    )
    qkv_all = (jnp.dot(attn_in, mat_qkv, preferred_element_type=jnp.float32) + vec_qkv).astype(
        jnp.bfloat16
    )
    queries = qkv_all[:, :model_width].reshape(slot_total, tok_dev, H, HD)
    keys_own = qkv_all[:, model_width : 2 * model_width].reshape(slot_total, tok_dev, model_width)
    values_own = qkv_all[:, 2 * model_width :].reshape(slot_total, tok_dev, model_width)
    pairs_own = jnp.concatenate([keys_own, values_own], axis=2)
    pairs_all = jnp.moveaxis(gather_tree(pairs_own, ("seq",)), 0, 1)
    pairs_all = pairs_all.reshape(slot_total, -1, 2 * model_width)
    keys_all, values_all = pairs_all[:, :, :model_width], pairs_all[:, :, model_width:]
    keys_heads = keys_all.reshape(slot_total, -1, H, HD)
    values_heads = values_all.reshape(slot_total, -1, H, HD)
    scores = (
        jnp.einsum("sqhd,skhd->shqk", queries, keys_heads, preferred_element_type=jnp.float32)
        * scale
    )
    row_max = jnp.max(scores, axis=-1, keepdims=True)
    row_total = jnp.sum(jnp.exp(scores - row_max), axis=-1, keepdims=True)
    attn_probs = jnp.exp(scores - row_max) / row_total
    probs_b = attn_probs.astype(jnp.bfloat16)
    attended = jnp.einsum(
        "shqk,skhd->sqhd", probs_b, values_heads, preferred_element_type=jnp.float32
    )
    attended_b = attended.reshape(row_count, model_width).astype(jnp.bfloat16)
    branch_att = (
        jnp.dot(attended_b, mat_out, preferred_element_type=jnp.float32) + vec_out
    ).reshape(slot_total, tok_dev, model_width)
    middle = latents + gate_att * branch_att
    normed_mlp, spread_mlp = normalize(middle)
    mlp_in = (
        (normed_mlp * (1.0 + scale_mlp) + shift_mlp)
        .astype(jnp.bfloat16)
        .reshape(row_count, model_width)
    )
    mlp_all = all_tokens(mlp_in)
    hidden = jnp.dot(mlp_all, mat_up, preferred_element_type=jnp.float32) + rounded(up_bias)
    activated = gelu_tanh(hidden).astype(jnp.bfloat16)
    activated, mat_down = lax.optimization_barrier((activated, mat_down))
    branch_mlp = (
        own_tokens(jnp.dot(activated, mat_down, preferred_element_type=jnp.float32)) + vec_down
    ).reshape(slot_total, tok_dev, model_width)
    block_output = jnp.where(live_mask, middle + gate_mlp * branch_mlp, 0.0)
    back_down = upstream * gate_mlp
    back_down_b = back_down.astype(jnp.bfloat16).reshape(row_count, model_width)
    back_down_all = all_tokens(back_down_b)
    down_sums = lax.psum_scatter(
        weight_term(activated, back_down_all), "dp", scatter_dimension=0, tiled=True
    )
    grad_downw = rows_to_owners(down_sums).astype(jnp.float32)
    sum_downb = jnp.sum(back_down, axis=(0, 1))
    back_hidden = jnp.einsum(
        "rd,fd->rf", back_down_all, mat_down, preferred_element_type=jnp.float32
    ) * gelu_slope(hidden)
    back_hidden_b = back_hidden.astype(jnp.bfloat16)
    grad_upw = lax.psum_scatter(
        weight_term(mlp_all, back_hidden_b), "dp", scatter_dimension=0, tiled=True
    ).astype(jnp.float32)
    up_total = jnp.zeros((lax.axis_size("seq") * up_bias.shape[0],), jnp.float32)
    sum_upb = lax.dynamic_update_slice_in_dim(
        up_total, jnp.sum(back_hidden, axis=0), lax.axis_index("seq") * up_bias.shape[0], 0
    )
    back_mlp_in = own_tokens(
        jnp.einsum("rf,cf->rc", back_hidden_b, mat_up, preferred_element_type=jnp.float32)
    ).reshape(slot_total, tok_dev, model_width)
    back_middle = upstream + norm_back(back_mlp_in * (1.0 + scale_mlp), normed_mlp, spread_mlp)
    back_att = back_middle * gate_att
    back_att_b = back_att.astype(jnp.bfloat16).reshape(row_count, model_width)
    term_out = weight_term(attended_b, back_att_b)
    sum_outb = jnp.sum(back_att, axis=(0, 1))
    back_attended = jnp.einsum(
        "rd,cd->rc", back_att_b, mat_out, preferred_element_type=jnp.float32
    ).astype(jnp.bfloat16)
    back_attended = back_attended.reshape(slot_total, tok_dev, H, HD)
    back_probs = jnp.einsum(
        "sqhd,skhd->shqk", back_attended, values_heads, preferred_element_type=jnp.float32
    )
    row_delta = jnp.einsum("sqhd,sqhd->shq", back_attended.astype(jnp.float32), attended)[..., None]
    back_scores = (attn_probs * (back_probs - row_delta) * scale).astype(jnp.bfloat16)
    back_queries = jnp.einsum(
        "shqk,skhd->sqhd", back_scores, keys_heads, preferred_element_type=jnp.float32
    )
    key_terms = jnp.einsum(
        "shqk,sqhd->skhd", back_scores, queries, preferred_element_type=jnp.float32
    ).reshape(slot_total, -1, model_width)
    value_terms = jnp.einsum(
        "shqk,sqhd->skhd", probs_b, back_attended, preferred_element_type=jnp.float32
    ).reshape(slot_total, -1, model_width)
    pair_terms = jnp.concatenate([key_terms, value_terms], axis=2)
    pair_terms = pair_terms.reshape(slot_total, -1, tok_dev, 2 * model_width)
    back_pairs = scatter_tree(jnp.moveaxis(pair_terms, 1, 0), ("seq",), jnp.bfloat16)
    back_keys, back_values = back_pairs[:, :, :model_width], back_pairs[:, :, model_width:]
    back_qkv = jnp.concatenate(
        [
            back_queries.reshape(row_count, model_width),
            back_keys.reshape(row_count, model_width),
            back_values.reshape(row_count, model_width),
        ],
        axis=1,
    )
    back_qkv_b = back_qkv.astype(jnp.bfloat16)
    term_qkv = weight_term(attn_in, back_qkv_b)
    grad_qkvw, grad_outw = spread_terms([term_qkv, term_out])
    sum_qkvb = jnp.sum(back_qkv, axis=0)
    back_attn_in = jnp.einsum(
        "rd,cd->rc", back_qkv_b, mat_qkv, preferred_element_type=jnp.float32
    ).reshape(slot_total, tok_dev, model_width)
    latent_gradient = jnp.where(
        live_mask,
        back_middle + norm_back(back_attn_in * (1.0 + scale_att), normed_att, spread_att),
        0.0,
    )
    slot_modgrad = jnp.concatenate(
        [
            jnp.sum(back_attn_in, axis=1),
            jnp.sum(back_attn_in * normed_att, axis=1),
            jnp.sum(back_middle * branch_att, axis=1),
            jnp.sum(back_mlp_in, axis=1),
            jnp.sum(back_mlp_in * normed_mlp, axis=1),
            jnp.sum(upstream * branch_mlp, axis=1),
        ],
        axis=1,
    )
    modgrad_table = jnp.dot(slot_matches.T, slot_modgrad, precision=lax.Precision.HIGHEST)
    modgrad_cols = scatter_tree(
        jnp.moveaxis(modgrad_table.reshape(latent_count, -1, ada_bias.shape[0]), 1, 0),
        ("dp", "seq"),
    )
    grad_adaw = jnp.dot(
        rounded(jax.nn.silu(condition)).T, modgrad_cols, precision=lax.Precision.HIGHEST
    )
    grad_adab = jnp.sum(modgrad_cols, axis=0)
    cond_term = jnp.dot(modgrad_cols, rounded(ada_weight).T, precision=lax.Precision.HIGHEST)
    cond_sum = sum_tree(cond_term, ("dp", "seq"))
    bias_sums = (sum_qkvb, sum_outb, sum_upb, sum_downb)
    totals, start, bias_totals = sum_tree(jnp.concatenate(bias_sums), ("dp", "seq")), 0, []
    for item in bias_sums:
        bias_totals.append(totals[start : start + item.shape[0]])
        start += item.shape[0]
    total_qkvb, total_outb, total_upb, total_downb = bias_totals
    condition_grad = cond_sum * silu_slope(condition)
    seq_index = lax.axis_index("seq")

    def own_part(full_sum, local_bias):
        length = local_bias.shape[0]
        return lax.dynamic_slice_in_dim(full_sum, seq_index * length, length)

    grad_qkvb = own_part(total_qkvb, qkv_bias)
    grad_outb = own_part(total_outb, out_bias)
    grad_upb = own_part(total_upb, up_bias)
    grad_downb = own_part(total_downb, down_bias)
    grads_all = (
        grad_adaw,
        grad_adab,
        grad_qkvw,
        grad_qkvb,
        grad_outw,
        grad_outb,
        grad_upw,
        grad_upb,
        grad_downw,
        grad_downb,
    )
    params_all = (
        ada_weight,
        ada_bias,
        qkv_weight,
        qkv_bias,
        out_weight,
        out_bias,
        up_weight,
        up_bias,
        down_weight,
        down_bias,
    )
    means_all = (
        mean_adaw,
        mean_adab,
        mean_qkvw,
        mean_qkvb,
        mean_outw,
        mean_outb,
        mean_upw,
        mean_upb,
        mean_downw,
        mean_downb,
    )
    squares_all = (
        sqmean_adaw,
        sqmean_adab,
        sqmean_qkvw,
        sqmean_qkvb,
        sqmean_outw,
        sqmean_outb,
        sqmean_upw,
        sqmean_upb,
        sqmean_downw,
        sqmean_downb,
    )
    updates = [
        adamw_step(p_item, g_item, m_item, v_item)
        for p_item, g_item, m_item, v_item in zip(params_all, grads_all, means_all, squares_all)
    ]
    newvals = tuple((entry[0] for entry in updates))
    newmeans = tuple((entry[1] for entry in updates))
    newsqrs = tuple((entry[2] for entry in updates))
    return (
        (block_output, latent_gradient, condition_grad) + grads_all + newvals + newmeans + newsqrs
    )


MESH_ID = pl.DeviceIdType.MESH
ANY = pl.BlockSpec(memory_space=pl.ANY)
VMEM = pl.BlockSpec(memory_space=pltpu.VMEM)


def params_of(number):
    return pltpu.CompilerParams(
        collective_id=number, has_side_effects=True, vmem_limit_bytes=56 * 2**20
    )


def place():
    group, x = lax.axis_index("dp"), lax.axis_index("seq")
    core, chip = group % 2, group // 2
    return chip // 2, chip % 2, core, x


def device(a, b, core, x):
    return ((a * 2 + b) * 2 + core, x)


def remote(src, dst, send, recv, target):
    return pltpu.make_async_remote_copy(
        src_ref=src,
        dst_ref=dst,
        send_sem=send,
        recv_sem=recv,
        device_id=target,
        device_id_type=MESH_ID,
    )


def greet(targets, present):
    barrier = pltpu.get_barrier_semaphore()
    amount = 0
    for target, there in zip(targets, present):

        def signal():
            pl.semaphore_signal(barrier, inc=1, device_id=target, device_id_type=MESH_ID)

        if there is True:
            signal()
            amount = amount + 1
        else:
            pl.when(there)(signal)
            amount = amount + there.astype(jnp.int32)
    pl.semaphore_wait(barrier, amount)


def greet_near(lines, grid, four):
    a, b, core, x = place()
    targets, present = [], []
    if grid:
        targets += [device(a, 1 - b, core, x), device(a - 1, b, core, x), device(a + 1, b, core, x)]
        present += [True, a > 0, a < lines - 1]
    if four:
        targets += [device(a, b, 1 - core, x), device(a, b, core, 1 - x)]
        present += [True, True]
    greet(targets, present)


class Part:
    def __init__(self, make, ins, in_specs, outs, out_specs, scratch):
        self.make, self.ins, self.in_specs = make, ins, in_specs
        self.outs, self.out_specs, self.scratch = outs, out_specs, scratch


def joint_kernel(parts, plan, lines, grid, four, *refs):
    ins = [len(part.ins) for part in parts]
    outs = [len(part.outs) for part in parts]
    at_in, at_out = 0, sum(ins)
    at_scratch = at_out + sum(outs)
    if four is None:
        greet_all()
    else:
        greet_near(lines, grid, four)
    stages = []
    for part, n_in, n_out in zip(parts, ins, outs):
        n_scratch = len(part.scratch)
        stages.append(
            part.make(
                refs[at_in : at_in + n_in],
                refs[at_out : at_out + n_out],
                refs[at_scratch : at_scratch + n_scratch],
            )
        )
        at_in, at_out, at_scratch = at_in + n_in, at_out + n_out, at_scratch + n_scratch
    for index, stage in plan:
        stages[index][stage]()


def run_parts(parts, plan, number, grid, four):
    lines = lax.axis_size("dp") // 4
    flat = pl.pallas_call(
        functools.partial(joint_kernel, parts, plan, lines, grid, four),
        out_shape=sum((part.outs for part in parts), []),
        in_specs=sum((part.in_specs for part in parts), []),
        out_specs=sum((part.out_specs for part in parts), []),
        scratch_shapes=sum((part.scratch for part in parts), []),
        compiler_params=params_of(number),
        name="joint",
    )(*sum((part.ins for part in parts), []))
    results, start = [], 0
    for part in parts:
        results.append(flat[start : start + len(part.outs)])
        start += len(part.outs)
    return results


def strips(rows):
    return [(i, 48) for i in range(0, rows, 48)] if rows % 48 == 0 else [(0, rows)]


def view(ref, rows, part, lead):
    if part == (0, rows):
        return ref
    cut_rows = pl.ds(*part)
    return ref.at[:, cut_rows, :] if lead else ref.at[cut_rows, :]


def views(refs, rows, lead):
    return [
        view(ref, size, part, lead) for ref, size in zip(refs, rows) for part in strips(size)
    ]


def grid_gather(pieces):
    lines = lax.axis_size("dp") // 4
    rows = [piece.shape[0] for piece in pieces]
    count, whole = sum(len(strips(size)) for size in rows), len(pieces)

    def make(ins, outs, scratch):
        ins, outs = views(ins, rows, False), views(outs, rows, True)
        keep, up_send, down_send, side_send, line_recv, side_recv = scratch
        a, b, core, x = place()
        own = a * 2 + b
        copies = [
            pltpu.make_async_copy(ins[p], outs[p].at[own], keep.at[p]) for p in range(count)
        ]

        def up(p, s, src):
            return remote(
                src, outs[p].at[s * 2 + b], up_send.at[p, s], line_recv.at[p, s],
                device(a + 1, b, core, x),
            )

        def down(p, s, src):
            return remote(
                src, outs[p].at[s * 2 + b], down_send.at[p, s], line_recv.at[p, s],
                device(a - 1, b, core, x),
            )

        def side(p, s, src):
            return remote(
                src, outs[p].at[s * 2 + b], side_send.at[p, s], side_recv.at[p, s],
                device(a, 1 - b, core, x),
            )

        def arrived(p, s):
            block = outs[p].at[s * 2 + b]
            remote(
                block, block, up_send.at[p, s], line_recv.at[p, s], device(a, 1 - b, core, x)
            ).wait_recv()
            return block

        def start():
            for p in range(count):
                pl.when(a < lines - 1)(lambda: up(p, a, ins[p]).start())
                pl.when(a > 0)(lambda: down(p, a, ins[p]).start())
                side(p, a, ins[p]).start()
                copies[p].start()

        def hop_of(hop):
            def run():
                for p in range(count):

                    def from_below():
                        block = arrived(p, a - hop)
                        pl.when(a < lines - 1)(lambda: up(p, a - hop, block).start())
                        side(p, a - hop, block).start()

                    def from_above():
                        block = arrived(p, a + hop)
                        pl.when(a > 0)(lambda: down(p, a + hop, block).start())
                        side(p, a + hop, block).start()

                    pl.when(a - hop >= 0)(from_below)
                    pl.when(a + hop < lines)(from_above)

            return run

        def got(p):
            copies[p].wait()
            for s in range(lines):
                block = outs[p].at[s * 2 + 1 - b]
                remote(
                    block, block, side_send.at[p, s], side_recv.at[p, s],
                    device(a, 1 - b, core, x),
                ).wait_recv()

        def sent(p):
            for s in range(lines):
                block = outs[p].at[s * 2 + b]
                side(p, s, block).wait_send()
                pl.when((s <= a) & (a < lines - 1))(lambda: up(p, s, block).wait_send())
                pl.when((s >= a) & (a > 0))(lambda: down(p, s, block).wait_send())

        def hops():
            for hop in range(1, lines):
                hop_of(hop)()

        def end():
            for p in range(count):
                got(p)
                sent(p)

        def early():
            got(0)

        def late():
            for p in range(1, count):
                got(p)
            for p in range(count):
                sent(p)

        return dict(start=start, hops=hops, end=end, early=early, late=late, hop=hop_of(1),
                    more=lambda: [hop_of(hop)() for hop in range(2, lines)])

    dma = pltpu.SemaphoreType.DMA
    return Part(
        make,
        list(pieces),
        [ANY] * whole,
        [jax.ShapeDtypeStruct((2 * lines,) + piece.shape, piece.dtype) for piece in pieces],
        [ANY] * whole,
        [dma((count,))] + [dma((count, lines))] * 5,
    )


AHEAD = 3


def grid_reduce(pieces):
    lines = lax.axis_size("dp") // 4
    rows = [piece.shape[1] for piece in pieces]
    count, whole = sum(len(strips(size)) for size in rows), len(pieces)

    def make(ins, outs, scratch):
        held, lower, upper = (
            views(scratch[i * whole : (i + 1) * whole], rows, True) for i in range(3)
        )
        up_send, down_send, side_send, up_recv, down_recv, side_recv = scratch[3 * whole :]
        ins, outs = views(ins, rows, True), views(outs, rows, False)
        a, b, core, x = place()

        def side(p, t):
            return remote(
                ins[p].at[t * 2 + 1 - b], held[p].at[t], side_send.at[p, t], side_recv.at[p, t],
                device(a, 1 - b, core, x),
            )

        def up(p, t):
            return remote(
                held[p].at[t], lower[p].at[t], up_send.at[p, t], up_recv.at[p, t],
                device(a + 1, b, core, x),
            )

        def down(p, t):
            return remote(
                held[p].at[t], upper[p].at[t], down_send.at[p, t], down_recv.at[p, t],
                device(a - 1, b, core, x),
            )

        def sum_into(p, t, target, others):
            total = ins[p][t * 2 + b].astype(jnp.float32)
            for other in others:
                total = total + other[...].astype(jnp.float32)
            target[...] = total.astype(target.dtype)

        half = lines // 2
        order = list(range(lines - 1, half - 1, -1)) + list(range(half))

        def turn(k):
            p, t = k // lines, order[k % lines]
            return p, jnp.where(a < half, t, lines - 1 - t)

        def start():
            for k in range(AHEAD):
                side(*turn(k)).start()

        def step(k):
            p, t = turn(k)
            side(p, t).wait_recv()
            mine = held[p].at[t]

            def upward():
                def joined():
                    up(p, t).wait_recv()
                    sum_into(p, t, mine, [mine, lower[p].at[t]])

                pl.when(a > 0)(joined)
                pl.when(a == 0)(lambda: sum_into(p, t, mine, [mine]))
                up(p, t).start()

            def downward():
                def joined():
                    down(p, t).wait_recv()
                    sum_into(p, t, mine, [mine, upper[p].at[t]])

                pl.when(a < lines - 1)(joined)
                pl.when(a == lines - 1)(lambda: sum_into(p, t, mine, [mine]))
                down(p, t).start()

            pl.when(a < t)(upward)
            pl.when(a > t)(downward)
            if k + AHEAD < count * lines:
                side(*turn(k + AHEAD)).start()

        def steps():
            for k in range(count * lines):
                step(k)

        def first():
            step(0)

        def others():
            for k in range(1, count * lines):
                step(k)

        def end():
            for p in range(count):
                terms = held[p].at[a], lower[p].at[a], upper[p].at[a]
                pl.when(a > 0)(lambda: up(p, a).wait_recv())
                pl.when(a < lines - 1)(lambda: down(p, a).wait_recv())
                pl.when(a == 0)(lambda: sum_into(p, a, outs[p], [terms[0], terms[2]]))
                pl.when(a == lines - 1)(lambda: sum_into(p, a, outs[p], [terms[0], terms[1]]))
                pl.when((a > 0) & (a < lines - 1))(lambda: sum_into(p, a, outs[p], terms))
            for p in range(count):
                for t in range(lines):
                    side(p, t).wait_send()
                    pl.when(a < t)(lambda: up(p, t).wait_send())
                    pl.when(a > t)(lambda: down(p, t).wait_send())

        return dict(start=start, steps=steps, first=first, others=others, end=end)

    dma = pltpu.SemaphoreType.DMA
    slots = [pltpu.VMEM((lines,) + piece.shape[1:], piece.dtype) for piece in pieces]
    return Part(
        make,
        list(pieces),
        [VMEM] * whole,
        [jax.ShapeDtypeStruct(piece.shape[1:], piece.dtype) for piece in pieces],
        [VMEM] * whole,
        slots * 3 + [dma((count, lines))] * 6,
    )


def four_stages(ins, outs, scratch):
    count = len(outs)
    keep, sib_send, x_send, fwd_send, sib_recv, x_recv, fwd_recv = scratch
    a, b, core, x = place()
    own, across = core * 2 + x, core * 2 + 1 - x
    sibling, peer = device(a, b, 1 - core, x), device(a, b, core, 1 - x)
    to_x, to_sib, to_fwd, copies = [], [], [], []
    for p in range(count):
        block, far = outs[p].at[own], outs[p].at[across]
        to_x.append(remote(ins[p], block, x_send.at[p], x_recv.at[p], peer))
        to_sib.append(remote(ins[p], block, sib_send.at[p], sib_recv.at[p], sibling))
        to_fwd.append(remote(far, far, fwd_send.at[p], fwd_recv.at[p], sibling))
        copies.append(pltpu.make_async_copy(ins[p], block, keep.at[p]))

    def start():
        for p in range(count):
            to_x[p].start()
            to_sib[p].start()
            copies[p].start()

    def middle():
        for p in range(count):
            to_x[p].wait_recv()
            to_fwd[p].start()

    def end():
        for p in range(count):
            to_sib[p].wait_recv()
            to_fwd[p].wait_recv()
            copies[p].wait()
            to_x[p].wait_send()
            to_sib[p].wait_send()
            to_fwd[p].wait_send()

    return dict(start=start, middle=middle, end=end)


def four_gather(pieces):
    count = len(pieces)
    return Part(
        four_stages,
        list(pieces),
        [VMEM] * count,
        [jax.ShapeDtypeStruct((4,) + piece.shape, piece.dtype) for piece in pieces],
        [VMEM] * count,
        [pltpu.SemaphoreType.DMA((count,))] * 7,
    )


def grid_four_gather(pieces):
    base = grid_gather(pieces)
    base_outs = len(base.outs)

    def make(ins, outs, scratch):
        stages = base.make(ins, outs[:base_outs], scratch[: len(base.scratch)])
        four = four_stages([outs[0]], outs[base_outs:], scratch[len(base.scratch) :])
        for name, stage in four.items():
            stages["four_" + name] = stage
        return stages

    first = base.outs[0]
    return Part(
        make,
        base.ins,
        base.in_specs,
        base.outs + [jax.ShapeDtypeStruct((4,) + first.shape, first.dtype)],
        base.out_specs + [ANY],
        base.scratch + [pltpu.SemaphoreType.DMA((1,))] * 7,
    )


def four_reduce(pieces):
    count = len(pieces)

    def make(ins, outs, scratch):
        near, out_x, in_x = (scratch[i * count : (i + 1) * count] for i in range(3))
        sib_send, sib_recv, x_send, x_recv = scratch[3 * count :]
        a, b, core, x = place()
        own, across = core * 2 + x, core * 2 + 1 - x
        sibling, peer = device(a, b, 1 - core, x), device(a, b, core, 1 - x)
        to_sib, to_x = [], []
        for p in range(count):
            to_sib.append(
                [
                    remote(
                        ins[p].at[(1 - core) * 2 + side], near[p].at[i], sib_send.at[p, i],
                        sib_recv.at[p, i], sibling,
                    )
                    for i, side in enumerate((1 - x, x))
                ]
            )
            to_x.append(remote(out_x[p], in_x[p], x_send.at[p], x_recv.at[p], peer))

        def start():
            for i in range(2):
                for p in range(count):
                    to_sib[p][i].start()

        def middle():
            for p in range(count):
                to_sib[p][0].wait_recv()
                out_x[p][...] = (ins[p][across] + near[p][0]).astype(out_x[p].dtype)
                to_x[p].start()

        def own_sums():
            for p in range(count):
                to_sib[p][1].wait_recv()
                outs[p][...] = ins[p][own] + near[p][1]

        def end():
            for p in range(count):
                to_x[p].wait_recv()
                outs[p][...] += in_x[p][...].astype(jnp.float32)
                to_x[p].wait_send()
                for i in range(2):
                    to_sib[p][i].wait_send()

        return dict(start=start, middle=middle, own=own_sums, end=end)

    dma = pltpu.SemaphoreType.DMA
    shapes = [piece.shape[1:] for piece in pieces]
    return Part(
        make,
        list(pieces),
        [VMEM] * count,
        [jax.ShapeDtypeStruct(shape, jnp.float32) for shape in shapes],
        [VMEM] * count,
        [pltpu.VMEM((2,) + shape, jnp.float32) for shape in shapes]
        + [pltpu.VMEM(shape, jnp.bfloat16) for shape in shapes] * 2
        + [dma((count, 2))] * 2
        + [dma((count,))] * 2,
    )


GATHER_PLAN = [
    (0, "start"), (1, "start"), (0, "hop"), (1, "middle"), (0, "more"), (1, "end"), (0, "end"),
]
GATHER_REDUCE_PLAN = [
    (0, "start"), (1, "start"), (1, "middle"), (1, "own"), (0, "hops"), (1, "end"), (0, "end"),
]
REDUCE_REDUCE_PLAN = [
    (1, "start"), (0, "start"), (1, "middle"), (1, "own"), (0, "steps"), (1, "end"), (0, "end"),
]
REDUCE_GATHER_PLAN = [
    (1, "start"), (0, "start"), (0, "first"), (1, "middle"), (0, "others"), (1, "end"), (0, "end"),
]


def total_devices():
    return lax.axis_size("dp") * lax.axis_size("seq")


def own_index():
    return lax.axis_index("dp") * lax.axis_size("seq") + lax.axis_index("seq")


def device_at(index):
    ways = lax.axis_size("seq")
    return (index // ways, index % ways)


def greet_all():
    devices, me = total_devices(), own_index()
    barrier = pltpu.get_barrier_semaphore()

    def signal(i, carry):
        target = device_at((me + i) % devices)
        pl.semaphore_signal(barrier, inc=1, device_id=target, device_id_type=MESH_ID)
        return carry

    lax.fori_loop(1, devices, signal, 0)
    pl.semaphore_wait(barrier, devices - 1)


def spread_all(blocks, landed, source, send, recv):
    devices, me = total_devices(), own_index()

    def post(i, carry):
        to = (me + i) % devices
        remote(source(to), landed.at[me], send, recv, device_at(to)).start()
        return carry

    lax.fori_loop(1, devices, post, 0)


def settle_all(landed, spare, send, recv):
    count = total_devices() - 1
    both = remote(
        landed.at[pl.ds(0, count)], spare.at[pl.ds(0, count)], send, recv,
        device_at((own_index() + 1) % total_devices()),
    )
    both.wait_recv()
    both.wait_send()


def closing(blocks, bias_tiles, weight):
    devices, rows, width = blocks.shape
    model_width = weight.shape[0]
    tiles = model_width // 128
    sums_shape = (devices, rows, 128)

    def make(ins, outs, scratch):
        blocks, bias_tiles, weight = ins
        columns, sums = outs
        landed, terms, landed_terms, part, *sems = scratch
        me = own_index()

        def start():
            spread_all(blocks, landed, lambda to: blocks.at[to], sems[0], sems[1])
            landed[me] = blocks[me]

        def middle():
            settle_all(landed, landed, sems[0], sems[1])
            total = jnp.sum(landed[...], axis=0)
            columns[...] = total
            cond = lax.dot_general(
                total, weight[...], (((1,), (1,)), ((), ())),
                precision=lax.Precision.HIGHEST, preferred_element_type=jnp.float32,
            )
            for i in range(tiles):
                terms[i] = cond[:, i * 128 : (i + 1) * 128]
            terms[pl.ds(tiles, devices - tiles)] = bias_tiles[...]
            spread_all(terms, landed_terms, lambda to: terms.at[to], sems[2], sems[3])
            landed_terms[me] = terms[me]

        def late():
            settle_all(landed_terms, landed_terms, sems[2], sems[3])
            total = jnp.sum(landed_terms[...], axis=0)
            part[...] = total
            spread_all(part, sums, lambda to: part, sems[4], sems[5])
            sums[me] = total

        def end():
            settle_all(sums, sums, sems[4], sems[5])

        return dict(start=start, middle=middle, late=late, end=end)

    return Part(
        make,
        [blocks, bias_tiles, weight],
        [VMEM] * 3,
        [
            jax.ShapeDtypeStruct((rows, width), jnp.float32),
            jax.ShapeDtypeStruct(sums_shape, jnp.float32),
        ],
        [VMEM] * 2,
        [
            pltpu.VMEM(blocks.shape, jnp.float32),
            pltpu.VMEM(sums_shape, jnp.float32),
            pltpu.VMEM(sums_shape, jnp.float32),
            pltpu.VMEM((rows, 128), jnp.float32),
        ]
        + [pltpu.SemaphoreType.DMA(())] * 6,
    )


CLOSING_PLAN = [
    (1, "start"), (0, "start"), (1, "middle"), (0, "first"), (1, "late"), (0, "others"),
    (1, "end"), (0, "end"),
]


def pad_to(values, axis, size):
    pads = [(0, 0)] * values.ndim
    pads[axis] = (0, size - values.shape[axis])
    return jnp.pad(values, pads)


def swap_core(values):
    return lax.ppermute(values, "dp", [(i, i ^ 1) for i in range(lax.axis_size("dp"))])


def swap_x(values):
    return lax.ppermute(values, "seq", [(0, 1), (1, 0)])


def row_moves(turn):
    groups = lax.axis_size("dp")
    chips, pairs = groups // 2, []
    for d in range(groups):
        for x in range(2):
            block = d * 2 + (turn + x) % 2
            f, c = block // chips, block % chips
            pairs.append((d * 2 + x, (c * 2 + f % 2) * 2 + f // 2))
    return pairs


def flip(pair, swapped):
    low = jnp.where(swapped, pair[1], pair[0])
    high = jnp.where(swapped, pair[0], pair[1])
    return low, high


def rows_to_blocks(pieces):
    x = lax.axis_index("seq")
    b = (lax.axis_index("dp") // 2) % 2
    sent = flip(pieces, x == 1)
    got = [lax.ppermute(sent[turn], ("dp", "seq"), row_moves(turn)) for turn in range(2)]
    return jnp.concatenate(flip(got, b == 1), axis=1)


def blocks_to_rows(block):
    x = lax.axis_index("seq")
    b = (lax.axis_index("dp") // 2) % 2
    half = block.shape[1] // 2
    sent = flip((block[:, :half], block[:, half:]), b == 1)
    got = [
        lax.ppermute(sent[turn], ("dp", "seq"), [(q, p) for p, q in row_moves(turn)])
        for turn in range(2)
    ]
    return flip(got, x == 1)


def cut(values, index, size, axis=1):
    return lax.dynamic_slice_in_dim(values, index * size, size, axis)


def gather_columns(qkv_block, up_block):
    x, core = lax.axis_index("seq"), lax.axis_index("dp") % 2
    width = qkv_block.shape[1] // 6
    first = x == 0
    got = swap_x(qkv_block[:, 2 * width : 4 * width])
    head, tail = qkv_block[:, : 2 * width], qkv_block[:, 4 * width :]
    queries = jnp.where(first, head, got)
    keys = jnp.where(first, tail, head)
    values = jnp.where(first, got, tail)
    high = core == 1

    def halves(block):
        size = block.shape[1] // 2
        low, up = block[:, :size], block[:, size:]
        return jnp.where(high, up, low), jnp.where(high, low, up)

    pairs = [halves(block) for block in (queries, keys, values, up_block)]
    mine = jnp.concatenate([pair[0] for pair in pairs], axis=1)
    other = swap_core(jnp.concatenate([pair[1] for pair in pairs], axis=1))
    full = jnp.concatenate(
        [jnp.where(high, other, mine), jnp.where(high, mine, other)], axis=0
    )
    return full[:, : 3 * width], full[:, 3 * width :]


def scatter_columns(qkv_block, up_block):
    x, core = lax.axis_index("seq"), lax.axis_index("dp") % 2
    width = qkv_block.shape[1] // 3
    first, high = x == 0, core == 1
    full = jnp.concatenate([qkv_block, up_block], axis=1)
    rows = full.shape[0] // 2
    low, up = full[:rows], full[rows:]
    mine = jnp.where(high, up, low)
    other = swap_core(jnp.where(high, low, up))
    parts = []
    for start, stop in ((0, width), (width, 2 * width), (2 * width, 3 * width), (3 * width, None)):
        own, far = mine[:, start:stop], other[:, start:stop]
        parts.append(
            jnp.concatenate([jnp.where(high, far, own), jnp.where(high, own, far)], axis=1)
        )
    queries, keys, values, up_rows = parts
    got = swap_x(jnp.where(first, values, queries))
    qkv_rows = jnp.concatenate(
        [jnp.where(first, queries, keys), got, jnp.where(first, keys, values)],
        axis=1,
    )
    return qkv_rows, up_rows


def on_device_grid(
    latents,
    condition,
    slot_latent,
    slot_counts,
    output_gradient,
    ada_weight,
    ada_bias,
    qkv_weight,
    qkv_bias,
    out_weight,
    out_bias,
    up_weight,
    up_bias,
    down_weight,
    down_bias,
    mean_adaw,
    mean_adab,
    mean_qkvw,
    mean_qkvb,
    mean_outw,
    mean_outb,
    mean_upw,
    mean_upb,
    mean_downw,
    mean_downb,
    sqmean_adaw,
    sqmean_adab,
    sqmean_qkvw,
    sqmean_qkvb,
    sqmean_outw,
    sqmean_outb,
    sqmean_upw,
    sqmean_upb,
    sqmean_downw,
    sqmean_downb,
):
    slot_total, tok_dev, model_width = latents.shape
    scale = HD ** (-0.5)
    latent_count = condition.shape[0]
    x_index, group = lax.axis_index("seq"), lax.axis_index("dp")
    core = group % 2
    share = 2 * x_index + core
    live = slot_counts[0] > 0
    slot_match = ((slot_latent[0, 0] == jnp.arange(latent_count)) & live).astype(jnp.float32)
    bf16 = jnp.bfloat16

    silu_cond = jax.nn.silu(condition).astype(bf16)
    mod_cols = jnp.dot(
        silu_cond, ada_weight.astype(bf16), preferred_element_type=jnp.float32
    ) + rounded(ada_bias)

    qkv_block, up_block = gather_columns(qkv_weight.astype(bf16), up_weight.astype(bf16))
    hidden_rows = down_weight.shape[0] // 2
    out_rows = out_weight.shape[0] // 2
    down_b, out_b = down_weight.astype(bf16), out_weight.astype(bf16)
    rows_block = rows_to_blocks(
        [
            jnp.concatenate(
                [cut(down_b, i, hidden_rows, 0), cut(out_b, i, out_rows, 0)], axis=0
            )
            for i in range(2)
        ]
    )
    down_block, out_block = rows_block[:hidden_rows], rows_block[hidden_rows:]
    grid_plan = [
        (0, stage)
        for stage in (
            "start", "hops", "early", "four_start", "four_middle", "four_end", "late",
        )
    ]
    ((_, qkv_grid, out_grid, mod_four),) = run_parts(
        [grid_four_gather([mod_cols, qkv_block, out_block])], grid_plan, 1, True, True
    )
    mat_qkv = qkv_grid.reshape(model_width, -1)
    mat_out = out_grid.reshape(-1, model_width)
    width = mat_out.shape[0]
    hidden_width = up_block.shape[1]
    heads = width // HD

    slot_mod = jnp.einsum("jcln,l->cjn", mod_four, slot_match, precision=lax.Precision.HIGHEST)
    slot_mod = slot_mod.reshape(6, 1, model_width)
    shift_att, scale_att, gate_att, shift_mlp, scale_mlp, gate_mlp = (
        slot_mod[i] for i in range(6)
    )

    biases = (qkv_bias, out_bias, down_bias)
    bias_own = jnp.concatenate(biases).astype(bf16)[None]
    bias_other = swap_x(bias_own)
    bias_pair = flip((bias_own, bias_other), x_index == 1)
    starts = [0]
    for item in biases:
        starts.append(starts[-1] + item.shape[0])
    vec_qkv, vec_out, vec_down = (
        jnp.concatenate(
            [half[0, starts[i] : starts[i + 1]] for half in bias_pair]
        ).astype(jnp.float32)
        for i in range(3)
    )
    vec_qkv = cut(vec_qkv.reshape(3, -1), share, width).reshape(-1)
    vec_up = cut(rounded(up_bias), core, hidden_width, 0)

    tokens = latents[0]
    upstream = jnp.where(live, output_gradient[0], 0.0)
    normed_att, spread_att = normalize(tokens)
    attn_own = (normed_att * (1.0 + scale_att) + shift_att).astype(bf16)
    back_down = upstream * gate_mlp
    (up_grid,), four_pair = run_parts(
        [grid_gather([up_block]), four_gather([attn_own, back_down.astype(bf16)])],
        GATHER_PLAN, 2, True, True,
    )
    attn_in, back_down_all = (item.reshape(-1, model_width) for item in four_pair)
    mat_up = up_grid.reshape(model_width, -1)
    qkv_all = (jnp.dot(attn_in, mat_qkv, preferred_element_type=jnp.float32) + vec_qkv).astype(bf16)
    split = (2, -1, heads, HD)
    queries = qkv_all[:, :width].reshape(split)
    keys_heads = qkv_all[:, width : 2 * width].reshape(split)
    values_heads = qkv_all[:, 2 * width :].reshape(split)
    scores = (
        jnp.einsum("sqhd,skhd->shqk", queries, keys_heads, preferred_element_type=jnp.float32)
        * scale
    )
    row_max = jnp.max(scores, axis=-1, keepdims=True)
    row_total = jnp.sum(jnp.exp(scores - row_max), axis=-1, keepdims=True)
    attn_probs = jnp.exp(scores - row_max) / row_total
    probs_b = attn_probs.astype(bf16)
    attended = jnp.einsum(
        "shqk,skhd->sqhd", probs_b, values_heads, preferred_element_type=jnp.float32
    )
    attended_b = attended.reshape(-1, width).astype(bf16)
    blocks = (4, tok_dev, model_width)
    out_terms = jnp.dot(attended_b, mat_out, preferred_element_type=jnp.float32)
    half = model_width // 2
    (down_low,), (branch_sum,) = run_parts(
        [grid_gather([down_block[:, :half]]), four_reduce([out_terms.reshape(blocks)])],
        GATHER_REDUCE_PLAN, 3, True, True,
    )
    branch_att = branch_sum + vec_out
    middle = tokens + gate_att * branch_att
    normed_mlp, spread_mlp = normalize(middle)
    mlp_own = (normed_mlp * (1.0 + scale_mlp) + shift_mlp).astype(bf16)
    (down_high,), (mlp_four,) = run_parts(
        [grid_gather([down_block[:, half:]]), four_gather([mlp_own])], GATHER_PLAN, 4, True, True
    )
    mat_down = jnp.concatenate([down_low, down_high], axis=2).reshape(-1, model_width)
    mlp_in = mlp_four.reshape(-1, model_width)
    hidden = jnp.dot(mlp_in, mat_up, preferred_element_type=jnp.float32) + vec_up
    activated = gelu_tanh(hidden).astype(bf16)
    branch_terms = jnp.dot(activated, mat_down, preferred_element_type=jnp.float32)
    term_down = weight_term(activated, back_down_all)
    sum_downb = jnp.sum(back_down, axis=0)
    back_hidden = jnp.einsum(
        "rd,fd->rf", back_down_all, mat_down, preferred_element_type=jnp.float32
    ) * gelu_slope(hidden)
    back_hidden_b = back_hidden.astype(bf16)
    term_up = weight_term(mlp_in, back_hidden_b)
    sum_upb = jnp.sum(back_hidden, axis=0)
    back_terms = jnp.einsum(
        "rf,cf->rc", back_hidden_b, mat_up, preferred_element_type=jnp.float32
    )
    chips = lax.axis_size("dp") // 2

    def by_chip(term):
        return term.reshape(chips, -1, term.shape[1])

    (down_sum,), (branch_mlp, back_mlp_in) = run_parts(
        [
            grid_reduce([by_chip(term_down)]),
            four_reduce([branch_terms.reshape(blocks), back_terms.reshape(blocks)]),
        ],
        REDUCE_REDUCE_PLAN, 5, True, True,
    )
    branch_mlp = branch_mlp + vec_down
    block_output = jnp.where(live, middle + gate_mlp * branch_mlp, 0.0)
    back_middle = upstream + norm_back(back_mlp_in * (1.0 + scale_mlp), normed_mlp, spread_mlp)
    back_att = back_middle * gate_att
    (up_sum,), (back_att_four,) = run_parts(
        [grid_reduce([by_chip(term_up)]), four_gather([back_att.astype(bf16)])],
        REDUCE_GATHER_PLAN, 6, True, True,
    )
    back_att_all = back_att_four.reshape(-1, model_width)
    term_out = weight_term(attended_b, back_att_all)
    sum_outb = jnp.sum(back_att, axis=0)
    back_attended = jnp.einsum(
        "rd,cd->rc", back_att_all, mat_out, preferred_element_type=jnp.float32
    ).astype(bf16)
    back_attended = back_attended.reshape(split)
    back_probs = jnp.einsum(
        "sqhd,skhd->shqk", back_attended, values_heads, preferred_element_type=jnp.float32
    )
    row_delta = jnp.einsum("sqhd,sqhd->shq", back_attended.astype(jnp.float32), attended)[..., None]
    back_scores = (attn_probs * (back_probs - row_delta) * scale).astype(bf16)
    back_queries = jnp.einsum(
        "shqk,skhd->sqhd", back_scores, keys_heads, preferred_element_type=jnp.float32
    )
    back_keys = jnp.einsum(
        "shqk,sqhd->skhd", back_scores, queries, preferred_element_type=jnp.float32
    )
    back_values = jnp.einsum(
        "shqk,sqhd->skhd", probs_b, back_attended, preferred_element_type=jnp.float32
    )
    back_qkv = jnp.concatenate(
        [item.reshape(-1, width) for item in (back_queries, back_keys, back_values)], axis=1
    )
    back_qkv_b = back_qkv.astype(bf16)
    term_qkv = weight_term(attn_in, back_qkv_b)
    sum_qkvb = jnp.sum(back_qkv, axis=0)
    attn_terms = jnp.einsum(
        "rd,cd->rc", back_qkv_b, mat_qkv, preferred_element_type=jnp.float32
    )
    ((back_attn_in,),) = run_parts(
        [four_reduce([attn_terms.reshape(blocks)])],
        [(0, "start"), (0, "middle"), (0, "own"), (0, "end")], 7, False, True,
    )
    latent_gradient = jnp.where(
        live,
        back_middle + norm_back(back_attn_in * (1.0 + scale_att), normed_att, spread_att),
        0.0,
    )[None]
    block_output = block_output[None]
    slot_modgrad = jnp.concatenate(
        [
            jnp.sum(back_attn_in, axis=0),
            jnp.sum(back_attn_in * normed_att, axis=0),
            jnp.sum(back_middle * branch_att, axis=0),
            jnp.sum(back_mlp_in, axis=0),
            jnp.sum(back_mlp_in * normed_mlp, axis=0),
            jnp.sum(upstream * branch_mlp, axis=0),
        ]
    )
    devices, own_cols = total_devices(), ada_bias.shape[0]
    qkvb_wide = lax.dynamic_update_slice(
        jnp.zeros((3, 4 * width), jnp.float32), sum_qkvb.reshape(3, width), (0, share * width)
    ).reshape(-1)
    upb_wide = lax.dynamic_update_slice(
        jnp.zeros((4 * hidden_width,), jnp.float32), sum_upb, (share * hidden_width,)
    )
    bias_sums = (qkvb_wide, sum_outb, upb_wide, sum_downb)
    tiles = model_width // 128
    bias_flat = jnp.concatenate(bias_sums)
    tile = latent_count * 128
    bias_tiles = pad_to(bias_flat, 0, (devices - tiles) * tile).reshape(-1, latent_count, 128)
    wide = -(-own_cols // 128) * 128
    sent = pad_to(slot_modgrad.reshape(devices, 1, own_cols), 2, wide) * slot_match[:, None]
    (qkv_sum, out_sum), (columns, sums) = run_parts(
        [
            grid_reduce([by_chip(term_qkv), by_chip(term_out)]),
            closing(sent, bias_tiles, pad_to(rounded(ada_weight), 1, wide)),
        ],
        CLOSING_PLAN, 8, True, None,
    )
    modgrad_cols = columns[:, :own_cols]
    cond_sum = jnp.moveaxis(sums[:tiles], 0, 1).reshape(latent_count, model_width)
    totals, start, bias_totals = sums[tiles:].reshape(-1), 0, []
    for item in bias_sums:
        bias_totals.append(totals[start : start + item.shape[0]])
        start += item.shape[0]
    total_qkvb, total_outb, total_upb, total_downb = bias_totals
    grad_qkvw, grad_upw = scatter_columns(qkv_sum, up_sum)
    owned = blocks_to_rows(jnp.concatenate([down_sum, out_sum], axis=0))
    grad_downw = jnp.concatenate([item[:hidden_rows] for item in owned], axis=0)
    grad_outw = jnp.concatenate([item[hidden_rows:] for item in owned], axis=0)
    grad_qkvw, grad_outw, grad_upw, grad_downw = (
        item.astype(jnp.float32) for item in (grad_qkvw, grad_outw, grad_upw, grad_downw)
    )

    grad_adaw = jnp.dot(
        rounded(jax.nn.silu(condition)).T, modgrad_cols, precision=lax.Precision.HIGHEST
    )
    grad_adab = jnp.sum(modgrad_cols, axis=0)
    condition_grad = cond_sum * silu_slope(condition)
    seq_index = lax.axis_index("seq")

    def own_part(full_sum, local_bias):
        length = local_bias.shape[0]
        return lax.dynamic_slice_in_dim(full_sum, seq_index * length, length)

    grad_qkvb = own_part(total_qkvb, qkv_bias)
    grad_outb = own_part(total_outb, out_bias)
    grad_upb = own_part(total_upb, up_bias)
    grad_downb = own_part(total_downb, down_bias)
    grads_all = (
        grad_adaw,
        grad_adab,
        grad_qkvw,
        grad_qkvb,
        grad_outw,
        grad_outb,
        grad_upw,
        grad_upb,
        grad_downw,
        grad_downb,
    )
    params_all = (
        ada_weight,
        ada_bias,
        qkv_weight,
        qkv_bias,
        out_weight,
        out_bias,
        up_weight,
        up_bias,
        down_weight,
        down_bias,
    )
    means_all = (
        mean_adaw,
        mean_adab,
        mean_qkvw,
        mean_qkvb,
        mean_outw,
        mean_outb,
        mean_upw,
        mean_upb,
        mean_downw,
        mean_downb,
    )
    squares_all = (
        sqmean_adaw,
        sqmean_adab,
        sqmean_qkvw,
        sqmean_qkvb,
        sqmean_outw,
        sqmean_outb,
        sqmean_upw,
        sqmean_upb,
        sqmean_downw,
        sqmean_downb,
    )
    updates = [
        adamw_step(p_item, g_item, m_item, v_item)
        for p_item, g_item, m_item, v_item in zip(params_all, grads_all, means_all, squares_all)
    ]
    newvals = tuple((entry[0] for entry in updates))
    newmeans = tuple((entry[1] for entry in updates))
    newsqrs = tuple((entry[2] for entry in updates))
    return (
        (block_output, latent_gradient, condition_grad) + grads_all + newvals + newmeans + newsqrs
    )


def fits(mesh, slots, latent_count, width, hidden):
    groups, ways = mesh.shape["dp"], mesh.shape["seq"]
    return (
        slots == groups
        and ways == 2
        and groups % 4 == 0
        and H % 4 == 0
        and width == H * HD
        and width % (2 * groups * 4) == 0
        and hidden % (2 * groups * 16) == 0
        and width % 128 == 0
        and width // 128 - (-(5 * width + hidden) // (latent_count * 128)) <= groups * ways
    )


def build(mesh, on_device):
    return jax.shard_map(
        on_device,
        mesh=mesh,
        in_specs=(
            P("dp", "seq", None),
            P(),
            P("dp", None),
            P("dp"),
            P("dp", "seq", None),
            P(None, ("dp", "seq")),
            P(("dp", "seq")),
            P("dp", "seq"),
            P("seq"),
            P("dp", "seq"),
            P("seq"),
            P("dp", "seq"),
            P("seq"),
            P("dp", "seq"),
            P("seq"),
            P(None, ("dp", "seq")),
            P(("dp", "seq")),
            P("dp", "seq"),
            P("seq"),
            P("dp", "seq"),
            P("seq"),
            P("dp", "seq"),
            P("seq"),
            P("dp", "seq"),
            P("seq"),
            P(None, ("dp", "seq")),
            P(("dp", "seq")),
            P("dp", "seq"),
            P("seq"),
            P("dp", "seq"),
            P("seq"),
            P("dp", "seq"),
            P("seq"),
            P("dp", "seq"),
            P("seq"),
        ),
        out_specs=(
            P("dp", "seq", None),
            P("dp", "seq", None),
            P(),
            P(None, ("dp", "seq")),
            P(("dp", "seq")),
            P("dp", "seq"),
            P("seq"),
            P("dp", "seq"),
            P("seq"),
            P("dp", "seq"),
            P("seq"),
            P("dp", "seq"),
            P("seq"),
            P(None, ("dp", "seq")),
            P(("dp", "seq")),
            P("dp", "seq"),
            P("seq"),
            P("dp", "seq"),
            P("seq"),
            P("dp", "seq"),
            P("seq"),
            P("dp", "seq"),
            P("seq"),
            P(None, ("dp", "seq")),
            P(("dp", "seq")),
            P("dp", "seq"),
            P("seq"),
            P("dp", "seq"),
            P("seq"),
            P("dp", "seq"),
            P("seq"),
            P("dp", "seq"),
            P("seq"),
            P(None, ("dp", "seq")),
            P(("dp", "seq")),
            P("dp", "seq"),
            P("seq"),
            P("dp", "seq"),
            P("seq"),
            P("dp", "seq"),
            P("seq"),
            P("dp", "seq"),
            P("seq"),
        ),
        check_vma=False,
    )


def solution(mesh):
    def program(latents, condition, *rest):
        hidden, width = rest[11].shape
        chosen = fits(mesh, latents.shape[0], condition.shape[0], width, hidden)
        return build(mesh, on_device_grid if chosen else on_device_general)(
            latents, condition, *rest
        )

    return program
```

```python
import functools

import jax
import jax.numpy as jnp
from jax import lax
from jax.experimental import pallas as pl
from jax.experimental.pallas import tpu as pltpu
from jax.sharding import PartitionSpec as P

H = 16
HD = 72
STEP = 2


EPS_NORM = 1e-06
GELU_COEF = 0.7978845608
GELU_CUBE = 0.044715
BETA_ONE = 0.9
BETA_TWO = 0.999
LEARN_RATE = 0.05
EPS_ADAM = 1e-08


def rounded(values):
    return lax.optimization_barrier(values.astype(jnp.bfloat16)).astype(jnp.float32)


def normalize(values):
    center = values - jnp.mean(values, axis=-1, keepdims=True)
    spread = lax.rsqrt(jnp.mean(center * center, axis=-1, keepdims=True) + EPS_NORM)
    return (center * spread, spread)


def norm_back(upstream, normed, spread):
    return spread * (
        upstream
        - jnp.mean(upstream, axis=-1, keepdims=True)
        - normed * jnp.mean(upstream * normed, axis=-1, keepdims=True)
    )


def gelu_tanh(values):
    tanh_part = jnp.tanh(GELU_COEF * (values + GELU_CUBE * values * values * values))
    return 0.5 * values * (1.0 + tanh_part)


def gelu_slope(values):
    tanh_part = jnp.tanh(GELU_COEF * (values + GELU_CUBE * values * values * values))
    return 0.5 * (1.0 + tanh_part) + 0.5 * values * (1.0 - tanh_part * tanh_part) * GELU_COEF * (
        1.0 + 3.0 * GELU_CUBE * values * values
    )


def silu_slope(values):
    sigmoid_part = jax.nn.sigmoid(values)
    return sigmoid_part * (1.0 + values * (1.0 - sigmoid_part))


def adamw_step(parameter, gradient, first_mom, second):
    first_new = BETA_ONE * first_mom + (1.0 - BETA_ONE) * gradient
    second_new = BETA_TWO * second + (1.0 - BETA_TWO) * gradient * gradient
    first_hat = first_new / (1.0 - BETA_ONE**STEP)
    second_hat = second_new / (1.0 - BETA_TWO**STEP)
    return (
        parameter - LEARN_RATE * first_hat / (jnp.sqrt(second_hat) + EPS_ADAM),
        first_new,
        second_new,
    )


def flat_index(axes):
    index = lax.axis_index(axes[0])
    for axis in axes[1:]:
        index = index * lax.axis_size(axis) + lax.axis_index(axis)
    return index


def swap_bit(values, axes, step):
    total = 1
    for axis in axes:
        total *= lax.axis_size(axis)
    return lax.ppermute(values, axes, [(i, i ^ step) for i in range(total)])


def axes_size(axes):
    total = 1
    for axis in axes:
        total *= lax.axis_size(axis)
    return total


def gather_tree(values, axes):
    index, blocks, step = flat_index(axes), values[None], 1
    while step < axes_size(axes):
        other = swap_bit(blocks, axes, step)
        upper = (index // step) % 2 == 1
        blocks = jnp.concatenate(
            [jnp.where(upper, other, blocks), jnp.where(upper, blocks, other)], axis=0
        )
        step *= 2
    return blocks


def scatter_tree(blocks, axes, sent=None):
    index, step = flat_index(axes), axes_size(axes) // 2
    while step >= 1:
        low, high = blocks[:step], blocks[step:]
        upper = (index // step) % 2 == 1
        away = jnp.where(upper, low, high)
        if sent is not None:
            away = away.astype(sent)
        kept = jnp.where(upper, high, low)
        blocks = kept + swap_bit(away, axes, step).astype(kept.dtype)
        step //= 2
    return blocks[0]


def sum_tree(values, axes):
    step = 1
    while step < axes_size(axes):
        values = values + swap_bit(values, axes, step)
        step *= 2
    return values


def join_columns(halves, widths):
    parts, start = [], 0
    for width in widths:
        part = halves[:, :, start : start + width]
        parts.append(jnp.moveaxis(part, 0, 1).reshape(part.shape[1], -1))
        start += width
    return parts


def split_columns(parts):
    ways = lax.axis_size("seq")
    blocks = [
        jnp.moveaxis(part.reshape(part.shape[0], ways, -1), 1, 0) for part in parts
    ]
    return jnp.concatenate(blocks, axis=2)


def piece_moves(turn):
    rows, ways = lax.axis_size("dp"), lax.axis_size("seq")
    pairs = []
    for g in range(rows):
        for x in range(ways):
            piece = g * ways + (turn + x) % ways
            pairs.append((g * ways + x, (piece % rows) * ways + piece // rows))
    return pairs


def own_piece():
    return lax.axis_index("seq") * lax.axis_size("dp") + lax.axis_index("dp")


def pick(blocks, index):
    return lax.dynamic_index_in_dim(blocks, index, 0, keepdims=False)


def rows_from_owners(block):
    ways, x = lax.axis_size("seq"), lax.axis_index("seq")
    pieces = block.reshape(ways, -1, block.shape[1])
    got = jnp.stack(
        [
            lax.ppermute(pick(pieces, (turn + x) % ways), ("dp", "seq"), piece_moves(turn))
            for turn in range(ways)
        ]
    )
    place = own_piece() % ways
    return jnp.concatenate([pick(got, (place - i + ways) % ways) for i in range(ways)], axis=1)


def rows_to_owners(piece):
    ways, x = lax.axis_size("seq"), lax.axis_index("seq")
    columns = jnp.moveaxis(piece.reshape(piece.shape[0], ways, -1), 1, 0)
    place = own_piece() % ways
    got = jnp.stack(
        [
            lax.ppermute(
                pick(columns, (place - turn + ways) % ways),
                ("dp", "seq"),
                [(taker, owner) for owner, taker in piece_moves(turn)],
            )
            for turn in range(ways)
        ]
    )
    ordered = jnp.stack([pick(got, (q - x + ways) % ways) for q in range(ways)])
    return ordered.reshape(-1, ordered.shape[2])


def all_tokens(values):
    return gather_tree(values, ("seq",)).reshape(-1, values.shape[1])


def own_tokens(terms):
    blocks = terms.reshape(lax.axis_size("seq"), -1, terms.shape[1])
    return scatter_tree(blocks, ("seq",), jnp.bfloat16)


def weight_term(left, right):
    return jnp.einsum("rc,rd->cd", left, right, preferred_element_type=jnp.float32).astype(
        jnp.bfloat16
    )


def spread_terms(terms):
    widths = [term.shape[1] // lax.axis_size("seq") for term in terms]
    joined = jnp.concatenate(terms, axis=1) if len(terms) > 1 else terms[0]
    rows = lax.psum_scatter(joined, "dp", scatter_dimension=0, tiled=True)
    pieces, start = [], 0
    for term in terms:
        pieces.append(rows[:, start : start + term.shape[1]])
        start += term.shape[1]
    own = scatter_tree(split_columns(pieces).astype(jnp.float32), ("seq",), jnp.bfloat16)
    blocks, start = [], 0
    for width in widths:
        blocks.append(own[:, start : start + width])
        start += width
    return blocks


def on_device_general(
    latents,
    condition,
    slot_latent,
    slot_counts,
    output_gradient,
    ada_weight,
    ada_bias,
    qkv_weight,
    qkv_bias,
    out_weight,
    out_bias,
    up_weight,
    up_bias,
    down_weight,
    down_bias,
    mean_adaw,
    mean_adab,
    mean_qkvw,
    mean_qkvb,
    mean_outw,
    mean_outb,
    mean_upw,
    mean_upb,
    mean_downw,
    mean_downb,
    sqmean_adaw,
    sqmean_adab,
    sqmean_qkvw,
    sqmean_qkvb,
    sqmean_outw,
    sqmean_outb,
    sqmean_upw,
    sqmean_upb,
    sqmean_downw,
    sqmean_downb,
):
    slot_total, tok_dev, model_width = latents.shape
    row_count = slot_total * tok_dev
    scale = HD ** (-0.5)
    live_slots = jnp.arange(slot_total) < slot_counts[0]
    live_mask = live_slots[:, None, None]
    latent_count = condition.shape[0]
    slot_matches = (
        (slot_latent[0][:, None] == jnp.arange(latent_count)[None, :]) & live_slots[:, None]
    ).astype(jnp.float32)
    silu_cond = jax.nn.silu(condition).astype(jnp.bfloat16)
    mod_cols = jnp.dot(
        silu_cond, ada_weight.astype(jnp.bfloat16), preferred_element_type=jnp.float32
    ) + rounded(ada_bias)
    modulation = jnp.moveaxis(gather_tree(mod_cols, ("dp", "seq")), 0, 1).reshape(
        latent_count, -1
    )
    slot_mod = jnp.dot(slot_matches, modulation, precision=lax.Precision.HIGHEST)[:, None, :]
    shift_att, scale_att, gate_att, shift_mlp, scale_mlp, gate_mlp = jnp.split(slot_mod, 6, axis=2)
    upstream = jnp.where(live_mask, output_gradient, 0.0)
    biases = (qkv_bias, out_bias, down_bias)
    bias_rows = gather_tree(
        jnp.concatenate(biases).astype(jnp.bfloat16)[None], ("seq",)
    )
    vec_qkv, vec_out, vec_down = (
        part[0].astype(jnp.float32)
        for part in join_columns(bias_rows, [item.shape[0] for item in biases])
    )
    wide = (qkv_weight, out_weight)
    wide_halves = gather_tree(jnp.concatenate(wide, axis=1).astype(jnp.bfloat16), ("seq",))
    wide_rows = jnp.concatenate(
        join_columns(wide_halves, [item.shape[1] for item in wide])
        + [up_weight.astype(jnp.bfloat16)],
        axis=1,
    )
    wide_full = lax.all_gather(wide_rows, "dp", axis=0, tiled=True)
    qkv_end = 3 * model_width
    mat_qkv = wide_full[:, :qkv_end]
    mat_out = wide_full[:, qkv_end : qkv_end + model_width]
    mat_up = wide_full[:, qkv_end + model_width :]
    down_rows = rows_from_owners(down_weight.astype(jnp.bfloat16))
    mat_down = lax.all_gather(down_rows, "dp", axis=0, tiled=True)
    normed_att, spread_att = normalize(latents)
    attn_in = (
        (normed_att * (1.0 + scale_att) + shift_att)
        .astype(jnp.bfloat16)
        .reshape(row_count, model_width)
    )
    qkv_all = (jnp.dot(attn_in, mat_qkv, preferred_element_type=jnp.float32) + vec_qkv).astype(
        jnp.bfloat16
    )
    queries = qkv_all[:, :model_width].reshape(slot_total, tok_dev, H, HD)
    keys_own = qkv_all[:, model_width : 2 * model_width].reshape(slot_total, tok_dev, model_width)
    values_own = qkv_all[:, 2 * model_width :].reshape(slot_total, tok_dev, model_width)
    pairs_own = jnp.concatenate([keys_own, values_own], axis=2)
    pairs_all = jnp.moveaxis(gather_tree(pairs_own, ("seq",)), 0, 1)
    pairs_all = pairs_all.reshape(slot_total, -1, 2 * model_width)
    keys_all, values_all = pairs_all[:, :, :model_width], pairs_all[:, :, model_width:]
    keys_heads = keys_all.reshape(slot_total, -1, H, HD)
    values_heads = values_all.reshape(slot_total, -1, H, HD)
    scores = (
        jnp.einsum("sqhd,skhd->shqk", queries, keys_heads, preferred_element_type=jnp.float32)
        * scale
    )
    row_max = jnp.max(scores, axis=-1, keepdims=True)
    row_total = jnp.sum(jnp.exp(scores - row_max), axis=-1, keepdims=True)
    attn_probs = jnp.exp(scores - row_max) / row_total
    probs_b = attn_probs.astype(jnp.bfloat16)
    attended = jnp.einsum(
        "shqk,skhd->sqhd", probs_b, values_heads, preferred_element_type=jnp.float32
    )
    attended_b = attended.reshape(row_count, model_width).astype(jnp.bfloat16)
    branch_att = (
        jnp.dot(attended_b, mat_out, preferred_element_type=jnp.float32) + vec_out
    ).reshape(slot_total, tok_dev, model_width)
    middle = latents + gate_att * branch_att
    normed_mlp, spread_mlp = normalize(middle)
    mlp_in = (
        (normed_mlp * (1.0 + scale_mlp) + shift_mlp)
        .astype(jnp.bfloat16)
        .reshape(row_count, model_width)
    )
    mlp_all = all_tokens(mlp_in)
    hidden = jnp.dot(mlp_all, mat_up, preferred_element_type=jnp.float32) + rounded(up_bias)
    activated = gelu_tanh(hidden).astype(jnp.bfloat16)
    activated, mat_down = lax.optimization_barrier((activated, mat_down))
    branch_mlp = (
        own_tokens(jnp.dot(activated, mat_down, preferred_element_type=jnp.float32)) + vec_down
    ).reshape(slot_total, tok_dev, model_width)
    block_output = jnp.where(live_mask, middle + gate_mlp * branch_mlp, 0.0)
    back_down = upstream * gate_mlp
    back_down_b = back_down.astype(jnp.bfloat16).reshape(row_count, model_width)
    back_down_all = all_tokens(back_down_b)
    down_sums = lax.psum_scatter(
        weight_term(activated, back_down_all), "dp", scatter_dimension=0, tiled=True
    )
    grad_downw = rows_to_owners(down_sums).astype(jnp.float32)
    sum_downb = jnp.sum(back_down, axis=(0, 1))
    back_hidden = jnp.einsum(
        "rd,fd->rf", back_down_all, mat_down, preferred_element_type=jnp.float32
    ) * gelu_slope(hidden)
    back_hidden_b = back_hidden.astype(jnp.bfloat16)
    grad_upw = lax.psum_scatter(
        weight_term(mlp_all, back_hidden_b), "dp", scatter_dimension=0, tiled=True
    ).astype(jnp.float32)
    up_total = jnp.zeros((lax.axis_size("seq") * up_bias.shape[0],), jnp.float32)
    sum_upb = lax.dynamic_update_slice_in_dim(
        up_total, jnp.sum(back_hidden, axis=0), lax.axis_index("seq") * up_bias.shape[0], 0
    )
    back_mlp_in = own_tokens(
        jnp.einsum("rf,cf->rc", back_hidden_b, mat_up, preferred_element_type=jnp.float32)
    ).reshape(slot_total, tok_dev, model_width)
    back_middle = upstream + norm_back(back_mlp_in * (1.0 + scale_mlp), normed_mlp, spread_mlp)
    back_att = back_middle * gate_att
    back_att_b = back_att.astype(jnp.bfloat16).reshape(row_count, model_width)
    term_out = weight_term(attended_b, back_att_b)
    sum_outb = jnp.sum(back_att, axis=(0, 1))
    back_attended = jnp.einsum(
        "rd,cd->rc", back_att_b, mat_out, preferred_element_type=jnp.float32
    ).astype(jnp.bfloat16)
    back_attended = back_attended.reshape(slot_total, tok_dev, H, HD)
    back_probs = jnp.einsum(
        "sqhd,skhd->shqk", back_attended, values_heads, preferred_element_type=jnp.float32
    )
    row_delta = jnp.einsum("sqhd,sqhd->shq", back_attended.astype(jnp.float32), attended)[..., None]
    back_scores = (attn_probs * (back_probs - row_delta) * scale).astype(jnp.bfloat16)
    back_queries = jnp.einsum(
        "shqk,skhd->sqhd", back_scores, keys_heads, preferred_element_type=jnp.float32
    )
    key_terms = jnp.einsum(
        "shqk,sqhd->skhd", back_scores, queries, preferred_element_type=jnp.float32
    ).reshape(slot_total, -1, model_width)
    value_terms = jnp.einsum(
        "shqk,sqhd->skhd", probs_b, back_attended, preferred_element_type=jnp.float32
    ).reshape(slot_total, -1, model_width)
    pair_terms = jnp.concatenate([key_terms, value_terms], axis=2)
    pair_terms = pair_terms.reshape(slot_total, -1, tok_dev, 2 * model_width)
    back_pairs = scatter_tree(jnp.moveaxis(pair_terms, 1, 0), ("seq",), jnp.bfloat16)
    back_keys, back_values = back_pairs[:, :, :model_width], back_pairs[:, :, model_width:]
    back_qkv = jnp.concatenate(
        [
            back_queries.reshape(row_count, model_width),
            back_keys.reshape(row_count, model_width),
            back_values.reshape(row_count, model_width),
        ],
        axis=1,
    )
    back_qkv_b = back_qkv.astype(jnp.bfloat16)
    term_qkv = weight_term(attn_in, back_qkv_b)
    grad_qkvw, grad_outw = spread_terms([term_qkv, term_out])
    sum_qkvb = jnp.sum(back_qkv, axis=0)
    back_attn_in = jnp.einsum(
        "rd,cd->rc", back_qkv_b, mat_qkv, preferred_element_type=jnp.float32
    ).reshape(slot_total, tok_dev, model_width)
    latent_gradient = jnp.where(
        live_mask,
        back_middle + norm_back(back_attn_in * (1.0 + scale_att), normed_att, spread_att),
        0.0,
    )
    slot_modgrad = jnp.concatenate(
        [
            jnp.sum(back_attn_in, axis=1),
            jnp.sum(back_attn_in * normed_att, axis=1),
            jnp.sum(back_middle * branch_att, axis=1),
            jnp.sum(back_mlp_in, axis=1),
            jnp.sum(back_mlp_in * normed_mlp, axis=1),
            jnp.sum(upstream * branch_mlp, axis=1),
        ],
        axis=1,
    )
    modgrad_table = jnp.dot(slot_matches.T, slot_modgrad, precision=lax.Precision.HIGHEST)
    modgrad_cols = scatter_tree(
        jnp.moveaxis(modgrad_table.reshape(latent_count, -1, ada_bias.shape[0]), 1, 0),
        ("dp", "seq"),
    )
    grad_adaw = jnp.dot(
        rounded(jax.nn.silu(condition)).T, modgrad_cols, precision=lax.Precision.HIGHEST
    )
    grad_adab = jnp.sum(modgrad_cols, axis=0)
    cond_term = jnp.dot(modgrad_cols, rounded(ada_weight).T, precision=lax.Precision.HIGHEST)
    cond_sum = sum_tree(cond_term, ("dp", "seq"))
    bias_sums = (sum_qkvb, sum_outb, sum_upb, sum_downb)
    totals, start, bias_totals = sum_tree(jnp.concatenate(bias_sums), ("dp", "seq")), 0, []
    for item in bias_sums:
        bias_totals.append(totals[start : start + item.shape[0]])
        start += item.shape[0]
    total_qkvb, total_outb, total_upb, total_downb = bias_totals
    condition_grad = cond_sum * silu_slope(condition)
    seq_index = lax.axis_index("seq")

    def own_part(full_sum, local_bias):
        length = local_bias.shape[0]
        return lax.dynamic_slice_in_dim(full_sum, seq_index * length, length)

    grad_qkvb = own_part(total_qkvb, qkv_bias)
    grad_outb = own_part(total_outb, out_bias)
    grad_upb = own_part(total_upb, up_bias)
    grad_downb = own_part(total_downb, down_bias)
    grads_all = (
        grad_adaw,
        grad_adab,
        grad_qkvw,
        grad_qkvb,
        grad_outw,
        grad_outb,
        grad_upw,
        grad_upb,
        grad_downw,
        grad_downb,
    )
    params_all = (
        ada_weight,
        ada_bias,
        qkv_weight,
        qkv_bias,
        out_weight,
        out_bias,
        up_weight,
        up_bias,
        down_weight,
        down_bias,
    )
    means_all = (
        mean_adaw,
        mean_adab,
        mean_qkvw,
        mean_qkvb,
        mean_outw,
        mean_outb,
        mean_upw,
        mean_upb,
        mean_downw,
        mean_downb,
    )
    squares_all = (
        sqmean_adaw,
        sqmean_adab,
        sqmean_qkvw,
        sqmean_qkvb,
        sqmean_outw,
        sqmean_outb,
        sqmean_upw,
        sqmean_upb,
        sqmean_downw,
        sqmean_downb,
    )
    updates = [
        adamw_step(p_item, g_item, m_item, v_item)
        for p_item, g_item, m_item, v_item in zip(params_all, grads_all, means_all, squares_all)
    ]
    newvals = tuple((entry[0] for entry in updates))
    newmeans = tuple((entry[1] for entry in updates))
    newsqrs = tuple((entry[2] for entry in updates))
    return (
        (block_output, latent_gradient, condition_grad) + grads_all + newvals + newmeans + newsqrs
    )


MESH_ID = pl.DeviceIdType.MESH
ANY = pl.BlockSpec(memory_space=pl.ANY)
VMEM = pl.BlockSpec(memory_space=pltpu.VMEM)


def params_of(number):
    return pltpu.CompilerParams(
        collective_id=number, has_side_effects=True, vmem_limit_bytes=56 * 2**20
    )


def place():
    group, x = lax.axis_index("dp"), lax.axis_index("seq")
    core, chip = group % 2, group // 2
    return chip // 2, chip % 2, core, x


def device(a, b, core, x):
    return ((a * 2 + b) * 2 + core, x)


def remote(src, dst, send, recv, target):
    return pltpu.make_async_remote_copy(
        src_ref=src,
        dst_ref=dst,
        send_sem=send,
        recv_sem=recv,
        device_id=target,
        device_id_type=MESH_ID,
    )


def greet(targets, present):
    barrier = pltpu.get_barrier_semaphore()
    amount = 0
    for target, there in zip(targets, present):

        def signal():
            pl.semaphore_signal(barrier, inc=1, device_id=target, device_id_type=MESH_ID)

        if there is True:
            signal()
            amount = amount + 1
        else:
            pl.when(there)(signal)
            amount = amount + there.astype(jnp.int32)
    pl.semaphore_wait(barrier, amount)


def greet_near(lines, grid, four):
    a, b, core, x = place()
    targets, present = [], []
    if grid:
        targets += [device(a, 1 - b, core, x), device(a - 1, b, core, x), device(a + 1, b, core, x)]
        present += [True, a > 0, a < lines - 1]
    if four:
        targets += [device(a, b, 1 - core, x), device(a, b, core, 1 - x)]
        present += [True, True]
    greet(targets, present)


class Part:
    def __init__(self, make, ins, in_specs, outs, out_specs, scratch):
        self.make, self.ins, self.in_specs = make, ins, in_specs
        self.outs, self.out_specs, self.scratch = outs, out_specs, scratch


def joint_kernel(parts, plan, lines, grid, four, *refs):
    ins = [len(part.ins) for part in parts]
    outs = [len(part.outs) for part in parts]
    at_in, at_out = 0, sum(ins)
    at_scratch = at_out + sum(outs)
    if four is None:
        greet_all()
    else:
        greet_near(lines, grid, four)
    stages = []
    for part, n_in, n_out in zip(parts, ins, outs):
        n_scratch = len(part.scratch)
        stages.append(
            part.make(
                refs[at_in : at_in + n_in],
                refs[at_out : at_out + n_out],
                refs[at_scratch : at_scratch + n_scratch],
            )
        )
        at_in, at_out, at_scratch = at_in + n_in, at_out + n_out, at_scratch + n_scratch
    for index, stage in plan:
        stages[index][stage]()


def run_parts(parts, plan, number, grid, four):
    lines = lax.axis_size("dp") // 4
    flat = pl.pallas_call(
        functools.partial(joint_kernel, parts, plan, lines, grid, four),
        out_shape=sum((part.outs for part in parts), []),
        in_specs=sum((part.in_specs for part in parts), []),
        out_specs=sum((part.out_specs for part in parts), []),
        scratch_shapes=sum((part.scratch for part in parts), []),
        compiler_params=params_of(number),
        name="joint",
    )(*sum((part.ins for part in parts), []))
    results, start = [], 0
    for part in parts:
        results.append(flat[start : start + len(part.outs)])
        start += len(part.outs)
    return results


def strips(rows):
    return [(i, 48) for i in range(0, rows, 48)] if rows % 48 == 0 else [(0, rows)]


def view(ref, rows, part, lead):
    if part == (0, rows):
        return ref
    cut_rows = pl.ds(*part)
    return ref.at[:, cut_rows, :] if lead else ref.at[cut_rows, :]


def views(refs, rows, lead):
    return [
        view(ref, size, part, lead) for ref, size in zip(refs, rows) for part in strips(size)
    ]


def grid_gather(pieces):
    lines = lax.axis_size("dp") // 4
    rows = [piece.shape[0] for piece in pieces]
    count, whole = sum(len(strips(size)) for size in rows), len(pieces)

    def make(ins, outs, scratch):
        ins, outs = views(ins, rows, False), views(outs, rows, True)
        keep, up_send, down_send, side_send, line_recv, side_recv = scratch
        a, b, core, x = place()
        own = a * 2 + b
        copies = [
            pltpu.make_async_copy(ins[p], outs[p].at[own], keep.at[p]) for p in range(count)
        ]

        def up(p, s, src):
            return remote(
                src, outs[p].at[s * 2 + b], up_send.at[p, s], line_recv.at[p, s],
                device(a + 1, b, core, x),
            )

        def down(p, s, src):
            return remote(
                src, outs[p].at[s * 2 + b], down_send.at[p, s], line_recv.at[p, s],
                device(a - 1, b, core, x),
            )

        def side(p, s, src):
            return remote(
                src, outs[p].at[s * 2 + b], side_send.at[p, s], side_recv.at[p, s],
                device(a, 1 - b, core, x),
            )

        def arrived(p, s):
            block = outs[p].at[s * 2 + b]
            remote(
                block, block, up_send.at[p, s], line_recv.at[p, s], device(a, 1 - b, core, x)
            ).wait_recv()
            return block

        def start():
            for p in range(count):
                pl.when(a < lines - 1)(lambda: up(p, a, ins[p]).start())
                pl.when(a > 0)(lambda: down(p, a, ins[p]).start())
                side(p, a, ins[p]).start()
                copies[p].start()

        def hop_of(hop):
            def run():
                for p in range(count):

                    def from_below():
                        block = arrived(p, a - hop)
                        pl.when(a < lines - 1)(lambda: up(p, a - hop, block).start())
                        side(p, a - hop, block).start()

                    def from_above():
                        block = arrived(p, a + hop)
                        pl.when(a > 0)(lambda: down(p, a + hop, block).start())
                        side(p, a + hop, block).start()

                    pl.when(a - hop >= 0)(from_below)
                    pl.when(a + hop < lines)(from_above)

            return run

        def got(p):
            copies[p].wait()
            for s in range(lines):
                block = outs[p].at[s * 2 + 1 - b]
                remote(
                    block, block, side_send.at[p, s], side_recv.at[p, s],
                    device(a, 1 - b, core, x),
                ).wait_recv()

        def sent(p):
            for s in range(lines):
                block = outs[p].at[s * 2 + b]
                side(p, s, block).wait_send()
                pl.when((s <= a) & (a < lines - 1))(lambda: up(p, s, block).wait_send())
                pl.when((s >= a) & (a > 0))(lambda: down(p, s, block).wait_send())

        def hops():
            for hop in range(1, lines):
                hop_of(hop)()

        def end():
            for p in range(count):
                got(p)
                sent(p)

        def early():
            got(0)

        def late():
            for p in range(1, count):
                got(p)
            for p in range(count):
                sent(p)

        return dict(start=start, hops=hops, end=end, early=early, late=late, hop=hop_of(1),
                    more=lambda: [hop_of(hop)() for hop in range(2, lines)])

    dma = pltpu.SemaphoreType.DMA
    return Part(
        make,
        list(pieces),
        [ANY] * whole,
        [jax.ShapeDtypeStruct((2 * lines,) + piece.shape, piece.dtype) for piece in pieces],
        [ANY] * whole,
        [dma((count,))] + [dma((count, lines))] * 5,
    )


AHEAD = 4


def grid_reduce(pieces):
    lines = lax.axis_size("dp") // 4
    rows = [piece.shape[1] for piece in pieces]
    count, whole = sum(len(strips(size)) for size in rows), len(pieces)

    def make(ins, outs, scratch):
        held, lower, upper = (
            views(scratch[i * whole : (i + 1) * whole], rows, True) for i in range(3)
        )
        up_send, down_send, side_send, up_recv, down_recv, side_recv = scratch[3 * whole :]
        ins, outs = views(ins, rows, True), views(outs, rows, False)
        a, b, core, x = place()

        def side(p, t):
            return remote(
                ins[p].at[t * 2 + 1 - b], held[p].at[t], side_send.at[p, t], side_recv.at[p, t],
                device(a, 1 - b, core, x),
            )

        def up(p, t):
            return remote(
                held[p].at[t], lower[p].at[t], up_send.at[p, t], up_recv.at[p, t],
                device(a + 1, b, core, x),
            )

        def down(p, t):
            return remote(
                held[p].at[t], upper[p].at[t], down_send.at[p, t], down_recv.at[p, t],
                device(a - 1, b, core, x),
            )

        def sum_into(p, t, target, others):
            total = ins[p][t * 2 + b].astype(jnp.float32)
            for other in others:
                total = total + other[...].astype(jnp.float32)
            target[...] = total.astype(target.dtype)

        half = lines // 2
        order = list(range(lines - 1, half - 1, -1)) + list(range(half))

        def turn(k):
            p, t = k % count, order[k // count]
            return p, jnp.where(a < half, t, lines - 1 - t)

        def start():
            for k in range(AHEAD):
                side(*turn(k)).start()

        def step(k):
            p, t = turn(k)
            side(p, t).wait_recv()
            mine = held[p].at[t]

            def upward():
                def joined():
                    up(p, t).wait_recv()
                    sum_into(p, t, mine, [mine, lower[p].at[t]])

                pl.when(a > 0)(joined)
                pl.when(a == 0)(lambda: sum_into(p, t, mine, [mine]))
                up(p, t).start()

            def downward():
                def joined():
                    down(p, t).wait_recv()
                    sum_into(p, t, mine, [mine, upper[p].at[t]])

                pl.when(a < lines - 1)(joined)
                pl.when(a == lines - 1)(lambda: sum_into(p, t, mine, [mine]))
                down(p, t).start()

            pl.when(a < t)(upward)
            pl.when(a > t)(downward)
            if k + AHEAD < count * lines:
                side(*turn(k + AHEAD)).start()

        def steps():
            for k in range(count * lines):
                step(k)

        def first():
            for k in range(count):
                step(k)

        def second():
            for k in range(count, 2 * count):
                step(k)

        def others():
            for k in range(2 * count, count * lines):
                step(k)

        def end():
            for p in range(count):
                terms = held[p].at[a], lower[p].at[a], upper[p].at[a]
                pl.when(a > 0)(lambda: up(p, a).wait_recv())
                pl.when(a < lines - 1)(lambda: down(p, a).wait_recv())
                pl.when(a == 0)(lambda: sum_into(p, a, outs[p], [terms[0], terms[2]]))
                pl.when(a == lines - 1)(lambda: sum_into(p, a, outs[p], [terms[0], terms[1]]))
                pl.when((a > 0) & (a < lines - 1))(lambda: sum_into(p, a, outs[p], terms))
            for p in range(count):
                for t in range(lines):
                    side(p, t).wait_send()
                    pl.when(a < t)(lambda: up(p, t).wait_send())
                    pl.when(a > t)(lambda: down(p, t).wait_send())

        return dict(
            start=start, steps=steps, first=first, second=second, others=others, end=end
        )

    dma = pltpu.SemaphoreType.DMA
    slots = [pltpu.VMEM((lines,) + piece.shape[1:], piece.dtype) for piece in pieces]
    return Part(
        make,
        list(pieces),
        [VMEM] * whole,
        [jax.ShapeDtypeStruct(piece.shape[1:], piece.dtype) for piece in pieces],
        [VMEM] * whole,
        slots * 3 + [dma((count, lines))] * 6,
    )


def four_stages(ins, outs, scratch):
    count = len(outs)
    keep, sib_send, x_send, fwd_send, sib_recv, x_recv, fwd_recv = scratch
    a, b, core, x = place()
    own, across = core * 2 + x, core * 2 + 1 - x
    sibling, peer = device(a, b, 1 - core, x), device(a, b, core, 1 - x)
    to_x, to_sib, to_fwd, copies = [], [], [], []
    for p in range(count):
        block, far = outs[p].at[own], outs[p].at[across]
        to_x.append(remote(ins[p], block, x_send.at[p], x_recv.at[p], peer))
        to_sib.append(remote(ins[p], block, sib_send.at[p], sib_recv.at[p], sibling))
        to_fwd.append(remote(far, far, fwd_send.at[p], fwd_recv.at[p], sibling))
        copies.append(pltpu.make_async_copy(ins[p], block, keep.at[p]))

    def start():
        for p in range(count):
            to_x[p].start()
            to_sib[p].start()
            copies[p].start()

    def middle():
        for p in range(count):
            to_x[p].wait_recv()
            to_fwd[p].start()

    def end():
        for p in range(count):
            to_sib[p].wait_recv()
            to_fwd[p].wait_recv()
            copies[p].wait()
            to_x[p].wait_send()
            to_sib[p].wait_send()
            to_fwd[p].wait_send()

    return dict(start=start, middle=middle, end=end)


def four_gather(pieces):
    count = len(pieces)
    return Part(
        four_stages,
        list(pieces),
        [VMEM] * count,
        [jax.ShapeDtypeStruct((4,) + piece.shape, piece.dtype) for piece in pieces],
        [VMEM] * count,
        [pltpu.SemaphoreType.DMA((count,))] * 7,
    )


def grid_four_gather(pieces):
    base = grid_gather(pieces)
    base_outs = len(base.outs)

    def make(ins, outs, scratch):
        stages = base.make(ins, outs[:base_outs], scratch[: len(base.scratch)])
        four = four_stages([outs[0]], outs[base_outs:], scratch[len(base.scratch) :])
        for name, stage in four.items():
            stages["four_" + name] = stage
        return stages

    first = base.outs[0]
    return Part(
        make,
        base.ins,
        base.in_specs,
        base.outs + [jax.ShapeDtypeStruct((4,) + first.shape, first.dtype)],
        base.out_specs + [ANY],
        base.scratch + [pltpu.SemaphoreType.DMA((1,))] * 7,
    )


def four_reduce(pieces):
    count = len(pieces)

    def make(ins, outs, scratch):
        near, out_x, in_x = (scratch[i * count : (i + 1) * count] for i in range(3))
        sib_send, sib_recv, x_send, x_recv = scratch[3 * count :]
        a, b, core, x = place()
        own, across = core * 2 + x, core * 2 + 1 - x
        sibling, peer = device(a, b, 1 - core, x), device(a, b, core, 1 - x)
        to_sib, to_x = [], []
        for p in range(count):
            to_sib.append(
                [
                    remote(
                        ins[p].at[(1 - core) * 2 + side], near[p].at[i], sib_send.at[p, i],
                        sib_recv.at[p, i], sibling,
                    )
                    for i, side in enumerate((1 - x, x))
                ]
            )
            to_x.append(remote(out_x[p], in_x[p], x_send.at[p], x_recv.at[p], peer))

        def start():
            for i in range(2):
                for p in range(count):
                    to_sib[p][i].start()

        def middle():
            for p in range(count):
                to_sib[p][0].wait_recv()
                out_x[p][...] = (ins[p][across] + near[p][0]).astype(out_x[p].dtype)
                to_x[p].start()

        def own_sums():
            for p in range(count):
                to_sib[p][1].wait_recv()
                outs[p][...] = ins[p][own] + near[p][1]

        def end():
            for p in range(count):
                to_x[p].wait_recv()
                outs[p][...] += in_x[p][...].astype(jnp.float32)
                to_x[p].wait_send()
                for i in range(2):
                    to_sib[p][i].wait_send()

        return dict(start=start, middle=middle, own=own_sums, end=end)

    dma = pltpu.SemaphoreType.DMA
    shapes = [piece.shape[1:] for piece in pieces]
    return Part(
        make,
        list(pieces),
        [VMEM] * count,
        [jax.ShapeDtypeStruct(shape, jnp.float32) for shape in shapes],
        [VMEM] * count,
        [pltpu.VMEM((2,) + shape, jnp.float32) for shape in shapes]
        + [pltpu.VMEM(shape, jnp.bfloat16) for shape in shapes] * 2
        + [dma((count, 2))] * 2
        + [dma((count,))] * 2,
    )


GATHER_PLAN = [
    (0, "start"), (1, "start"), (0, "hop"), (1, "middle"), (0, "more"), (1, "end"), (0, "end"),
]
GATHER_REDUCE_PLAN = [
    (0, "start"), (1, "start"), (0, "hop"), (1, "middle"), (0, "more"), (1, "own"), (1, "end"),
    (0, "end"),
]
REDUCE_REDUCE_PLAN = [
    (1, "start"), (0, "start"), (0, "first"), (1, "middle"), (0, "second"), (1, "own"),
    (0, "others"), (1, "end"), (0, "end"),
]
REDUCE_GATHER_PLAN = [
    (1, "start"), (0, "start"), (0, "first"), (1, "middle"), (0, "second"), (0, "others"),
    (1, "end"), (0, "end"),
]


def total_devices():
    return lax.axis_size("dp") * lax.axis_size("seq")


def own_index():
    return lax.axis_index("dp") * lax.axis_size("seq") + lax.axis_index("seq")


def device_at(index):
    ways = lax.axis_size("seq")
    return (index // ways, index % ways)


def greet_all():
    devices, me = total_devices(), own_index()
    barrier = pltpu.get_barrier_semaphore()

    def signal(i, carry):
        target = device_at((me + i) % devices)
        pl.semaphore_signal(barrier, inc=1, device_id=target, device_id_type=MESH_ID)
        return carry

    lax.fori_loop(1, devices, signal, 0)
    pl.semaphore_wait(barrier, devices - 1)


def spread_all(blocks, landed, source, send, recv):
    devices, me = total_devices(), own_index()

    def post(i, carry):
        to = (me + i) % devices
        remote(source(to), landed.at[me], send, recv, device_at(to)).start()
        return carry

    lax.fori_loop(1, devices, post, 0)


def settle_all(landed, spare, send, recv):
    count = total_devices() - 1
    both = remote(
        landed.at[pl.ds(0, count)], spare.at[pl.ds(0, count)], send, recv,
        device_at((own_index() + 1) % total_devices()),
    )
    both.wait_recv()
    both.wait_send()


def closing(blocks, bias_tiles, weight):
    devices, rows, width = blocks.shape
    model_width = weight.shape[0]
    tiles = model_width // 128
    sums_shape = (devices, rows, 128)

    def make(ins, outs, scratch):
        blocks, bias_tiles, weight = ins
        columns, sums = outs
        landed, terms, landed_terms, part, *sems = scratch
        me = own_index()

        def start():
            spread_all(blocks, landed, lambda to: blocks.at[to], sems[0], sems[1])
            landed[me] = blocks[me]

        def middle():
            settle_all(landed, landed, sems[0], sems[1])
            total = jnp.sum(landed[...], axis=0)
            columns[...] = total
            cond = lax.dot_general(
                total, weight[...], (((1,), (1,)), ((), ())),
                precision=lax.Precision.HIGHEST, preferred_element_type=jnp.float32,
            )
            for i in range(tiles):
                terms[i] = cond[:, i * 128 : (i + 1) * 128]
            terms[pl.ds(tiles, devices - tiles)] = bias_tiles[...]
            spread_all(terms, landed_terms, lambda to: terms.at[to], sems[2], sems[3])
            landed_terms[me] = terms[me]

        def late():
            settle_all(landed_terms, landed_terms, sems[2], sems[3])
            total = jnp.sum(landed_terms[...], axis=0)
            part[...] = total
            spread_all(part, sums, lambda to: part, sems[4], sems[5])
            sums[me] = total

        def end():
            settle_all(sums, sums, sems[4], sems[5])

        return dict(start=start, middle=middle, late=late, end=end)

    return Part(
        make,
        [blocks, bias_tiles, weight],
        [VMEM] * 3,
        [
            jax.ShapeDtypeStruct((rows, width), jnp.float32),
            jax.ShapeDtypeStruct(sums_shape, jnp.float32),
        ],
        [VMEM] * 2,
        [
            pltpu.VMEM(blocks.shape, jnp.float32),
            pltpu.VMEM(sums_shape, jnp.float32),
            pltpu.VMEM(sums_shape, jnp.float32),
            pltpu.VMEM((rows, 128), jnp.float32),
        ]
        + [pltpu.SemaphoreType.DMA(())] * 6,
    )


CLOSING_PLAN = [
    (1, "start"), (0, "start"), (0, "first"), (1, "middle"), (0, "second"), (1, "late"),
    (0, "others"), (1, "end"), (0, "end"),
]


def pad_to(values, axis, size):
    pads = [(0, 0)] * values.ndim
    pads[axis] = (0, size - values.shape[axis])
    return jnp.pad(values, pads)


def swap_core(values):
    return lax.ppermute(values, "dp", [(i, i ^ 1) for i in range(lax.axis_size("dp"))])


def swap_x(values):
    return lax.ppermute(values, "seq", [(0, 1), (1, 0)])


def row_moves(turn):
    groups = lax.axis_size("dp")
    chips, pairs = groups // 2, []
    for d in range(groups):
        for x in range(2):
            block = d * 2 + (turn + x) % 2
            f, c = block // chips, block % chips
            pairs.append((d * 2 + x, (c * 2 + f % 2) * 2 + f // 2))
    return pairs


def flip(pair, swapped):
    low = jnp.where(swapped, pair[1], pair[0])
    high = jnp.where(swapped, pair[0], pair[1])
    return low, high


def rows_to_blocks(pieces):
    x = lax.axis_index("seq")
    b = (lax.axis_index("dp") // 2) % 2
    sent = flip(pieces, x == 1)
    got = [lax.ppermute(sent[turn], ("dp", "seq"), row_moves(turn)) for turn in range(2)]
    return jnp.concatenate(flip(got, b == 1), axis=1)


def blocks_to_rows(block):
    x = lax.axis_index("seq")
    b = (lax.axis_index("dp") // 2) % 2
    half = block.shape[1] // 2
    sent = flip((block[:, :half], block[:, half:]), b == 1)
    got = [
        lax.ppermute(sent[turn], ("dp", "seq"), [(q, p) for p, q in row_moves(turn)])
        for turn in range(2)
    ]
    return flip(got, x == 1)


def cut(values, index, size, axis=1):
    return lax.dynamic_slice_in_dim(values, index * size, size, axis)


def swap_both(values):
    groups = lax.axis_size("dp")
    pairs = [(d * 2 + x, (d ^ 1) * 2 + 1 - x) for d in range(groups) for x in range(2)]
    return lax.ppermute(values, ("dp", "seq"), pairs)


def by_core(high, own, far):
    return jnp.where(high, far, own), jnp.where(high, own, far)


def gather_columns(qkv_block, up_block):
    x, core = lax.axis_index("seq"), lax.axis_index("dp") % 2
    width, half = qkv_block.shape[1] // 6, up_block.shape[1] // 2
    first, high = x == 0, core == 1

    def pair(k):
        return jnp.concatenate(
            [
                qkv_block[:, k * width : (k + 1) * width],
                qkv_block[:, (4 + k) * width : (5 + k) * width],
            ],
            axis=1,
        )

    def across(k):
        return qkv_block[:, (2 + k) * width : (3 + k) * width]

    pairs = by_core(high, pair(0), pair(1))
    crosses = by_core(high, across(0), across(1))
    ups = by_core(high, up_block[:, :half], up_block[:, half:])
    cross_x = swap_x(crosses[0])
    cross_both = swap_both(crosses[1])
    pair_far = swap_core(pairs[1])
    up_far = swap_core(ups[1])
    pair_rows = jnp.concatenate(by_core(high, pairs[0], pair_far), axis=0)
    cross_rows = jnp.concatenate(by_core(high, cross_x, cross_both), axis=0)
    up_rows = jnp.concatenate(by_core(high, ups[0], up_far), axis=0)
    full = jnp.where(
        first,
        jnp.concatenate([pair_rows, cross_rows], axis=1),
        jnp.concatenate([cross_rows, pair_rows], axis=1),
    )
    return full, up_rows


def scatter_qkv(qkv_block):
    x, core = lax.axis_index("seq"), lax.axis_index("dp") % 2
    width, rows = qkv_block.shape[1] // 3, qkv_block.shape[0] // 2
    first, high = x == 0, core == 1
    pair = jnp.where(first, qkv_block[:, : 2 * width], qkv_block[:, width:])
    across = jnp.where(first, qkv_block[:, 2 * width :], qkv_block[:, :width])
    pairs = by_core(high, pair[:rows], pair[rows:])
    crosses = by_core(high, across[:rows], across[rows:])
    got_pairs = by_core(high, pairs[0], swap_core(pairs[1]))
    got_cross = by_core(high, swap_x(crosses[0]), swap_both(crosses[1]))
    return jnp.concatenate(
        [item[:, :width] for item in got_pairs]
        + list(got_cross)
        + [item[:, width:] for item in got_pairs],
        axis=1,
    )


def scatter_up(up_block):
    high = lax.axis_index("dp") % 2 == 1
    rows = up_block.shape[0] // 2
    ups = by_core(high, up_block[:rows], up_block[rows:])
    return jnp.concatenate(by_core(high, ups[0], swap_core(ups[1])), axis=1)


def on_device_grid(
    latents,
    condition,
    slot_latent,
    slot_counts,
    output_gradient,
    ada_weight,
    ada_bias,
    qkv_weight,
    qkv_bias,
    out_weight,
    out_bias,
    up_weight,
    up_bias,
    down_weight,
    down_bias,
    mean_adaw,
    mean_adab,
    mean_qkvw,
    mean_qkvb,
    mean_outw,
    mean_outb,
    mean_upw,
    mean_upb,
    mean_downw,
    mean_downb,
    sqmean_adaw,
    sqmean_adab,
    sqmean_qkvw,
    sqmean_qkvb,
    sqmean_outw,
    sqmean_outb,
    sqmean_upw,
    sqmean_upb,
    sqmean_downw,
    sqmean_downb,
):
    slot_total, tok_dev, model_width = latents.shape
    scale = HD ** (-0.5)
    latent_count = condition.shape[0]
    x_index, group = lax.axis_index("seq"), lax.axis_index("dp")
    core = group % 2
    share = 2 * x_index + core
    live = slot_counts[0] > 0
    slot_match = ((slot_latent[0, 0] == jnp.arange(latent_count)) & live).astype(jnp.float32)
    bf16 = jnp.bfloat16

    silu_cond = jax.nn.silu(condition).astype(bf16)
    mod_cols = jnp.dot(
        silu_cond, ada_weight.astype(bf16), preferred_element_type=jnp.float32
    ) + rounded(ada_bias)

    qkv_block, up_block = gather_columns(qkv_weight.astype(bf16), up_weight.astype(bf16))
    hidden_rows = down_weight.shape[0] // 2
    out_rows = out_weight.shape[0] // 2
    down_b, out_b = down_weight.astype(bf16), out_weight.astype(bf16)
    rows_block = rows_to_blocks(
        [
            jnp.concatenate(
                [cut(down_b, i, hidden_rows, 0), cut(out_b, i, out_rows, 0)], axis=0
            )
            for i in range(2)
        ]
    )
    down_block, out_block = rows_block[:hidden_rows], rows_block[hidden_rows:]
    grid_plan = [
        (0, stage)
        for stage in (
            "start", "hops", "early", "four_start", "four_middle", "four_end", "late",
        )
    ]
    ((_, qkv_grid, out_grid, mod_four),) = run_parts(
        [grid_four_gather([mod_cols, qkv_block, out_block])], grid_plan, 1, True, True
    )
    mat_qkv = qkv_grid.reshape(model_width, -1)
    mat_out = out_grid.reshape(-1, model_width)
    width = mat_out.shape[0]
    hidden_width = up_block.shape[1]
    heads = width // HD

    slot_mod = jnp.einsum("jcln,l->cjn", mod_four, slot_match, precision=lax.Precision.HIGHEST)
    slot_mod = slot_mod.reshape(6, 1, model_width)
    shift_att, scale_att, gate_att, shift_mlp, scale_mlp, gate_mlp = (
        slot_mod[i] for i in range(6)
    )

    biases = (qkv_bias, out_bias, down_bias)
    bias_own = jnp.concatenate(biases).astype(bf16)[None]
    bias_other = swap_x(bias_own)
    bias_pair = flip((bias_own, bias_other), x_index == 1)
    starts = [0]
    for item in biases:
        starts.append(starts[-1] + item.shape[0])
    vec_qkv, vec_out, vec_down = (
        jnp.concatenate(
            [half[0, starts[i] : starts[i + 1]] for half in bias_pair]
        ).astype(jnp.float32)
        for i in range(3)
    )
    vec_qkv = cut(vec_qkv.reshape(3, -1), share, width).reshape(-1)
    vec_up = cut(rounded(up_bias), core, hidden_width, 0)

    tokens = latents[0]
    upstream = jnp.where(live, output_gradient[0], 0.0)
    normed_att, spread_att = normalize(tokens)
    attn_own = (normed_att * (1.0 + scale_att) + shift_att).astype(bf16)
    back_down = upstream * gate_mlp
    (up_grid,), four_pair = run_parts(
        [grid_gather([up_block]), four_gather([attn_own, back_down.astype(bf16)])],
        GATHER_PLAN, 2, True, True,
    )
    attn_in, back_down_all = (item.reshape(-1, model_width) for item in four_pair)
    mat_up = up_grid.reshape(model_width, -1)
    qkv_all = (jnp.dot(attn_in, mat_qkv, preferred_element_type=jnp.float32) + vec_qkv).astype(bf16)
    split = (2, -1, heads, HD)
    queries = qkv_all[:, :width].reshape(split)
    keys_heads = qkv_all[:, width : 2 * width].reshape(split)
    values_heads = qkv_all[:, 2 * width :].reshape(split)
    scores = (
        jnp.einsum("sqhd,skhd->shqk", queries, keys_heads, preferred_element_type=jnp.float32)
        * scale
    )
    row_max = jnp.max(scores, axis=-1, keepdims=True)
    row_total = jnp.sum(jnp.exp(scores - row_max), axis=-1, keepdims=True)
    attn_probs = jnp.exp(scores - row_max) / row_total
    probs_b = attn_probs.astype(bf16)
    attended = jnp.einsum(
        "shqk,skhd->sqhd", probs_b, values_heads, preferred_element_type=jnp.float32
    )
    attended_b = attended.reshape(-1, width).astype(bf16)
    blocks = (4, tok_dev, model_width)
    out_terms = jnp.dot(attended_b, mat_out, preferred_element_type=jnp.float32)
    (down_grid,), (branch_sum,) = run_parts(
        [grid_gather([down_block]), four_reduce([out_terms.reshape(blocks)])],
        GATHER_REDUCE_PLAN, 3, True, True,
    )
    mat_down = down_grid.reshape(-1, model_width)
    branch_att = branch_sum + vec_out
    middle = tokens + gate_att * branch_att
    normed_mlp, spread_mlp = normalize(middle)
    mlp_own = (normed_mlp * (1.0 + scale_mlp) + shift_mlp).astype(bf16)
    ((mlp_four,),) = run_parts(
        [four_gather([mlp_own])], [(0, "start"), (0, "middle"), (0, "end")], 4, False, True
    )
    mlp_in = mlp_four.reshape(-1, model_width)
    hidden = jnp.dot(mlp_in, mat_up, preferred_element_type=jnp.float32) + vec_up
    activated = gelu_tanh(hidden).astype(bf16)
    branch_terms = jnp.dot(activated, mat_down, preferred_element_type=jnp.float32)
    term_down = weight_term(activated, back_down_all)
    sum_downb = jnp.sum(back_down, axis=0)
    back_hidden = jnp.einsum(
        "rd,fd->rf", back_down_all, mat_down, preferred_element_type=jnp.float32
    ) * gelu_slope(hidden)
    back_hidden_b = back_hidden.astype(bf16)
    term_up = weight_term(mlp_in, back_hidden_b)
    sum_upb = jnp.sum(back_hidden, axis=0)
    back_terms = jnp.einsum(
        "rf,cf->rc", back_hidden_b, mat_up, preferred_element_type=jnp.float32
    )
    chips = lax.axis_size("dp") // 2

    def by_chip(term):
        return term.reshape(chips, -1, term.shape[1])

    (down_sum,), (branch_mlp, back_mlp_in) = run_parts(
        [
            grid_reduce([by_chip(term_down)]),
            four_reduce([branch_terms.reshape(blocks), back_terms.reshape(blocks)]),
        ],
        REDUCE_REDUCE_PLAN, 5, True, True,
    )
    branch_mlp = branch_mlp + vec_down
    block_output = jnp.where(live, middle + gate_mlp * branch_mlp, 0.0)
    back_middle = upstream + norm_back(back_mlp_in * (1.0 + scale_mlp), normed_mlp, spread_mlp)
    back_att = back_middle * gate_att
    (up_sum,), (back_att_four,) = run_parts(
        [grid_reduce([by_chip(term_up)]), four_gather([back_att.astype(bf16)])],
        REDUCE_GATHER_PLAN, 6, True, True,
    )
    back_att_all = back_att_four.reshape(-1, model_width)
    term_out = weight_term(attended_b, back_att_all)
    sum_outb = jnp.sum(back_att, axis=0)
    back_attended = jnp.einsum(
        "rd,cd->rc", back_att_all, mat_out, preferred_element_type=jnp.float32
    ).astype(bf16)
    back_attended = back_attended.reshape(split)
    back_probs = jnp.einsum(
        "sqhd,skhd->shqk", back_attended, values_heads, preferred_element_type=jnp.float32
    )
    row_delta = jnp.einsum("sqhd,sqhd->shq", back_attended.astype(jnp.float32), attended)[..., None]
    back_scores = (attn_probs * (back_probs - row_delta) * scale).astype(bf16)
    back_queries = jnp.einsum(
        "shqk,skhd->sqhd", back_scores, keys_heads, preferred_element_type=jnp.float32
    )
    back_keys = jnp.einsum(
        "shqk,sqhd->skhd", back_scores, queries, preferred_element_type=jnp.float32
    )
    back_values = jnp.einsum(
        "shqk,sqhd->skhd", probs_b, back_attended, preferred_element_type=jnp.float32
    )
    back_parts = [item.reshape(-1, width) for item in (back_queries, back_keys, back_values)]
    sum_qkvb = jnp.concatenate([jnp.sum(item, axis=0) for item in back_parts])
    back_parts = [item.astype(bf16) for item in back_parts]
    qkv_width = 3 * width
    qkv_wide = -(-qkv_width // 128) * 128
    spare = jnp.zeros((back_parts[0].shape[0], qkv_wide - qkv_width), bf16)
    back_qkv_b = jnp.concatenate(back_parts + [spare], axis=1)
    term_qkv = weight_term(attn_in, back_qkv_b)
    back_qkv_b = back_qkv_b[:, :qkv_width]
    attn_terms = jnp.einsum(
        "rd,cd->rc", back_qkv_b, mat_qkv, preferred_element_type=jnp.float32
    )
    ((back_attn_in,),) = run_parts(
        [four_reduce([attn_terms.reshape(blocks)])],
        [(0, "start"), (0, "middle"), (0, "own"), (0, "end")], 7, False, True,
    )
    latent_gradient = jnp.where(
        live,
        back_middle + norm_back(back_attn_in * (1.0 + scale_att), normed_att, spread_att),
        0.0,
    )[None]
    block_output = block_output[None]
    slot_modgrad = jnp.concatenate(
        [
            jnp.sum(back_attn_in, axis=0),
            jnp.sum(back_attn_in * normed_att, axis=0),
            jnp.sum(back_middle * branch_att, axis=0),
            jnp.sum(back_mlp_in, axis=0),
            jnp.sum(back_mlp_in * normed_mlp, axis=0),
            jnp.sum(upstream * branch_mlp, axis=0),
        ]
    )
    devices, own_cols = total_devices(), ada_bias.shape[0]
    qkvb_wide = lax.dynamic_update_slice(
        jnp.zeros((3, 4 * width), jnp.float32), sum_qkvb.reshape(3, width), (0, share * width)
    ).reshape(-1)
    upb_wide = lax.dynamic_update_slice(
        jnp.zeros((4 * hidden_width,), jnp.float32), sum_upb, (share * hidden_width,)
    )
    bias_sums = (qkvb_wide, sum_outb, upb_wide, sum_downb)
    tiles = model_width // 128
    bias_flat = jnp.concatenate(bias_sums)
    tile = latent_count * 128
    bias_tiles = pad_to(bias_flat, 0, (devices - tiles) * tile).reshape(-1, latent_count, 128)
    wide = -(-own_cols // 128) * 128
    sent = pad_to(slot_modgrad.reshape(devices, 1, own_cols), 2, wide) * slot_match[:, None]
    (qkv_sum, out_sum), (columns, sums) = run_parts(
        [
            grid_reduce([by_chip(term_qkv), by_chip(term_out)]),
            closing(sent, bias_tiles, pad_to(rounded(ada_weight), 1, wide)),
        ],
        CLOSING_PLAN, 8, True, None,
    )
    modgrad_cols = columns[:, :own_cols]
    cond_sum = jnp.moveaxis(sums[:tiles], 0, 1).reshape(latent_count, model_width)
    totals, start, bias_totals = sums[tiles:].reshape(-1), 0, []
    for item in bias_sums:
        bias_totals.append(totals[start : start + item.shape[0]])
        start += item.shape[0]
    total_qkvb, total_outb, total_upb, total_downb = bias_totals
    grad_qkvw, grad_upw = scatter_qkv(qkv_sum[:, :qkv_width]), scatter_up(up_sum)
    owned = blocks_to_rows(jnp.concatenate([down_sum, out_sum], axis=0))
    grad_downw = jnp.concatenate([item[:hidden_rows] for item in owned], axis=0)
    grad_outw = jnp.concatenate([item[hidden_rows:] for item in owned], axis=0)
    grad_qkvw, grad_outw, grad_upw, grad_downw = (
        item.astype(jnp.float32) for item in (grad_qkvw, grad_outw, grad_upw, grad_downw)
    )

    grad_adaw = jnp.dot(
        rounded(jax.nn.silu(condition)).T, modgrad_cols, precision=lax.Precision.HIGHEST
    )
    grad_adab = jnp.sum(modgrad_cols, axis=0)
    condition_grad = cond_sum * silu_slope(condition)
    seq_index = lax.axis_index("seq")

    def own_part(full_sum, local_bias):
        length = local_bias.shape[0]
        return lax.dynamic_slice_in_dim(full_sum, seq_index * length, length)

    grad_qkvb = own_part(total_qkvb, qkv_bias)
    grad_outb = own_part(total_outb, out_bias)
    grad_upb = own_part(total_upb, up_bias)
    grad_downb = own_part(total_downb, down_bias)
    grads_all = (
        grad_adaw,
        grad_adab,
        grad_qkvw,
        grad_qkvb,
        grad_outw,
        grad_outb,
        grad_upw,
        grad_upb,
        grad_downw,
        grad_downb,
    )
    params_all = (
        ada_weight,
        ada_bias,
        qkv_weight,
        qkv_bias,
        out_weight,
        out_bias,
        up_weight,
        up_bias,
        down_weight,
        down_bias,
    )
    means_all = (
        mean_adaw,
        mean_adab,
        mean_qkvw,
        mean_qkvb,
        mean_outw,
        mean_outb,
        mean_upw,
        mean_upb,
        mean_downw,
        mean_downb,
    )
    squares_all = (
        sqmean_adaw,
        sqmean_adab,
        sqmean_qkvw,
        sqmean_qkvb,
        sqmean_outw,
        sqmean_outb,
        sqmean_upw,
        sqmean_upb,
        sqmean_downw,
        sqmean_downb,
    )
    updates = [
        adamw_step(p_item, g_item, m_item, v_item)
        for p_item, g_item, m_item, v_item in zip(params_all, grads_all, means_all, squares_all)
    ]
    newvals = tuple((entry[0] for entry in updates))
    newmeans = tuple((entry[1] for entry in updates))
    newsqrs = tuple((entry[2] for entry in updates))
    return (
        (block_output, latent_gradient, condition_grad) + grads_all + newvals + newmeans + newsqrs
    )


def fits(mesh, slots, latent_count, width, hidden):
    groups, ways = mesh.shape["dp"], mesh.shape["seq"]
    return (
        slots == groups
        and ways == 2
        and groups % 4 == 0
        and H % 4 == 0
        and width == H * HD
        and width % (2 * groups * 4) == 0
        and hidden % (2 * groups * 16) == 0
        and width % 128 == 0
        and width // 128 - (-(5 * width + hidden) // (latent_count * 128)) <= groups * ways
    )


def build(mesh, on_device):
    return jax.shard_map(
        on_device,
        mesh=mesh,
        in_specs=(
            P("dp", "seq", None),
            P(),
            P("dp", None),
            P("dp"),
            P("dp", "seq", None),
            P(None, ("dp", "seq")),
            P(("dp", "seq")),
            P("dp", "seq"),
            P("seq"),
            P("dp", "seq"),
            P("seq"),
            P("dp", "seq"),
            P("seq"),
            P("dp", "seq"),
            P("seq"),
            P(None, ("dp", "seq")),
            P(("dp", "seq")),
            P("dp", "seq"),
            P("seq"),
            P("dp", "seq"),
            P("seq"),
            P("dp", "seq"),
            P("seq"),
            P("dp", "seq"),
            P("seq"),
            P(None, ("dp", "seq")),
            P(("dp", "seq")),
            P("dp", "seq"),
            P("seq"),
            P("dp", "seq"),
            P("seq"),
            P("dp", "seq"),
            P("seq"),
            P("dp", "seq"),
            P("seq"),
        ),
        out_specs=(
            P("dp", "seq", None),
            P("dp", "seq", None),
            P(),
            P(None, ("dp", "seq")),
            P(("dp", "seq")),
            P("dp", "seq"),
            P("seq"),
            P("dp", "seq"),
            P("seq"),
            P("dp", "seq"),
            P("seq"),
            P("dp", "seq"),
            P("seq"),
            P(None, ("dp", "seq")),
            P(("dp", "seq")),
            P("dp", "seq"),
            P("seq"),
            P("dp", "seq"),
            P("seq"),
            P("dp", "seq"),
            P("seq"),
            P("dp", "seq"),
            P("seq"),
            P(None, ("dp", "seq")),
            P(("dp", "seq")),
            P("dp", "seq"),
            P("seq"),
            P("dp", "seq"),
            P("seq"),
            P("dp", "seq"),
            P("seq"),
            P("dp", "seq"),
            P("seq"),
            P(None, ("dp", "seq")),
            P(("dp", "seq")),
            P("dp", "seq"),
            P("seq"),
            P("dp", "seq"),
            P("seq"),
            P("dp", "seq"),
            P("seq"),
            P("dp", "seq"),
            P("seq"),
        ),
        check_vma=False,
    )


def solution(mesh):
    def program(latents, condition, *rest):
        hidden, width = rest[11].shape
        chosen = fits(mesh, latents.shape[0], condition.shape[0], width, hidden)
        return build(mesh, on_device_grid if chosen else on_device_general)(
            latents, condition, *rest
        )

    return program
```

```python
import functools

import jax
import jax.numpy as jnp
from jax import lax
from jax.experimental import pallas as pl
from jax.experimental.pallas import tpu as pltpu
from jax.sharding import PartitionSpec as P

H = 16
HD = 72
STEP = 2


EPS_NORM = 1e-06
GELU_COEF = 0.7978845608
GELU_CUBE = 0.044715
BETA_ONE = 0.9
BETA_TWO = 0.999
LEARN_RATE = 0.05
EPS_ADAM = 1e-08


def rounded(values):
    return lax.optimization_barrier(values.astype(jnp.bfloat16)).astype(jnp.float32)


def normalize(values):
    center = values - jnp.mean(values, axis=-1, keepdims=True)
    spread = lax.rsqrt(jnp.mean(center * center, axis=-1, keepdims=True) + EPS_NORM)
    return (center * spread, spread)


def norm_back(upstream, normed, spread):
    return spread * (
        upstream
        - jnp.mean(upstream, axis=-1, keepdims=True)
        - normed * jnp.mean(upstream * normed, axis=-1, keepdims=True)
    )


def gelu_tanh(values):
    tanh_part = jnp.tanh(GELU_COEF * (values + GELU_CUBE * values * values * values))
    return 0.5 * values * (1.0 + tanh_part)


def gelu_slope(values):
    tanh_part = jnp.tanh(GELU_COEF * (values + GELU_CUBE * values * values * values))
    return 0.5 * (1.0 + tanh_part) + 0.5 * values * (1.0 - tanh_part * tanh_part) * GELU_COEF * (
        1.0 + 3.0 * GELU_CUBE * values * values
    )


def silu_slope(values):
    sigmoid_part = jax.nn.sigmoid(values)
    return sigmoid_part * (1.0 + values * (1.0 - sigmoid_part))


def adamw_step(parameter, gradient, first_mom, second):
    first_new = BETA_ONE * first_mom + (1.0 - BETA_ONE) * gradient
    second_new = BETA_TWO * second + (1.0 - BETA_TWO) * gradient * gradient
    first_hat = first_new / (1.0 - BETA_ONE**STEP)
    second_hat = second_new / (1.0 - BETA_TWO**STEP)
    return (
        parameter - LEARN_RATE * first_hat / (jnp.sqrt(second_hat) + EPS_ADAM),
        first_new,
        second_new,
    )


def flat_index(axes):
    index = lax.axis_index(axes[0])
    for axis in axes[1:]:
        index = index * lax.axis_size(axis) + lax.axis_index(axis)
    return index


def swap_bit(values, axes, step):
    total = 1
    for axis in axes:
        total *= lax.axis_size(axis)
    return lax.ppermute(values, axes, [(i, i ^ step) for i in range(total)])


def axes_size(axes):
    total = 1
    for axis in axes:
        total *= lax.axis_size(axis)
    return total


def gather_tree(values, axes):
    index, blocks, step = flat_index(axes), values[None], 1
    while step < axes_size(axes):
        other = swap_bit(blocks, axes, step)
        upper = (index // step) % 2 == 1
        blocks = jnp.concatenate(
            [jnp.where(upper, other, blocks), jnp.where(upper, blocks, other)], axis=0
        )
        step *= 2
    return blocks


def scatter_tree(blocks, axes, sent=None):
    index, step = flat_index(axes), axes_size(axes) // 2
    while step >= 1:
        low, high = blocks[:step], blocks[step:]
        upper = (index // step) % 2 == 1
        away = jnp.where(upper, low, high)
        if sent is not None:
            away = away.astype(sent)
        kept = jnp.where(upper, high, low)
        blocks = kept + swap_bit(away, axes, step).astype(kept.dtype)
        step //= 2
    return blocks[0]


def sum_tree(values, axes):
    step = 1
    while step < axes_size(axes):
        values = values + swap_bit(values, axes, step)
        step *= 2
    return values


def join_columns(halves, widths):
    parts, start = [], 0
    for width in widths:
        part = halves[:, :, start : start + width]
        parts.append(jnp.moveaxis(part, 0, 1).reshape(part.shape[1], -1))
        start += width
    return parts


def split_columns(parts):
    ways = lax.axis_size("seq")
    blocks = [
        jnp.moveaxis(part.reshape(part.shape[0], ways, -1), 1, 0) for part in parts
    ]
    return jnp.concatenate(blocks, axis=2)


def piece_moves(turn):
    rows, ways = lax.axis_size("dp"), lax.axis_size("seq")
    pairs = []
    for g in range(rows):
        for x in range(ways):
            piece = g * ways + (turn + x) % ways
            pairs.append((g * ways + x, (piece % rows) * ways + piece // rows))
    return pairs


def own_piece():
    return lax.axis_index("seq") * lax.axis_size("dp") + lax.axis_index("dp")


def pick(blocks, index):
    return lax.dynamic_index_in_dim(blocks, index, 0, keepdims=False)


def rows_from_owners(block):
    ways, x = lax.axis_size("seq"), lax.axis_index("seq")
    pieces = block.reshape(ways, -1, block.shape[1])
    got = jnp.stack(
        [
            lax.ppermute(pick(pieces, (turn + x) % ways), ("dp", "seq"), piece_moves(turn))
            for turn in range(ways)
        ]
    )
    place = own_piece() % ways
    return jnp.concatenate([pick(got, (place - i + ways) % ways) for i in range(ways)], axis=1)


def rows_to_owners(piece):
    ways, x = lax.axis_size("seq"), lax.axis_index("seq")
    columns = jnp.moveaxis(piece.reshape(piece.shape[0], ways, -1), 1, 0)
    place = own_piece() % ways
    got = jnp.stack(
        [
            lax.ppermute(
                pick(columns, (place - turn + ways) % ways),
                ("dp", "seq"),
                [(taker, owner) for owner, taker in piece_moves(turn)],
            )
            for turn in range(ways)
        ]
    )
    ordered = jnp.stack([pick(got, (q - x + ways) % ways) for q in range(ways)])
    return ordered.reshape(-1, ordered.shape[2])


def all_tokens(values):
    return gather_tree(values, ("seq",)).reshape(-1, values.shape[1])


def own_tokens(terms):
    blocks = terms.reshape(lax.axis_size("seq"), -1, terms.shape[1])
    return scatter_tree(blocks, ("seq",), jnp.bfloat16)


def weight_term(left, right):
    return jnp.einsum("rc,rd->cd", left, right, preferred_element_type=jnp.float32).astype(
        jnp.bfloat16
    )


def spread_terms(terms):
    widths = [term.shape[1] // lax.axis_size("seq") for term in terms]
    joined = jnp.concatenate(terms, axis=1) if len(terms) > 1 else terms[0]
    rows = lax.psum_scatter(joined, "dp", scatter_dimension=0, tiled=True)
    pieces, start = [], 0
    for term in terms:
        pieces.append(rows[:, start : start + term.shape[1]])
        start += term.shape[1]
    own = scatter_tree(split_columns(pieces).astype(jnp.float32), ("seq",), jnp.bfloat16)
    blocks, start = [], 0
    for width in widths:
        blocks.append(own[:, start : start + width])
        start += width
    return blocks


def on_device_general(
    latents,
    condition,
    slot_latent,
    slot_counts,
    output_gradient,
    ada_weight,
    ada_bias,
    qkv_weight,
    qkv_bias,
    out_weight,
    out_bias,
    up_weight,
    up_bias,
    down_weight,
    down_bias,
    mean_adaw,
    mean_adab,
    mean_qkvw,
    mean_qkvb,
    mean_outw,
    mean_outb,
    mean_upw,
    mean_upb,
    mean_downw,
    mean_downb,
    sqmean_adaw,
    sqmean_adab,
    sqmean_qkvw,
    sqmean_qkvb,
    sqmean_outw,
    sqmean_outb,
    sqmean_upw,
    sqmean_upb,
    sqmean_downw,
    sqmean_downb,
):
    slot_total, tok_dev, model_width = latents.shape
    row_count = slot_total * tok_dev
    scale = HD ** (-0.5)
    live_slots = jnp.arange(slot_total) < slot_counts[0]
    live_mask = live_slots[:, None, None]
    latent_count = condition.shape[0]
    slot_matches = (
        (slot_latent[0][:, None] == jnp.arange(latent_count)[None, :]) & live_slots[:, None]
    ).astype(jnp.float32)
    silu_cond = jax.nn.silu(condition).astype(jnp.bfloat16)
    mod_cols = jnp.dot(
        silu_cond, ada_weight.astype(jnp.bfloat16), preferred_element_type=jnp.float32
    ) + rounded(ada_bias)
    modulation = jnp.moveaxis(gather_tree(mod_cols, ("dp", "seq")), 0, 1).reshape(
        latent_count, -1
    )
    slot_mod = jnp.dot(slot_matches, modulation, precision=lax.Precision.HIGHEST)[:, None, :]
    shift_att, scale_att, gate_att, shift_mlp, scale_mlp, gate_mlp = jnp.split(slot_mod, 6, axis=2)
    upstream = jnp.where(live_mask, output_gradient, 0.0)
    biases = (qkv_bias, out_bias, down_bias)
    bias_rows = gather_tree(
        jnp.concatenate(biases).astype(jnp.bfloat16)[None], ("seq",)
    )
    vec_qkv, vec_out, vec_down = (
        part[0].astype(jnp.float32)
        for part in join_columns(bias_rows, [item.shape[0] for item in biases])
    )
    wide = (qkv_weight, out_weight)
    wide_halves = gather_tree(jnp.concatenate(wide, axis=1).astype(jnp.bfloat16), ("seq",))
    wide_rows = jnp.concatenate(
        join_columns(wide_halves, [item.shape[1] for item in wide])
        + [up_weight.astype(jnp.bfloat16)],
        axis=1,
    )
    wide_full = lax.all_gather(wide_rows, "dp", axis=0, tiled=True)
    qkv_end = 3 * model_width
    mat_qkv = wide_full[:, :qkv_end]
    mat_out = wide_full[:, qkv_end : qkv_end + model_width]
    mat_up = wide_full[:, qkv_end + model_width :]
    down_rows = rows_from_owners(down_weight.astype(jnp.bfloat16))
    mat_down = lax.all_gather(down_rows, "dp", axis=0, tiled=True)
    normed_att, spread_att = normalize(latents)
    attn_in = (
        (normed_att * (1.0 + scale_att) + shift_att)
        .astype(jnp.bfloat16)
        .reshape(row_count, model_width)
    )
    qkv_all = (jnp.dot(attn_in, mat_qkv, preferred_element_type=jnp.float32) + vec_qkv).astype(
        jnp.bfloat16
    )
    queries = qkv_all[:, :model_width].reshape(slot_total, tok_dev, H, HD)
    keys_own = qkv_all[:, model_width : 2 * model_width].reshape(slot_total, tok_dev, model_width)
    values_own = qkv_all[:, 2 * model_width :].reshape(slot_total, tok_dev, model_width)
    pairs_own = jnp.concatenate([keys_own, values_own], axis=2)
    pairs_all = jnp.moveaxis(gather_tree(pairs_own, ("seq",)), 0, 1)
    pairs_all = pairs_all.reshape(slot_total, -1, 2 * model_width)
    keys_all, values_all = pairs_all[:, :, :model_width], pairs_all[:, :, model_width:]
    keys_heads = keys_all.reshape(slot_total, -1, H, HD)
    values_heads = values_all.reshape(slot_total, -1, H, HD)
    scores = (
        jnp.einsum("sqhd,skhd->shqk", queries, keys_heads, preferred_element_type=jnp.float32)
        * scale
    )
    row_max = jnp.max(scores, axis=-1, keepdims=True)
    row_total = jnp.sum(jnp.exp(scores - row_max), axis=-1, keepdims=True)
    attn_probs = jnp.exp(scores - row_max) / row_total
    probs_b = attn_probs.astype(jnp.bfloat16)
    attended = jnp.einsum(
        "shqk,skhd->sqhd", probs_b, values_heads, preferred_element_type=jnp.float32
    )
    attended_b = attended.reshape(row_count, model_width).astype(jnp.bfloat16)
    branch_att = (
        jnp.dot(attended_b, mat_out, preferred_element_type=jnp.float32) + vec_out
    ).reshape(slot_total, tok_dev, model_width)
    middle = latents + gate_att * branch_att
    normed_mlp, spread_mlp = normalize(middle)
    mlp_in = (
        (normed_mlp * (1.0 + scale_mlp) + shift_mlp)
        .astype(jnp.bfloat16)
        .reshape(row_count, model_width)
    )
    mlp_all = all_tokens(mlp_in)
    hidden = jnp.dot(mlp_all, mat_up, preferred_element_type=jnp.float32) + rounded(up_bias)
    activated = gelu_tanh(hidden).astype(jnp.bfloat16)
    activated, mat_down = lax.optimization_barrier((activated, mat_down))
    branch_mlp = (
        own_tokens(jnp.dot(activated, mat_down, preferred_element_type=jnp.float32)) + vec_down
    ).reshape(slot_total, tok_dev, model_width)
    block_output = jnp.where(live_mask, middle + gate_mlp * branch_mlp, 0.0)
    back_down = upstream * gate_mlp
    back_down_b = back_down.astype(jnp.bfloat16).reshape(row_count, model_width)
    back_down_all = all_tokens(back_down_b)
    down_sums = lax.psum_scatter(
        weight_term(activated, back_down_all), "dp", scatter_dimension=0, tiled=True
    )
    grad_downw = rows_to_owners(down_sums).astype(jnp.float32)
    sum_downb = jnp.sum(back_down, axis=(0, 1))
    back_hidden = jnp.einsum(
        "rd,fd->rf", back_down_all, mat_down, preferred_element_type=jnp.float32
    ) * gelu_slope(hidden)
    back_hidden_b = back_hidden.astype(jnp.bfloat16)
    grad_upw = lax.psum_scatter(
        weight_term(mlp_all, back_hidden_b), "dp", scatter_dimension=0, tiled=True
    ).astype(jnp.float32)
    up_total = jnp.zeros((lax.axis_size("seq") * up_bias.shape[0],), jnp.float32)
    sum_upb = lax.dynamic_update_slice_in_dim(
        up_total, jnp.sum(back_hidden, axis=0), lax.axis_index("seq") * up_bias.shape[0], 0
    )
    back_mlp_in = own_tokens(
        jnp.einsum("rf,cf->rc", back_hidden_b, mat_up, preferred_element_type=jnp.float32)
    ).reshape(slot_total, tok_dev, model_width)
    back_middle = upstream + norm_back(back_mlp_in * (1.0 + scale_mlp), normed_mlp, spread_mlp)
    back_att = back_middle * gate_att
    back_att_b = back_att.astype(jnp.bfloat16).reshape(row_count, model_width)
    term_out = weight_term(attended_b, back_att_b)
    sum_outb = jnp.sum(back_att, axis=(0, 1))
    back_attended = jnp.einsum(
        "rd,cd->rc", back_att_b, mat_out, preferred_element_type=jnp.float32
    ).astype(jnp.bfloat16)
    back_attended = back_attended.reshape(slot_total, tok_dev, H, HD)
    back_probs = jnp.einsum(
        "sqhd,skhd->shqk", back_attended, values_heads, preferred_element_type=jnp.float32
    )
    row_delta = jnp.einsum("sqhd,sqhd->shq", back_attended.astype(jnp.float32), attended)[..., None]
    back_scores = (attn_probs * (back_probs - row_delta) * scale).astype(jnp.bfloat16)
    back_queries = jnp.einsum(
        "shqk,skhd->sqhd", back_scores, keys_heads, preferred_element_type=jnp.float32
    )
    key_terms = jnp.einsum(
        "shqk,sqhd->skhd", back_scores, queries, preferred_element_type=jnp.float32
    ).reshape(slot_total, -1, model_width)
    value_terms = jnp.einsum(
        "shqk,sqhd->skhd", probs_b, back_attended, preferred_element_type=jnp.float32
    ).reshape(slot_total, -1, model_width)
    pair_terms = jnp.concatenate([key_terms, value_terms], axis=2)
    pair_terms = pair_terms.reshape(slot_total, -1, tok_dev, 2 * model_width)
    back_pairs = scatter_tree(jnp.moveaxis(pair_terms, 1, 0), ("seq",), jnp.bfloat16)
    back_keys, back_values = back_pairs[:, :, :model_width], back_pairs[:, :, model_width:]
    back_qkv = jnp.concatenate(
        [
            back_queries.reshape(row_count, model_width),
            back_keys.reshape(row_count, model_width),
            back_values.reshape(row_count, model_width),
        ],
        axis=1,
    )
    back_qkv_b = back_qkv.astype(jnp.bfloat16)
    term_qkv = weight_term(attn_in, back_qkv_b)
    grad_qkvw, grad_outw = spread_terms([term_qkv, term_out])
    sum_qkvb = jnp.sum(back_qkv, axis=0)
    back_attn_in = jnp.einsum(
        "rd,cd->rc", back_qkv_b, mat_qkv, preferred_element_type=jnp.float32
    ).reshape(slot_total, tok_dev, model_width)
    latent_gradient = jnp.where(
        live_mask,
        back_middle + norm_back(back_attn_in * (1.0 + scale_att), normed_att, spread_att),
        0.0,
    )
    slot_modgrad = jnp.concatenate(
        [
            jnp.sum(back_attn_in, axis=1),
            jnp.sum(back_attn_in * normed_att, axis=1),
            jnp.sum(back_middle * branch_att, axis=1),
            jnp.sum(back_mlp_in, axis=1),
            jnp.sum(back_mlp_in * normed_mlp, axis=1),
            jnp.sum(upstream * branch_mlp, axis=1),
        ],
        axis=1,
    )
    modgrad_table = jnp.dot(slot_matches.T, slot_modgrad, precision=lax.Precision.HIGHEST)
    modgrad_cols = scatter_tree(
        jnp.moveaxis(modgrad_table.reshape(latent_count, -1, ada_bias.shape[0]), 1, 0),
        ("dp", "seq"),
    )
    grad_adaw = jnp.dot(
        rounded(jax.nn.silu(condition)).T, modgrad_cols, precision=lax.Precision.HIGHEST
    )
    grad_adab = jnp.sum(modgrad_cols, axis=0)
    cond_term = jnp.dot(modgrad_cols, rounded(ada_weight).T, precision=lax.Precision.HIGHEST)
    cond_sum = sum_tree(cond_term, ("dp", "seq"))
    bias_sums = (sum_qkvb, sum_outb, sum_upb, sum_downb)
    totals, start, bias_totals = sum_tree(jnp.concatenate(bias_sums), ("dp", "seq")), 0, []
    for item in bias_sums:
        bias_totals.append(totals[start : start + item.shape[0]])
        start += item.shape[0]
    total_qkvb, total_outb, total_upb, total_downb = bias_totals
    condition_grad = cond_sum * silu_slope(condition)
    seq_index = lax.axis_index("seq")

    def own_part(full_sum, local_bias):
        length = local_bias.shape[0]
        return lax.dynamic_slice_in_dim(full_sum, seq_index * length, length)

    grad_qkvb = own_part(total_qkvb, qkv_bias)
    grad_outb = own_part(total_outb, out_bias)
    grad_upb = own_part(total_upb, up_bias)
    grad_downb = own_part(total_downb, down_bias)
    grads_all = (
        grad_adaw,
        grad_adab,
        grad_qkvw,
        grad_qkvb,
        grad_outw,
        grad_outb,
        grad_upw,
        grad_upb,
        grad_downw,
        grad_downb,
    )
    params_all = (
        ada_weight,
        ada_bias,
        qkv_weight,
        qkv_bias,
        out_weight,
        out_bias,
        up_weight,
        up_bias,
        down_weight,
        down_bias,
    )
    means_all = (
        mean_adaw,
        mean_adab,
        mean_qkvw,
        mean_qkvb,
        mean_outw,
        mean_outb,
        mean_upw,
        mean_upb,
        mean_downw,
        mean_downb,
    )
    squares_all = (
        sqmean_adaw,
        sqmean_adab,
        sqmean_qkvw,
        sqmean_qkvb,
        sqmean_outw,
        sqmean_outb,
        sqmean_upw,
        sqmean_upb,
        sqmean_downw,
        sqmean_downb,
    )
    updates = [
        adamw_step(p_item, g_item, m_item, v_item)
        for p_item, g_item, m_item, v_item in zip(params_all, grads_all, means_all, squares_all)
    ]
    newvals = tuple((entry[0] for entry in updates))
    newmeans = tuple((entry[1] for entry in updates))
    newsqrs = tuple((entry[2] for entry in updates))
    return (
        (block_output, latent_gradient, condition_grad) + grads_all + newvals + newmeans + newsqrs
    )


MESH_ID = pl.DeviceIdType.MESH
ANY = pl.BlockSpec(memory_space=pl.ANY)
VMEM = pl.BlockSpec(memory_space=pltpu.VMEM)


def params_of(number):
    return pltpu.CompilerParams(
        collective_id=number, has_side_effects=True, vmem_limit_bytes=56 * 2**20
    )


def place():
    group, x = lax.axis_index("dp"), lax.axis_index("seq")
    core, chip = group % 2, group // 2
    return chip // 2, chip % 2, core, x


def device(a, b, core, x):
    return ((a * 2 + b) * 2 + core, x)


def remote(src, dst, send, recv, target):
    return pltpu.make_async_remote_copy(
        src_ref=src,
        dst_ref=dst,
        send_sem=send,
        recv_sem=recv,
        device_id=target,
        device_id_type=MESH_ID,
    )


def greet(targets, present):
    barrier = pltpu.get_barrier_semaphore()
    amount = 0
    for target, there in zip(targets, present):

        def signal():
            pl.semaphore_signal(barrier, inc=1, device_id=target, device_id_type=MESH_ID)

        if there is True:
            signal()
            amount = amount + 1
        else:
            pl.when(there)(signal)
            amount = amount + there.astype(jnp.int32)
    pl.semaphore_wait(barrier, amount)


def greet_near(lines, grid, four):
    a, b, core, x = place()
    targets, present = [], []
    if grid:
        targets += [device(a, 1 - b, core, x), device(a - 1, b, core, x), device(a + 1, b, core, x)]
        present += [True, a > 0, a < lines - 1]
    if four:
        targets += [device(a, b, 1 - core, x), device(a, b, core, 1 - x)]
        present += [True, True]
    greet(targets, present)


class Part:
    def __init__(self, make, ins, in_specs, outs, out_specs, scratch):
        self.make, self.ins, self.in_specs = make, ins, in_specs
        self.outs, self.out_specs, self.scratch = outs, out_specs, scratch


def joint_kernel(parts, plan, lines, grid, four, *refs):
    ins = [len(part.ins) for part in parts]
    outs = [len(part.outs) for part in parts]
    at_in, at_out = 0, sum(ins)
    at_scratch = at_out + sum(outs)
    if four is None:
        greet_all()
    else:
        greet_near(lines, grid, four)
    stages = []
    for part, n_in, n_out in zip(parts, ins, outs):
        n_scratch = len(part.scratch)
        stages.append(
            part.make(
                refs[at_in : at_in + n_in],
                refs[at_out : at_out + n_out],
                refs[at_scratch : at_scratch + n_scratch],
            )
        )
        at_in, at_out, at_scratch = at_in + n_in, at_out + n_out, at_scratch + n_scratch
    for index, stage in plan:
        stages[index][stage]()


def run_parts(parts, plan, number, grid, four):
    lines = lax.axis_size("dp") // 4
    flat = pl.pallas_call(
        functools.partial(joint_kernel, parts, plan, lines, grid, four),
        out_shape=sum((part.outs for part in parts), []),
        in_specs=sum((part.in_specs for part in parts), []),
        out_specs=sum((part.out_specs for part in parts), []),
        scratch_shapes=sum((part.scratch for part in parts), []),
        compiler_params=params_of(number),
        name="joint",
    )(*sum((part.ins for part in parts), []))
    results, start = [], 0
    for part in parts:
        results.append(flat[start : start + len(part.outs)])
        start += len(part.outs)
    return results


def strips(rows):
    return [(i, 48) for i in range(0, rows, 48)] if rows % 48 == 0 else [(0, rows)]


def view(ref, rows, part, lead):
    if part == (0, rows):
        return ref
    cut_rows = pl.ds(*part)
    return ref.at[:, cut_rows, :] if lead else ref.at[cut_rows, :]


def views(refs, rows, lead):
    return [
        view(ref, size, part, lead) for ref, size in zip(refs, rows) for part in strips(size)
    ]


def grid_gather(pieces):
    lines = lax.axis_size("dp") // 4
    rows = [piece.shape[0] for piece in pieces]
    count, whole = sum(len(strips(size)) for size in rows), len(pieces)

    def make(ins, outs, scratch):
        ins, outs = views(ins, rows, False), views(outs, rows, True)
        keep, up_send, down_send, side_send, line_recv, side_recv = scratch
        a, b, core, x = place()
        own = a * 2 + b
        copies = [
            pltpu.make_async_copy(ins[p], outs[p].at[own], keep.at[p]) for p in range(count)
        ]

        def up(p, s, src):
            return remote(
                src, outs[p].at[s * 2 + b], up_send.at[p, s], line_recv.at[p, s],
                device(a + 1, b, core, x),
            )

        def down(p, s, src):
            return remote(
                src, outs[p].at[s * 2 + b], down_send.at[p, s], line_recv.at[p, s],
                device(a - 1, b, core, x),
            )

        def side(p, s, src):
            return remote(
                src, outs[p].at[s * 2 + b], side_send.at[p, s], side_recv.at[p, s],
                device(a, 1 - b, core, x),
            )

        def arrived(p, s):
            block = outs[p].at[s * 2 + b]
            remote(
                block, block, up_send.at[p, s], line_recv.at[p, s], device(a, 1 - b, core, x)
            ).wait_recv()
            return block

        def start():
            for p in range(count):
                pl.when(a < lines - 1)(lambda: up(p, a, ins[p]).start())
                pl.when(a > 0)(lambda: down(p, a, ins[p]).start())
                side(p, a, ins[p]).start()
                copies[p].start()

        def hop_of(hop):
            def run():
                for p in range(count):

                    def from_below():
                        block = arrived(p, a - hop)
                        pl.when(a < lines - 1)(lambda: up(p, a - hop, block).start())
                        side(p, a - hop, block).start()

                    def from_above():
                        block = arrived(p, a + hop)
                        pl.when(a > 0)(lambda: down(p, a + hop, block).start())
                        side(p, a + hop, block).start()

                    pl.when(a - hop >= 0)(from_below)
                    pl.when(a + hop < lines)(from_above)

            return run

        def got(p):
            copies[p].wait()
            for s in range(lines):
                block = outs[p].at[s * 2 + 1 - b]
                remote(
                    block, block, side_send.at[p, s], side_recv.at[p, s],
                    device(a, 1 - b, core, x),
                ).wait_recv()

        def sent(p):
            for s in range(lines):
                block = outs[p].at[s * 2 + b]
                side(p, s, block).wait_send()
                pl.when((s <= a) & (a < lines - 1))(lambda: up(p, s, block).wait_send())
                pl.when((s >= a) & (a > 0))(lambda: down(p, s, block).wait_send())

        def hops():
            for hop in range(1, lines):
                hop_of(hop)()

        def end():
            for p in range(count):
                got(p)
                sent(p)

        def early():
            got(0)

        def late():
            for p in range(1, count):
                got(p)
            for p in range(count):
                sent(p)

        return dict(start=start, hops=hops, end=end, early=early, late=late, hop=hop_of(1),
                    more=lambda: [hop_of(hop)() for hop in range(2, lines)])

    dma = pltpu.SemaphoreType.DMA
    return Part(
        make,
        list(pieces),
        [ANY] * whole,
        [jax.ShapeDtypeStruct((2 * lines,) + piece.shape, piece.dtype) for piece in pieces],
        [ANY] * whole,
        [dma((count,))] + [dma((count, lines))] * 5,
    )


AHEAD = 4


def grid_reduce(pieces):
    lines = lax.axis_size("dp") // 4
    rows = [piece.shape[1] for piece in pieces]
    count, whole = sum(len(strips(size)) for size in rows), len(pieces)

    def make(ins, outs, scratch):
        held, lower, upper = (
            views(scratch[i * whole : (i + 1) * whole], rows, True) for i in range(3)
        )
        up_send, down_send, side_send, up_recv, down_recv, side_recv = scratch[3 * whole :]
        ins, outs = views(ins, rows, True), views(outs, rows, False)
        a, b, core, x = place()

        def side(p, t):
            return remote(
                ins[p].at[t * 2 + 1 - b], held[p].at[t], side_send.at[p, t], side_recv.at[p, t],
                device(a, 1 - b, core, x),
            )

        def up(p, t):
            return remote(
                held[p].at[t], lower[p].at[t], up_send.at[p, t], up_recv.at[p, t],
                device(a + 1, b, core, x),
            )

        def down(p, t):
            return remote(
                held[p].at[t], upper[p].at[t], down_send.at[p, t], down_recv.at[p, t],
                device(a - 1, b, core, x),
            )

        def sum_into(p, t, target, others):
            total = ins[p][t * 2 + b].astype(jnp.float32)
            for other in others:
                total = total + other[...].astype(jnp.float32)
            target[...] = total.astype(target.dtype)

        half = lines // 2
        order = list(range(lines - 1, half - 1, -1)) + list(range(half))

        def turn(k):
            p, t = k % count, order[k // count]
            return p, jnp.where(a < half, t, lines - 1 - t)

        def start():
            for k in range(min(AHEAD, count * lines)):
                side(*turn(k)).start()

        def step(k):
            p, t = turn(k)
            side(p, t).wait_recv()
            mine = held[p].at[t]

            def upward():
                def joined():
                    up(p, t).wait_recv()
                    sum_into(p, t, mine, [mine, lower[p].at[t]])

                pl.when(a > 0)(joined)
                pl.when(a == 0)(lambda: sum_into(p, t, mine, [mine]))
                up(p, t).start()

            def downward():
                def joined():
                    down(p, t).wait_recv()
                    sum_into(p, t, mine, [mine, upper[p].at[t]])

                pl.when(a < lines - 1)(joined)
                pl.when(a == lines - 1)(lambda: sum_into(p, t, mine, [mine]))
                down(p, t).start()

            pl.when(a < t)(upward)
            pl.when(a > t)(downward)
            if k + AHEAD < count * lines:
                side(*turn(k + AHEAD)).start()

        def steps():
            for k in range(count * lines):
                step(k)

        def first():
            for k in range(count):
                step(k)

        def second():
            for k in range(count, 2 * count):
                step(k)

        def others():
            for k in range(2 * count, count * lines):
                step(k)

        def end():
            for p in range(count):
                terms = held[p].at[a], lower[p].at[a], upper[p].at[a]
                pl.when(a > 0)(lambda: up(p, a).wait_recv())
                pl.when(a < lines - 1)(lambda: down(p, a).wait_recv())
                pl.when(a == 0)(lambda: sum_into(p, a, outs[p], [terms[0], terms[2]]))
                pl.when(a == lines - 1)(lambda: sum_into(p, a, outs[p], [terms[0], terms[1]]))
                pl.when((a > 0) & (a < lines - 1))(lambda: sum_into(p, a, outs[p], terms))
            for p in range(count):
                for t in range(lines):
                    side(p, t).wait_send()
                    pl.when(a < t)(lambda: up(p, t).wait_send())
                    pl.when(a > t)(lambda: down(p, t).wait_send())

        return dict(
            start=start, steps=steps, first=first, second=second, others=others, end=end
        )

    dma = pltpu.SemaphoreType.DMA
    slots = [pltpu.VMEM((lines,) + piece.shape[1:], piece.dtype) for piece in pieces]
    return Part(
        make,
        list(pieces),
        [VMEM] * whole,
        [jax.ShapeDtypeStruct(piece.shape[1:], piece.dtype) for piece in pieces],
        [VMEM] * whole,
        slots * 3 + [dma((count, lines))] * 6,
    )


def four_stages(ins, outs, scratch):
    count = len(outs)
    keep, sib_send, x_send, fwd_send, sib_recv, x_recv, fwd_recv = scratch
    a, b, core, x = place()
    own, across = core * 2 + x, core * 2 + 1 - x
    sibling, peer = device(a, b, 1 - core, x), device(a, b, core, 1 - x)
    to_x, to_sib, to_fwd, copies = [], [], [], []
    for p in range(count):
        block, far = outs[p].at[own], outs[p].at[across]
        to_x.append(remote(ins[p], block, x_send.at[p], x_recv.at[p], peer))
        to_sib.append(remote(ins[p], block, sib_send.at[p], sib_recv.at[p], sibling))
        to_fwd.append(remote(far, far, fwd_send.at[p], fwd_recv.at[p], sibling))
        copies.append(pltpu.make_async_copy(ins[p], block, keep.at[p]))

    def start():
        for p in range(count):
            to_x[p].start()
            to_sib[p].start()
            copies[p].start()

    def middle():
        for p in range(count):
            to_x[p].wait_recv()
            to_fwd[p].start()

    def end():
        for p in range(count):
            to_sib[p].wait_recv()
            to_fwd[p].wait_recv()
            copies[p].wait()
            to_x[p].wait_send()
            to_sib[p].wait_send()
            to_fwd[p].wait_send()

    return dict(start=start, middle=middle, end=end)


def four_gather(pieces):
    count = len(pieces)
    return Part(
        four_stages,
        list(pieces),
        [VMEM] * count,
        [jax.ShapeDtypeStruct((4,) + piece.shape, piece.dtype) for piece in pieces],
        [VMEM] * count,
        [pltpu.SemaphoreType.DMA((count,))] * 7,
    )


def grid_four_gather(pieces):
    base = grid_gather(pieces)
    base_outs = len(base.outs)

    def make(ins, outs, scratch):
        stages = base.make(ins, outs[:base_outs], scratch[: len(base.scratch)])
        four = four_stages([outs[0]], outs[base_outs:], scratch[len(base.scratch) :])
        for name, stage in four.items():
            stages["four_" + name] = stage
        return stages

    first = base.outs[0]
    return Part(
        make,
        base.ins,
        base.in_specs,
        base.outs + [jax.ShapeDtypeStruct((4,) + first.shape, first.dtype)],
        base.out_specs + [ANY],
        base.scratch + [pltpu.SemaphoreType.DMA((1,))] * 7,
    )


def four_reduce(pieces):
    count = len(pieces)

    def make(ins, outs, scratch):
        near, out_x, in_x = (scratch[i * count : (i + 1) * count] for i in range(3))
        sib_send, sib_recv, x_send, x_recv = scratch[3 * count :]
        a, b, core, x = place()
        own, across = core * 2 + x, core * 2 + 1 - x
        sibling, peer = device(a, b, 1 - core, x), device(a, b, core, 1 - x)
        to_sib, to_x = [], []
        for p in range(count):
            to_sib.append(
                [
                    remote(
                        ins[p].at[(1 - core) * 2 + side], near[p].at[i], sib_send.at[p, i],
                        sib_recv.at[p, i], sibling,
                    )
                    for i, side in enumerate((1 - x, x))
                ]
            )
            to_x.append(remote(out_x[p], in_x[p], x_send.at[p], x_recv.at[p], peer))

        def start():
            for i in range(2):
                for p in range(count):
                    to_sib[p][i].start()

        def middle():
            for p in range(count):
                to_sib[p][0].wait_recv()
                out_x[p][...] = (ins[p][across] + near[p][0]).astype(out_x[p].dtype)
                to_x[p].start()

        def own_sums():
            for p in range(count):
                to_sib[p][1].wait_recv()
                outs[p][...] = ins[p][own] + near[p][1]

        def end():
            for p in range(count):
                to_x[p].wait_recv()
                outs[p][...] += in_x[p][...].astype(jnp.float32)
                to_x[p].wait_send()
                for i in range(2):
                    to_sib[p][i].wait_send()

        return dict(start=start, middle=middle, own=own_sums, end=end)

    dma = pltpu.SemaphoreType.DMA
    shapes = [piece.shape[1:] for piece in pieces]
    return Part(
        make,
        list(pieces),
        [VMEM] * count,
        [jax.ShapeDtypeStruct(shape, jnp.float32) for shape in shapes],
        [VMEM] * count,
        [pltpu.VMEM((2,) + shape, jnp.float32) for shape in shapes]
        + [pltpu.VMEM(shape, jnp.bfloat16) for shape in shapes] * 2
        + [dma((count, 2))] * 2
        + [dma((count,))] * 2,
    )


GATHER_PLAN = [
    (0, "start"), (1, "start"), (0, "hop"), (1, "middle"), (0, "more"), (1, "end"), (0, "end"),
]
GATHER_REDUCE_PLAN = [
    (0, "start"), (1, "start"), (0, "hop"), (1, "middle"), (0, "more"), (1, "own"), (1, "end"),
    (0, "end"),
]
REDUCE_REDUCE_PLAN = [
    (0, "start"), (1, "start"), (0, "first"), (1, "middle"), (0, "second"), (1, "own"),
    (0, "others"), (1, "end"), (0, "end"),
]
REDUCE_GATHER_PLAN = [
    (1, "start"), (0, "start"), (0, "first"), (1, "middle"), (0, "second"), (0, "others"),
    (1, "end"), (0, "end"),
]


def total_devices():
    return lax.axis_size("dp") * lax.axis_size("seq")


def own_index():
    return lax.axis_index("dp") * lax.axis_size("seq") + lax.axis_index("seq")


def device_at(index):
    ways = lax.axis_size("seq")
    return (index // ways, index % ways)


def greet_all():
    devices, me = total_devices(), own_index()
    barrier = pltpu.get_barrier_semaphore()

    def signal(i, carry):
        target = device_at((me + i) % devices)
        pl.semaphore_signal(barrier, inc=1, device_id=target, device_id_type=MESH_ID)
        return carry

    lax.fori_loop(1, devices, signal, 0)
    pl.semaphore_wait(barrier, devices - 1)


def spread_all(blocks, landed, source, send, recv):
    devices, me = total_devices(), own_index()

    def post(i, carry):
        to = (me + i) % devices
        remote(source(to), landed.at[me], send, recv, device_at(to)).start()
        return carry

    lax.fori_loop(1, devices, post, 0)


def settle_all(landed, spare, send, recv):
    count = total_devices() - 1
    both = remote(
        landed.at[pl.ds(0, count)], spare.at[pl.ds(0, count)], send, recv,
        device_at((own_index() + 1) % total_devices()),
    )
    both.wait_recv()
    both.wait_send()


def closing(blocks, bias_tiles, weight):
    devices, rows, width = blocks.shape
    model_width = weight.shape[0]
    tiles = model_width // 128
    sums_shape = (devices, rows, 128)

    def make(ins, outs, scratch):
        blocks, bias_tiles, weight = ins
        columns, sums = outs
        landed, terms, landed_terms, part, *sems = scratch
        me = own_index()

        def start():
            spread_all(blocks, landed, lambda to: blocks.at[to], sems[0], sems[1])
            landed[me] = blocks[me]

        def middle():
            settle_all(landed, landed, sems[0], sems[1])
            total = jnp.sum(landed[...], axis=0)
            columns[...] = total
            cond = lax.dot_general(
                total, weight[...], (((1,), (1,)), ((), ())),
                precision=lax.Precision.HIGHEST, preferred_element_type=jnp.float32,
            )
            for i in range(tiles):
                terms[i] = cond[:, i * 128 : (i + 1) * 128]
            terms[pl.ds(tiles, devices - tiles)] = bias_tiles[...]
            spread_all(terms, landed_terms, lambda to: terms.at[to], sems[2], sems[3])
            landed_terms[me] = terms[me]

        def late():
            settle_all(landed_terms, landed_terms, sems[2], sems[3])
            total = jnp.sum(landed_terms[...], axis=0)
            part[...] = total
            spread_all(part, sums, lambda to: part, sems[4], sems[5])
            sums[me] = total

        def end():
            settle_all(sums, sums, sems[4], sems[5])

        return dict(start=start, middle=middle, late=late, end=end)

    return Part(
        make,
        [blocks, bias_tiles, weight],
        [VMEM] * 3,
        [
            jax.ShapeDtypeStruct((rows, width), jnp.float32),
            jax.ShapeDtypeStruct(sums_shape, jnp.float32),
        ],
        [VMEM] * 2,
        [
            pltpu.VMEM(blocks.shape, jnp.float32),
            pltpu.VMEM(sums_shape, jnp.float32),
            pltpu.VMEM(sums_shape, jnp.float32),
            pltpu.VMEM((rows, 128), jnp.float32),
        ]
        + [pltpu.SemaphoreType.DMA(())] * 6,
    )


CLOSING_PLAN = [
    (1, "start"), (0, "start"), (0, "first"), (1, "middle"), (0, "second"), (1, "late"),
    (0, "others"), (1, "end"), (0, "end"),
]


def pad_to(values, axis, size):
    pads = [(0, 0)] * values.ndim
    pads[axis] = (0, size - values.shape[axis])
    return jnp.pad(values, pads)


def swap_core(values):
    return lax.ppermute(values, "dp", [(i, i ^ 1) for i in range(lax.axis_size("dp"))])


def swap_x(values):
    return lax.ppermute(values, "seq", [(0, 1), (1, 0)])


def row_moves(turn):
    groups = lax.axis_size("dp")
    chips, pairs = groups // 2, []
    for d in range(groups):
        for x in range(2):
            block = d * 2 + (turn + x) % 2
            f, c = block // chips, block % chips
            pairs.append((d * 2 + x, (c * 2 + f % 2) * 2 + f // 2))
    return pairs


def flip(pair, swapped):
    low = jnp.where(swapped, pair[1], pair[0])
    high = jnp.where(swapped, pair[0], pair[1])
    return low, high


def rows_to_blocks(pieces):
    x = lax.axis_index("seq")
    b = (lax.axis_index("dp") // 2) % 2
    sent = flip(pieces, x == 1)
    got = [lax.ppermute(sent[turn], ("dp", "seq"), row_moves(turn)) for turn in range(2)]
    return jnp.concatenate(flip(got, b == 1), axis=1)


def blocks_to_rows(block):
    x = lax.axis_index("seq")
    b = (lax.axis_index("dp") // 2) % 2
    half = block.shape[1] // 2
    sent = flip((block[:, :half], block[:, half:]), b == 1)
    got = [
        lax.ppermute(sent[turn], ("dp", "seq"), [(q, p) for p, q in row_moves(turn)])
        for turn in range(2)
    ]
    return flip(got, x == 1)


def cut(values, index, size, axis=1):
    return lax.dynamic_slice_in_dim(values, index * size, size, axis)


def swap_both(values):
    groups = lax.axis_size("dp")
    pairs = [(d * 2 + x, (d ^ 1) * 2 + 1 - x) for d in range(groups) for x in range(2)]
    return lax.ppermute(values, ("dp", "seq"), pairs)


def by_core(high, own, far):
    return jnp.where(high, far, own), jnp.where(high, own, far)


def gather_columns(qkv_block, up_block):
    x, core = lax.axis_index("seq"), lax.axis_index("dp") % 2
    width, half = qkv_block.shape[1] // 6, up_block.shape[1] // 2
    first, high = x == 0, core == 1

    def pair(k):
        return jnp.concatenate(
            [
                qkv_block[:, k * width : (k + 1) * width],
                qkv_block[:, (4 + k) * width : (5 + k) * width],
            ],
            axis=1,
        )

    def across(k):
        return qkv_block[:, (2 + k) * width : (3 + k) * width]

    pairs = by_core(high, pair(0), pair(1))
    crosses = by_core(high, across(0), across(1))
    ups = by_core(high, up_block[:, :half], up_block[:, half:])
    cross_x = swap_x(crosses[0])
    cross_both = swap_both(crosses[1])
    pair_far = swap_core(pairs[1])
    up_far = swap_core(ups[1])
    pair_rows = jnp.concatenate(by_core(high, pairs[0], pair_far), axis=0)
    cross_rows = jnp.concatenate(by_core(high, cross_x, cross_both), axis=0)
    up_rows = jnp.concatenate(by_core(high, ups[0], up_far), axis=0)
    full = jnp.where(
        first,
        jnp.concatenate([pair_rows, cross_rows], axis=1),
        jnp.concatenate([cross_rows, pair_rows], axis=1),
    )
    return full, up_rows


def scatter_qkv(qkv_block):
    x, core = lax.axis_index("seq"), lax.axis_index("dp") % 2
    width, rows = qkv_block.shape[1] // 3, qkv_block.shape[0] // 2
    first, high = x == 0, core == 1
    pair = jnp.where(first, qkv_block[:, : 2 * width], qkv_block[:, width:])
    across = jnp.where(first, qkv_block[:, 2 * width :], qkv_block[:, :width])
    pairs = by_core(high, pair[:rows], pair[rows:])
    crosses = by_core(high, across[:rows], across[rows:])
    got_pairs = by_core(high, pairs[0], swap_core(pairs[1]))
    got_cross = by_core(high, swap_x(crosses[0]), swap_both(crosses[1]))
    return jnp.concatenate(
        [item[:, :width] for item in got_pairs]
        + list(got_cross)
        + [item[:, width:] for item in got_pairs],
        axis=1,
    )


def scatter_up(up_block):
    high = lax.axis_index("dp") % 2 == 1
    rows = up_block.shape[0] // 2
    ups = by_core(high, up_block[:rows], up_block[rows:])
    return jnp.concatenate(by_core(high, ups[0], swap_core(ups[1])), axis=1)


def on_device_grid(
    latents,
    condition,
    slot_latent,
    slot_counts,
    output_gradient,
    ada_weight,
    ada_bias,
    qkv_weight,
    qkv_bias,
    out_weight,
    out_bias,
    up_weight,
    up_bias,
    down_weight,
    down_bias,
    mean_adaw,
    mean_adab,
    mean_qkvw,
    mean_qkvb,
    mean_outw,
    mean_outb,
    mean_upw,
    mean_upb,
    mean_downw,
    mean_downb,
    sqmean_adaw,
    sqmean_adab,
    sqmean_qkvw,
    sqmean_qkvb,
    sqmean_outw,
    sqmean_outb,
    sqmean_upw,
    sqmean_upb,
    sqmean_downw,
    sqmean_downb,
):
    slot_total, tok_dev, model_width = latents.shape
    scale = HD ** (-0.5)
    latent_count = condition.shape[0]
    x_index, group = lax.axis_index("seq"), lax.axis_index("dp")
    core = group % 2
    share = 2 * x_index + core
    live = slot_counts[0] > 0
    slot_match = ((slot_latent[0, 0] == jnp.arange(latent_count)) & live).astype(jnp.float32)
    bf16 = jnp.bfloat16

    silu_cond = jax.nn.silu(condition).astype(bf16)
    mod_cols = jnp.dot(
        silu_cond, ada_weight.astype(bf16), preferred_element_type=jnp.float32
    ) + rounded(ada_bias)

    qkv_block, up_block = gather_columns(qkv_weight.astype(bf16), up_weight.astype(bf16))
    hidden_rows = down_weight.shape[0] // 2
    out_rows = out_weight.shape[0] // 2
    down_b, out_b = down_weight.astype(bf16), out_weight.astype(bf16)
    rows_block = rows_to_blocks(
        [
            jnp.concatenate(
                [cut(down_b, i, hidden_rows, 0), cut(out_b, i, out_rows, 0)], axis=0
            )
            for i in range(2)
        ]
    )
    down_block, out_block = rows_block[:hidden_rows], rows_block[hidden_rows:]
    grid_plan = [
        (0, stage)
        for stage in (
            "start", "hops", "early", "four_start", "four_middle", "four_end", "late",
        )
    ]
    ((_, qkv_grid, out_grid, mod_four),) = run_parts(
        [grid_four_gather([mod_cols, qkv_block, out_block])], grid_plan, 1, True, True
    )
    mat_qkv = qkv_grid.reshape(model_width, -1)
    mat_out = lax.optimization_barrier(out_grid.reshape(-1, model_width))
    width = mat_out.shape[0]
    hidden_width = up_block.shape[1]
    heads = width // HD

    slot_mod = jnp.einsum("jcln,l->cjn", mod_four, slot_match, precision=lax.Precision.HIGHEST)
    slot_mod = slot_mod.reshape(6, 1, model_width)
    shift_att, scale_att, gate_att, shift_mlp, scale_mlp, gate_mlp = (
        slot_mod[i] for i in range(6)
    )

    biases = (qkv_bias, out_bias, down_bias)
    bias_own = jnp.concatenate(biases).astype(bf16)[None]
    bias_other = swap_x(bias_own)
    bias_pair = flip((bias_own, bias_other), x_index == 1)
    starts = [0]
    for item in biases:
        starts.append(starts[-1] + item.shape[0])
    vec_qkv, vec_out, vec_down = (
        jnp.concatenate(
            [half[0, starts[i] : starts[i + 1]] for half in bias_pair]
        ).astype(jnp.float32)
        for i in range(3)
    )
    vec_qkv = cut(vec_qkv.reshape(3, -1), share, width).reshape(-1)
    vec_up = cut(rounded(up_bias), core, hidden_width, 0)

    tokens = latents[0]
    upstream = jnp.where(live, output_gradient[0], 0.0)
    normed_att, spread_att = normalize(tokens)
    attn_own = (normed_att * (1.0 + scale_att) + shift_att).astype(bf16)
    back_down = upstream * gate_mlp
    (up_grid,), four_pair = run_parts(
        [grid_gather([up_block]), four_gather([attn_own, back_down.astype(bf16)])],
        GATHER_PLAN, 2, True, True,
    )
    attn_in, back_down_all = (item.reshape(-1, model_width) for item in four_pair)
    mat_up = up_grid.reshape(model_width, -1)
    qkv_all = (jnp.dot(attn_in, mat_qkv, preferred_element_type=jnp.float32) + vec_qkv).astype(bf16)
    split = (2, -1, heads, HD)
    queries = qkv_all[:, :width].reshape(split)
    keys_heads = qkv_all[:, width : 2 * width].reshape(split)
    values_heads = qkv_all[:, 2 * width :].reshape(split)
    scores = (
        jnp.einsum("sqhd,skhd->shqk", queries, keys_heads, preferred_element_type=jnp.float32)
        * scale
    )
    row_max = jnp.max(scores, axis=-1, keepdims=True)
    row_total = jnp.sum(jnp.exp(scores - row_max), axis=-1, keepdims=True)
    attn_probs = jnp.exp(scores - row_max) / row_total
    probs_b = attn_probs.astype(bf16)
    attended = jnp.einsum(
        "shqk,skhd->sqhd", probs_b, values_heads, preferred_element_type=jnp.float32
    )
    attended_b = attended.reshape(-1, width).astype(bf16)
    blocks = (4, tok_dev, model_width)
    out_terms = jnp.dot(attended_b, mat_out, preferred_element_type=jnp.float32)
    (down_grid,), (branch_sum,) = run_parts(
        [grid_gather([down_block]), four_reduce([out_terms.reshape(blocks)])],
        GATHER_REDUCE_PLAN, 3, True, True,
    )
    mat_down = down_grid.reshape(-1, model_width)
    branch_att = branch_sum + vec_out
    middle = tokens + gate_att * branch_att
    normed_mlp, spread_mlp = normalize(middle)
    mlp_own = (normed_mlp * (1.0 + scale_mlp) + shift_mlp).astype(bf16)
    ((mlp_four,),) = run_parts(
        [four_gather([mlp_own])], [(0, "start"), (0, "middle"), (0, "end")], 4, False, True
    )
    mlp_in = mlp_four.reshape(-1, model_width)
    hidden = jnp.dot(mlp_in, mat_up, preferred_element_type=jnp.float32) + vec_up
    activated = gelu_tanh(hidden).astype(bf16)
    branch_terms = jnp.dot(activated, mat_down, preferred_element_type=jnp.float32)
    term_down = weight_term(activated, back_down_all)
    sum_downb = jnp.sum(back_down, axis=0)
    back_hidden = jnp.einsum(
        "rd,fd->rf", back_down_all, mat_down, preferred_element_type=jnp.float32
    ) * gelu_slope(hidden)
    back_hidden_b = back_hidden.astype(bf16)
    term_up = weight_term(mlp_in, back_hidden_b)
    sum_upb = jnp.sum(back_hidden, axis=0)
    back_terms = jnp.einsum(
        "rf,cf->rc", back_hidden_b, mat_up, preferred_element_type=jnp.float32
    )
    chips = lax.axis_size("dp") // 2

    def by_chip(term):
        return term.reshape(chips, -1, term.shape[1])

    (down_sum,), (branch_mlp, back_mlp_in) = run_parts(
        [
            grid_reduce([by_chip(term_down)]),
            four_reduce([branch_terms.reshape(blocks), back_terms.reshape(blocks)]),
        ],
        REDUCE_REDUCE_PLAN, 5, True, True,
    )
    branch_mlp = branch_mlp + vec_down
    block_output = jnp.where(live, middle + gate_mlp * branch_mlp, 0.0)
    back_middle = upstream + norm_back(back_mlp_in * (1.0 + scale_mlp), normed_mlp, spread_mlp)
    back_att = back_middle * gate_att
    up_terms = by_chip(term_up)
    later = up_terms.shape[1] // 3
    (up_first,), (back_att_four,) = run_parts(
        [grid_reduce([up_terms[:, later:]]), four_gather([back_att.astype(bf16)])],
        REDUCE_GATHER_PLAN, 6, True, True,
    )
    back_att_all = back_att_four.reshape(-1, model_width)
    term_out = weight_term(attended_b, back_att_all)
    sum_outb = jnp.sum(back_att, axis=0)
    back_attended = jnp.einsum(
        "rd,cd->rc", back_att_all, mat_out, preferred_element_type=jnp.float32
    ).astype(bf16)
    back_attended = back_attended.reshape(split)
    back_probs = jnp.einsum(
        "sqhd,skhd->shqk", back_attended, values_heads, preferred_element_type=jnp.float32
    )
    row_delta = jnp.einsum("sqhd,sqhd->shq", back_attended.astype(jnp.float32), attended)[..., None]
    back_scores = (attn_probs * (back_probs - row_delta) * scale).astype(bf16)
    back_queries = jnp.einsum(
        "shqk,skhd->sqhd", back_scores, keys_heads, preferred_element_type=jnp.float32
    )
    back_keys = jnp.einsum(
        "shqk,sqhd->skhd", back_scores, queries, preferred_element_type=jnp.float32
    )
    back_values = jnp.einsum(
        "shqk,sqhd->skhd", probs_b, back_attended, preferred_element_type=jnp.float32
    )
    back_parts = [item.reshape(-1, width) for item in (back_queries, back_keys, back_values)]
    sum_qkvb = jnp.concatenate([jnp.sum(item, axis=0) for item in back_parts])
    back_parts = [item.astype(bf16) for item in back_parts]
    qkv_width = 3 * width
    qkv_wide = -(-qkv_width // 128) * 128
    spare = jnp.zeros((back_parts[0].shape[0], qkv_wide - qkv_width), bf16)
    back_qkv_b = jnp.concatenate(back_parts + [spare], axis=1)
    term_qkv = weight_term(attn_in, back_qkv_b)
    back_qkv_b = back_qkv_b[:, :qkv_width]
    attn_terms = jnp.einsum(
        "rd,cd->rc", back_qkv_b, mat_qkv, preferred_element_type=jnp.float32
    )
    (up_second,), (back_attn_in,) = run_parts(
        [grid_reduce([up_terms[:, :later]]), four_reduce([attn_terms.reshape(blocks)])],
        REDUCE_REDUCE_PLAN, 7, True, True,
    )
    up_sum = jnp.concatenate([up_second, up_first], axis=0)
    latent_gradient = jnp.where(
        live,
        back_middle + norm_back(back_attn_in * (1.0 + scale_att), normed_att, spread_att),
        0.0,
    )[None]
    block_output = block_output[None]
    slot_modgrad = jnp.concatenate(
        [
            jnp.sum(back_attn_in, axis=0),
            jnp.sum(back_attn_in * normed_att, axis=0),
            jnp.sum(back_middle * branch_att, axis=0),
            jnp.sum(back_mlp_in, axis=0),
            jnp.sum(back_mlp_in * normed_mlp, axis=0),
            jnp.sum(upstream * branch_mlp, axis=0),
        ]
    )
    devices, own_cols = total_devices(), ada_bias.shape[0]
    qkvb_wide = lax.dynamic_update_slice(
        jnp.zeros((3, 4 * width), jnp.float32), sum_qkvb.reshape(3, width), (0, share * width)
    ).reshape(-1)
    upb_wide = lax.dynamic_update_slice(
        jnp.zeros((4 * hidden_width,), jnp.float32), sum_upb, (share * hidden_width,)
    )
    bias_sums = (qkvb_wide, sum_outb, upb_wide, sum_downb)
    tiles = model_width // 128
    bias_flat = jnp.concatenate(bias_sums)
    tile = latent_count * 128
    bias_tiles = pad_to(bias_flat, 0, (devices - tiles) * tile).reshape(-1, latent_count, 128)
    wide = -(-own_cols // 128) * 128
    sent = pad_to(slot_modgrad.reshape(devices, 1, own_cols), 2, wide) * slot_match[:, None]
    (qkv_sum, out_sum), (columns, sums) = run_parts(
        [
            grid_reduce([by_chip(term_qkv), by_chip(term_out)]),
            closing(sent, bias_tiles, pad_to(rounded(ada_weight), 1, wide)),
        ],
        CLOSING_PLAN, 8, True, None,
    )
    modgrad_cols = columns[:, :own_cols]
    cond_sum = jnp.moveaxis(sums[:tiles], 0, 1).reshape(latent_count, model_width)
    totals, start, bias_totals = sums[tiles:].reshape(-1), 0, []
    for item in bias_sums:
        bias_totals.append(totals[start : start + item.shape[0]])
        start += item.shape[0]
    total_qkvb, total_outb, total_upb, total_downb = bias_totals
    grad_qkvw, grad_upw = scatter_qkv(qkv_sum[:, :qkv_width]), scatter_up(up_sum)
    owned = blocks_to_rows(jnp.concatenate([down_sum, out_sum], axis=0))
    grad_downw = jnp.concatenate([item[:hidden_rows] for item in owned], axis=0)
    grad_outw = jnp.concatenate([item[hidden_rows:] for item in owned], axis=0)
    grad_qkvw, grad_outw, grad_upw, grad_downw = (
        item.astype(jnp.float32) for item in (grad_qkvw, grad_outw, grad_upw, grad_downw)
    )

    grad_adaw = jnp.dot(
        rounded(jax.nn.silu(condition)).T, modgrad_cols, precision=lax.Precision.HIGHEST
    )
    grad_adab = jnp.sum(modgrad_cols, axis=0)
    condition_grad = cond_sum * silu_slope(condition)
    seq_index = lax.axis_index("seq")

    def own_part(full_sum, local_bias):
        length = local_bias.shape[0]
        return lax.dynamic_slice_in_dim(full_sum, seq_index * length, length)

    grad_qkvb = own_part(total_qkvb, qkv_bias)
    grad_outb = own_part(total_outb, out_bias)
    grad_upb = own_part(total_upb, up_bias)
    grad_downb = own_part(total_downb, down_bias)
    grads_all = (
        grad_adaw,
        grad_adab,
        grad_qkvw,
        grad_qkvb,
        grad_outw,
        grad_outb,
        grad_upw,
        grad_upb,
        grad_downw,
        grad_downb,
    )
    params_all = (
        ada_weight,
        ada_bias,
        qkv_weight,
        qkv_bias,
        out_weight,
        out_bias,
        up_weight,
        up_bias,
        down_weight,
        down_bias,
    )
    means_all = (
        mean_adaw,
        mean_adab,
        mean_qkvw,
        mean_qkvb,
        mean_outw,
        mean_outb,
        mean_upw,
        mean_upb,
        mean_downw,
        mean_downb,
    )
    squares_all = (
        sqmean_adaw,
        sqmean_adab,
        sqmean_qkvw,
        sqmean_qkvb,
        sqmean_outw,
        sqmean_outb,
        sqmean_upw,
        sqmean_upb,
        sqmean_downw,
        sqmean_downb,
    )
    updates = [
        adamw_step(p_item, g_item, m_item, v_item)
        for p_item, g_item, m_item, v_item in zip(params_all, grads_all, means_all, squares_all)
    ]
    newvals = tuple((entry[0] for entry in updates))
    newmeans = tuple((entry[1] for entry in updates))
    newsqrs = tuple((entry[2] for entry in updates))
    return (
        (block_output, latent_gradient, condition_grad) + grads_all + newvals + newmeans + newsqrs
    )


def fits(mesh, slots, latent_count, width, hidden):
    groups, ways = mesh.shape["dp"], mesh.shape["seq"]
    return (
        slots == groups
        and ways == 2
        and groups % 4 == 0
        and H % 4 == 0
        and width == H * HD
        and width % (2 * groups * 4) == 0
        and hidden % (2 * groups * 16) == 0
        and width % 128 == 0
        and width // 128 - (-(5 * width + hidden) // (latent_count * 128)) <= groups * ways
    )


def build(mesh, on_device):
    return jax.shard_map(
        on_device,
        mesh=mesh,
        in_specs=(
            P("dp", "seq", None),
            P(),
            P("dp", None),
            P("dp"),
            P("dp", "seq", None),
            P(None, ("dp", "seq")),
            P(("dp", "seq")),
            P("dp", "seq"),
            P("seq"),
            P("dp", "seq"),
            P("seq"),
            P("dp", "seq"),
            P("seq"),
            P("dp", "seq"),
            P("seq"),
            P(None, ("dp", "seq")),
            P(("dp", "seq")),
            P("dp", "seq"),
            P("seq"),
            P("dp", "seq"),
            P("seq"),
            P("dp", "seq"),
            P("seq"),
            P("dp", "seq"),
            P("seq"),
            P(None, ("dp", "seq")),
            P(("dp", "seq")),
            P("dp", "seq"),
            P("seq"),
            P("dp", "seq"),
            P("seq"),
            P("dp", "seq"),
            P("seq"),
            P("dp", "seq"),
            P("seq"),
        ),
        out_specs=(
            P("dp", "seq", None),
            P("dp", "seq", None),
            P(),
            P(None, ("dp", "seq")),
            P(("dp", "seq")),
            P("dp", "seq"),
            P("seq"),
            P("dp", "seq"),
            P("seq"),
            P("dp", "seq"),
            P("seq"),
            P("dp", "seq"),
            P("seq"),
            P(None, ("dp", "seq")),
            P(("dp", "seq")),
            P("dp", "seq"),
            P("seq"),
            P("dp", "seq"),
            P("seq"),
            P("dp", "seq"),
            P("seq"),
            P("dp", "seq"),
            P("seq"),
            P(None, ("dp", "seq")),
            P(("dp", "seq")),
            P("dp", "seq"),
            P("seq"),
            P("dp", "seq"),
            P("seq"),
            P("dp", "seq"),
            P("seq"),
            P("dp", "seq"),
            P("seq"),
            P(None, ("dp", "seq")),
            P(("dp", "seq")),
            P("dp", "seq"),
            P("seq"),
            P("dp", "seq"),
            P("seq"),
            P("dp", "seq"),
            P("seq"),
            P("dp", "seq"),
            P("seq"),
        ),
        check_vma=False,
    )


def solution(mesh):
    def program(latents, condition, *rest):
        hidden, width = rest[11].shape
        chosen = fits(mesh, latents.shape[0], condition.shape[0], width, hidden)
        return build(mesh, on_device_grid if chosen else on_device_general)(
            latents, condition, *rest
        )

    return program
```
